32 devices in a mesh: fsdp: 16 (over z, y, x), rep: 2 (over core).
Axes of the slice: x: 2, y: 2, z: 4, core: 2. Of those that a mesh axis runs over, the one named last changes fastest.
Arguments:
- tokens: bfloat16 [2, 16, 1024, 1024], P('rep', None, 'fsdp'), may hold values from -6 to 6
- cotangent: bfloat16 [2, 16, 1024, 1024], P('rep', None, 'fsdp'), may hold values from -6 to 6
- w_qkv: bfloat16 [1024, 3072], P('fsdp'), may hold values from -0.1875 to 0.1875
- w_out: bfloat16 [1024, 1024], P('fsdp'), may hold values from -1.5 to 1.5
- w_up: bfloat16 [1024, 4096], P('fsdp'), may hold values from -0.1875 to 0.1875
- w_down: bfloat16 [4096, 1024], P('fsdp'), may hold values from -0.09375 to 0.09375
- w_router: bfloat16 [1024], P('fsdp'), may hold values from -0.1875 to 0.1875
- gain_attn: bfloat16 [1024], P('fsdp'), may hold values from 0.5 to 1.5
- gain_mlp: bfloat16 [1024], P('fsdp'), may hold values from 0.5 to 1.5
- lengths: int32 [2, 16], P('rep'), may hold values from 512 to 1024, as said below
- routed: int32 [2, 16, 128], P('rep'), may hold values from -1 to 1023, as said below
- dealing: int32 [2, 16], P('rep'), may hold values from 0 to 15, each once within a row
Outputs:
- output: bfloat16 [2, 16, 1024, 1024], P('rep', None, 'fsdp')
- grad_input: bfloat16 [2, 16, 1024, 1024], P('rep', None, 'fsdp')
- grad_qkv: float32 [1024, 3072], P('fsdp')
- grad_out: float32 [1024, 1024], P('fsdp')
- grad_up: float32 [1024, 4096], P('fsdp')
- grad_down: float32 [4096, 1024], P('fsdp')
- grad_router: float32 [1024], P('fsdp')
- grad_gain_attn: float32 [1024], P('fsdp')
- grad_gain_mlp: float32 [1024], P('fsdp')
The draws below stay inside these ranges and needn't reach their ends.
Inputs may be any that keep to these rules, and one draw needn't show every extreme that they name: `lengths`: in each group one sequence has length exactly 1024 and another exactly 512. `routed`: for sequence s of group g, slots c < lengths[g, s] // 8 hold distinct positions below lengths[g, s] in rising order, the last of them lengths[g, s] - 1; the other slots hold -1.
All inputs are finite; a program needn't handle non-finite values.
Results may differ from the reference program's by a relative error of at most 0.013.
Values may be sent and summed in bfloat16 or wider, within the bound.
A program may use at most 192 MiB of HBM per device.

```python
import math
import jax
import jax.numpy as jnp
from jax import lax

D = 1024
HEADS = 16
HEAD_DIM = 64
FF = 4096
SEQ_MAX = 1024
CAP = 128
GROUP_SEQS = 16
REPLICAS = 2


def routing_tables(key):
    length_key = jax.random.fold_in(key, 101)
    longest_key = jax.random.fold_in(key, 102)
    score_key = jax.random.fold_in(key, 103)
    seq_lengths = jax.random.randint(length_key, (REPLICAS, GROUP_SEQS), SEQ_MAX // 2, SEQ_MAX + 1)
    longest = jax.random.randint(longest_key, (REPLICAS, 1), 0, GROUP_SEQS)
    shortest = (longest + 1) % GROUP_SEQS
    seq_index = jnp.arange(GROUP_SEQS, dtype=jnp.int32)[None, :]
    seq_lengths = jnp.where(seq_index == longest, SEQ_MAX, seq_lengths)
    seq_lengths = jnp.where(seq_index == shortest, SEQ_MAX // 2, seq_lengths).astype(jnp.int32)
    positions = jnp.arange(SEQ_MAX, dtype=jnp.int32)
    score_int = jax.random.randint(score_key, (REPLICAS, GROUP_SEQS, SEQ_MAX), 0, 2 ** 20) * SEQ_MAX + positions
    score_int = jnp.where(positions == seq_lengths[:, :, None] - 1, -1, score_int)
    score_int = jnp.where(positions >= seq_lengths[:, :, None], 2 ** 30 + positions, score_int)
    unused, picked = lax.top_k(-score_int, CAP)
    slot_ids = jnp.arange(CAP, dtype=jnp.int32)
    keeping = slot_ids[None, None, :] < (seq_lengths // 8)[:, :, None]
    picked = jnp.where(keeping, picked, 2 * SEQ_MAX)
    picked = jnp.sort(picked, axis=-1)
    routes = jnp.where(picked >= SEQ_MAX, -1, picked).astype(jnp.int32)
    return (seq_lengths, routes)


def draw_lengths(key, part):
    return routing_tables(key)[0]


def draw_routed(key, part):
    return routing_tables(key)[1]


def levels(own_key, shape, shards, smallest, top_value):
    loudness, own = 1.0, jax.random.fold_in(own_key, 6)
    for position, blocks in shards:
        heights = jnp.exp(jax.random.uniform(jax.random.fold_in(own, position), (blocks,), jnp.float32, smallest / len(shards), top_value / len(shards)))
        loudness = loudness * jnp.repeat(heights, shape[position] // blocks).reshape([-1 if axis == position else 1 for axis in range(len(shape))])
    return loudness


def gaussian(key, dims, deviation, reach, pieces=(), held_as=jnp.bfloat16):
    array = jax.random.normal(key, dims, jnp.float32) * deviation
    if len(pieces) > 0:
        array = levels(key, dims, pieces, -0.22, 0.18) * array
    return jnp.clip(array, min=-reach, max=reach).astype(held_as)


def setup_inputs(seed: int = 0) -> dict:
    arg_keys = jax.random.split(jax.random.key(seed), 13)
    return {
        "tokens": gaussian(arg_keys[0], (REPLICAS, GROUP_SEQS, SEQ_MAX, D), 1.0, 6.0, ((0, 2), (2, 16))),
        "cotangent": gaussian(arg_keys[1], (REPLICAS, GROUP_SEQS, SEQ_MAX, D), 1.0, 6.0, ((0, 2), (2, 16))),
        "w_qkv": gaussian(arg_keys[2], (D, 3 * D), D ** -0.5, 0.1875, ((0, 16),)),
        "w_out": gaussian(arg_keys[3], (D, D), (2 * D // CAP) ** -0.5, 1.5, ((0, 16),)),
        "w_up": gaussian(arg_keys[4], (D, FF), D ** -0.5, 0.1875, ((0, 16),)),
        "w_down": gaussian(arg_keys[5], (FF, D), FF ** -0.5, 0.09375, ((0, 16),)),
        "w_router": gaussian(arg_keys[6], (D,), D ** -0.5, 0.1875, ((0, 16),)),
        "gain_attn": jnp.clip(1.0 + 0.1 * jax.random.normal(arg_keys[7], (D,), jnp.float32), 0.5, 1.5).astype(jnp.bfloat16),
        "gain_mlp": jnp.clip(1.0 + 0.1 * jax.random.normal(arg_keys[8], (D,), jnp.float32), 0.5, 1.5).astype(jnp.bfloat16),
        "lengths": draw_lengths(jax.random.fold_in(arg_keys[12], 71), 0),
        "routed": draw_routed(jax.random.fold_in(arg_keys[12], 71), 0),
        "dealing": jax.vmap(lambda own: jax.random.permutation(own, GROUP_SEQS))(jax.random.split(arg_keys[11], REPLICAS)).reshape((REPLICAS, GROUP_SEQS)).astype(jnp.int32),
    }


EPSILON = 1e-06
EXACT_PRECISION = lax.Precision.HIGHEST

@jax.custom_vjp
def low(v):
    return lax.optimization_barrier(v.astype(jnp.bfloat16)).astype(jnp.float32)

@jax.custom_vjp
def low_back(v):
    return v

def low_keep(v):
    return (low(v), None)

def low_pass(kept, grad):
    return (grad,)

def back_keep(v):
    return (v, None)

def back_low(kept, grad):
    return (low(grad),)
low.defvjp(low_keep, low_pass)
low_back.defvjp(back_keep, back_low)

def rms_norm(values, gain):
    return values * lax.rsqrt(lax.optimization_barrier(jnp.mean(values * values, axis=-1, keepdims=True)) + EPSILON) * gain

def block_forward(tokens_f, w_qkv, w_out, w_up, w_down, w_router, gain_attn, gain_mlp, one_hot_matrix, valid_slot, living):
    factor = 1.0 / math.sqrt(HEAD_DIM)
    incoming_rows = jnp.einsum('gscl,gsld->gscd', one_hot_matrix, tokens_f, precision=EXACT_PRECISION)
    router_val = jnp.einsum('gscd,d->gsc', incoming_rows, w_router, precision=EXACT_PRECISION)
    normed_attn = low(rms_norm(incoming_rows, gain_attn))
    packed = low_back(low(jnp.einsum('gscd,de->gsce', normed_attn, w_qkv, precision=EXACT_PRECISION)))
    head_shape = packed.shape[:3] + (HEADS, HEAD_DIM)
    queries = packed[..., :D].reshape(head_shape)
    keys_heads = packed[..., D:2 * D].reshape(head_shape)
    values_heads = packed[..., 2 * D:].reshape(head_shape)
    scores = low_back(jnp.einsum('gsqhe,gskhe->gshqk', queries, keys_heads, precision=EXACT_PRECISION) * factor)
    slot_ids = jnp.arange(CAP, dtype=jnp.int32)
    allowed = (slot_ids[None, :] <= slot_ids[:, None])[None, None, None] & valid_slot[:, :, None, None, :]
    scores = jnp.where(allowed, scores, -1e+30)
    probs_low = low(jax.nn.softmax(scores, axis=-1))
    attended = low_back(low(jnp.einsum('gshqk,gskhe->gsqhe', probs_low, values_heads, precision=EXACT_PRECISION)))
    attended = attended.reshape(packed.shape[:3] + (D,))
    branch_attn = low_back(jnp.einsum('gsce,ed->gscd', attended, w_out, precision=EXACT_PRECISION))
    middle = incoming_rows + branch_attn
    normed_mid = low(rms_norm(middle, gain_mlp))
    upward = low_back(jnp.einsum('gscd,df->gscf', normed_mid, w_up, precision=EXACT_PRECISION))
    activated = low(jax.nn.gelu(upward))
    branch_mlp = low_back(jnp.einsum('gscf,fd->gscd', activated, w_down, precision=EXACT_PRECISION))
    refreshed_rows = incoming_rows + router_val[..., None] * (branch_attn + branch_mlp)
    scattered = jnp.einsum('gscl,gscd->gsld', one_hot_matrix, refreshed_rows, precision=EXACT_PRECISION)
    touched = lax.optimization_barrier(jnp.sum(one_hot_matrix, axis=2)) > 0.5
    result = jnp.where(touched[..., None], scattered, tokens_f)
    return jnp.where(living[..., None], result, jnp.zeros_like(result))

def reference(tokens, cotangent, w_qkv, w_out, w_up, w_down, w_router, gain_attn, gain_mlp, lengths, routed, dealing):
    seq_lengths = jnp.take_along_axis(lengths, dealing, axis=1)
    seq_routes = jnp.take_along_axis(routed, dealing[:, :, None], axis=1)
    slot_ids = jnp.arange(CAP, dtype=jnp.int32)
    valid_slot = slot_ids[None, None, :] < (seq_lengths // 8)[:, :, None]
    positions = jnp.arange(SEQ_MAX, dtype=jnp.int32)
    living = positions[None, None, :] < seq_lengths[:, :, None]
    one_hot_matrix = ((seq_routes[..., None] == positions) & valid_slot[..., None]).astype(jnp.float32)
    params = (w_qkv.astype(jnp.float32), w_out.astype(jnp.float32), w_up.astype(jnp.float32), w_down.astype(jnp.float32), w_router.astype(jnp.float32), gain_attn.astype(jnp.float32), gain_mlp.astype(jnp.float32))

    def forward(tokens_f, qkv_m, out_m, up_m, down_m, router_m, gain_one, gain_two):
        return block_forward(tokens_f, qkv_m, out_m, up_m, down_m, router_m, gain_one, gain_two, one_hot_matrix, valid_slot, living)
    result, pullback = jax.vjp(forward, tokens.astype(jnp.float32), *params)
    grads = pullback(cotangent.astype(jnp.float32))
    return (result.astype(jnp.bfloat16), grads[0].astype(jnp.bfloat16), grads[1], grads[2], grads[3], grads[4], grads[5], grads[6], grads[7])
```

```python
import functools

import jax
import jax.numpy as jnp
from jax import lax
from jax.experimental import pallas as pl
from jax.experimental.pallas import tpu as pltpu

MESH = pl.DeviceIdType.MESH
ANY = pl.ANY


def grid_axes(mesh):
    devices = mesh.devices[:, 0]
    count = len(devices)
    axes = []
    spots = [getattr(d, "coords", None) for d in devices]
    if all(s is not None for s in spots) and len(set(map(tuple, spots))) == count:
        low = [min(s[k] for s in spots) for k in range(3)]
        at = {tuple(s[k] - low[k] for k in range(3)): f for f, s in enumerate(spots)}
        for k in range(3):
            size = max(s[k] for s in spots) - low[k] + 1
            one = tuple(int(j == k) for j in range(3))
            axes.append((at[one] if size > 1 else 1, size, k))
        ok = all(
            f == sum(stride * spot[k] for stride, _, k in axes) for spot, f in at.items()
        )
        axes = [a[:2] for a in axes] if ok else []
    if not axes:
        axes, left = [], count
        for size in (2, 2):
            size = size if left % size == 0 and left > 1 else 1
            axes.append((count // left, size))
            left //= size
        axes.append((count // left, left))
    return sorted(axes, key=lambda a: -a[1])


def xor(a, b, size):
    out, bit = 0, 1
    while bit < size:
        out = out + ((a // bit + b // bit) % 2) * bit
        bit *= 2
    return out


class Piece:
    def __init__(self, array, half, offset, width):
        self.array, self.half, self.offset, self.width = array, half, offset, width

    def cols(self, core):
        start = self.offset
        if self.half:
            start = core * self.half + start
            start = pl.multiple_of(start, 128)
        return pl.ds(start, self.width)


def colours(axes, widths):
    qkv, out, up, down = (w // 2 for w in widths[:4])
    a, b, c = axes
    third = qkv // 3
    return [
        ((b, c, a), [Piece(1, out, 0, out), Piece(4, 0, 0, widths[4])]),
        ((c, b, a), [Piece(0, qkv, 0, third)]),
        ((a, b, c), [Piece(2, up, 0, up), Piece(0, qkv, third, third)]),
        ((a, c, b), [Piece(3, down, 0, down), Piece(0, qkv, 2 * third, third)]),
    ]


def neighbours(axes, me):
    found = []
    for stride, size in axes:
        at = (me // stride) % size
        if size == 2:
            found.append((None, (1 - 2 * at) * stride))
        elif size > 2:
            found.append((at < size - 1, stride))
            found.append((at > 0, -stride))
    return found


def guarded(cond, fn):
    if cond is None:
        fn()
    else:
        pl.when(cond)(fn)


def enter(axes, me, core):
    barrier = pltpu.get_barrier_semaphore()
    total = 1
    for cond, step in neighbours(axes, me):
        def hello(step=step):
            pl.semaphore_signal(barrier, inc=1, device_id=(me + step, core), device_id_type=MESH)
        guarded(cond, hello)
        total = total + (1 if cond is None else cond.astype(jnp.int32))
    pl.semaphore_signal(barrier, inc=1, device_id=(me, 1 - core), device_id_type=MESH)
    pl.semaphore_wait(barrier, total)


def gather_kernel(axes, plan, n, *refs):
    k = 5
    ins, outs = refs[:k], refs[k : 2 * k]
    stages = refs[2 * k : 3 * k]
    send_sem, recv_sem, pair_send, pair_recv, local_sem = refs[3 * k :]
    me, core = lax.axis_index("fsdp"), lax.axis_index("rep")
    enter(axes, me, core)
    numbered, number = [], 0
    for order, pieces in plan:
        numbered.append((order, [(number + i, p) for i, p in enumerate(pieces)]))
        number += len(pieces)

    def spot(axis):
        return (me // axis[0]) % axis[1]

    def dst(piece, block):
        return outs[piece.array].at[block, :, piece.cols(core)]

    def put(pieces, block, own, phase, way, device, pair=False):
        for i, piece in pieces:
            if pair and not piece.half:
                continue
            src = ins[piece.array].at[:, piece.cols(core)] if own else dst(piece, block)
            pltpu.make_async_remote_copy(
                src_ref=src,
                dst_ref=dst(piece, block),
                send_sem=pair_send.at[i] if pair else send_sem.at[i, phase, way],
                recv_sem=pair_recv.at[i] if pair else recv_sem.at[i, block],
                device_id=device,
                device_id_type=MESH,
            ).start()

    def along(pieces, order, block, own, phase, ways):
        stride, size = order[phase]
        at = spot(order[phase])
        if size == 1:
            return
        if size == 2:
            put(pieces, block, own, phase, 0, (me + (1 - 2 * at) * stride, core))
            return
        for way in ways:
            step = 1 - 2 * way
            pl.when(at < size - 1 if way == 0 else at > 0)(
                functools.partial(put, pieces, block, own, phase, way, (me + step * stride, core))
            )

    def arrived(pieces, order, block, phase, way):
        for i, piece in pieces:
            pltpu.make_async_remote_copy(
                src_ref=dst(piece, block),
                dst_ref=dst(piece, block),
                send_sem=send_sem.at[i, phase, way],
                recv_sem=recv_sem.at[i, block],
                device_id=(me, 1 - core),
                device_id_type=MESH,
            ).wait_recv()
        if order[phase][1] > 2:
            along(pieces, order, block, False, phase, (way,))
        for later in range(phase + 1, 3):
            along(pieces, order, block, False, later, (0, 1))
        put(pieces, block, False, 0, 0, (me, 1 - core), pair=True)

    for order, pieces in numbered:
        for phase in range(3):
            along(pieces, order, me, True, phase, (0, 1))
    local = []
    for j in range(k):
        local.append(pltpu.make_async_copy(ins[j], stages[j], local_sem.at[j]))
        local[-1].start()
    events = []
    for number, (order, pieces) in enumerate(numbered):
        heavy = number >= 2
        sizes = [a[1] for a in order]
        for phase in range(3):
            size = sizes[phase]
            rest = 1
            for s in sizes[:phase]:
                rest *= s
            for t in range(1, size):
                ways = (0,) if size == 2 else (0, 1)
                for way in ways:
                    for j in range(rest):
                        if heavy:
                            key = 20 * t if phase == 0 else 20 * phase + 20 * (j + (t - 1) * rest + 1)
                        else:
                            key = 5 if phase == 0 else 10 + 5 * j if phase == 1 else 15 + 40 * t + 5 * j
                        events.append((key, len(events), order, pieces, phase, t, way, j))
    events.sort(key=lambda e: e[:2])

    def run(order, pieces, phase, t, way, j):
        stride, size = order[phase]
        at = spot(order[phase])
        origin = 1 - at if size == 2 else at - (1 - 2 * way) * t
        block = me + (origin - at) * stride
        for s, z in order[:phase]:
            here = (me // s) % z
            block = block + (xor(here, j % z, z) - here) * s
            j = j // z
        if size == 2:
            arrived(pieces, order, block, phase, 0)
        else:
            pl.when((origin >= 0) & (origin < size))(
                functools.partial(arrived, pieces, order, block, phase, way)
            )

    def settle():
        for j in range(k):
            local[j].wait()
            local[j] = pltpu.make_async_copy(stages[j], outs[j].at[me], local_sem.at[j])
            local[j].start()

    for number, (_, _, order, pieces, phase, t, way, j) in enumerate(events):
        run(order, pieces, phase, t, way, j)
        if number == 3:
            settle()
    for copy in local:
        copy.wait()

    def drain(i, piece, count, send, recv, which):
        many = outs[piece.array].at[pl.ds(0, count), :, piece.cols(core)]
        copy = pltpu.make_async_remote_copy(
            src_ref=many, dst_ref=many, send_sem=send, recv_sem=recv,
            device_id=(me, 1 - core), device_id_type=MESH,
        )
        if which == "send":
            copy.wait_send()
        else:
            copy.wait_recv()

    for order, pieces in numbered:
        rest = 1
        for phase in range(3):
            stride, size = order[phase]
            at = spot(order[phase])
            for i, piece in pieces:
                if size == 2:
                    drain(i, piece, rest, send_sem.at[i, phase, 0], recv_sem.at[i, 0], "send")
                elif size > 2:
                    for here in range(size):
                        def both(here=here, i=i, piece=piece, phase=phase, rest=rest, size=size):
                            if here < size - 1:
                                drain(i, piece, (here + 1) * rest, send_sem.at[i, phase, 0], recv_sem.at[i, 0], "send")
                            if here > 0:
                                drain(i, piece, (size - here) * rest, send_sem.at[i, phase, 1], recv_sem.at[i, 0], "send")
                        pl.when(at == here)(both)
            rest *= size
        for i, piece in pieces:
            if piece.half:
                drain(i, piece, n - 1, pair_send.at[i], pair_recv.at[i], "send")
                drain(i, piece, n - 1, pair_send.at[i], pair_recv.at[i], "recv")


def gather_all(axes, n, arrays, collective_id):
    plan = colours(axes, [a.shape[1] for a in arrays])
    pieces = sum(len(p) for _, p in plan)
    return pl.pallas_call(
        functools.partial(gather_kernel, axes, plan, n),
        out_shape=[jax.ShapeDtypeStruct((n,) + a.shape, a.dtype) for a in arrays],
        in_specs=[pl.BlockSpec(memory_space=ANY)] * len(arrays),
        out_specs=[pl.BlockSpec(memory_space=ANY)] * len(arrays),
        scratch_shapes=[pltpu.VMEM(a.shape, a.dtype) for a in arrays]
        + [
            pltpu.SemaphoreType.DMA((pieces, 3, 2)),
            pltpu.SemaphoreType.DMA((pieces, n)),
            pltpu.SemaphoreType.DMA((pieces,)),
            pltpu.SemaphoreType.DMA((pieces,)),
            pltpu.SemaphoreType.DMA((len(arrays),)),
        ],
        compiler_params=pltpu.CompilerParams(collective_id=collective_id, has_side_effects=True),
        name="gather_all",
    )(*arrays)
def add_into(acc, a, got, g, rows):
    step = min(rows, 16)

    def go(i, _):
        at = pl.ds(pl.multiple_of(i * step, step), step)
        acc[a, at, :] = (acc[a, at, :].astype(jnp.float32) + got[g, at, :].astype(jnp.float32)).astype(acc.dtype)
        return 0

    lax.fori_loop(0, rows // step, go, 0)


def slots(size):
    return 1 if size <= 2 else size + 1


def scatter_kernel(axes, plan, n, *refs):
    k = 5
    ins, outs = refs[:k], refs[k : 2 * k]
    total = sum(len(p) for _, p in plan)
    buffers = refs[2 * k : 2 * k + 5 * total]
    own_sem, pair_send, pair_recv, send_sem, recv_sems, last_send, last_recv = (
        refs[-9], refs[-8], refs[-7], refs[-6], refs[-5:-2], refs[-2], refs[-1]
    )
    me, core = lax.axis_index("fsdp"), lax.axis_index("rep")
    enter(axes, me, core)
    numbered, number = [], 0
    for order, pieces in plan:
        numbered.append((order, [(number + i, p) for i, p in enumerate(pieces)]))
        number += len(pieces)
    acc = [buffers[5 * i] for i in range(total)]
    pair = [buffers[5 * i + 1] for i in range(total)]
    got = [buffers[5 * i + 2 : 5 * i + 5] for i in range(total)]

    def spot(axis):
        return (me // axis[0]) % axis[1]

    def pair_copy(i, piece, block):
        return pltpu.make_async_remote_copy(
            src_ref=ins[piece.array].at[block, :, piece.cols(1 - core)],
            dst_ref=pair[i].at[block],
            send_sem=pair_send.at[i],
            recv_sem=pair_recv.at[i, block],
            device_id=(me, 1 - core),
            device_id_type=MESH,
        )

    def own_copy(i, piece, block):
        return pltpu.make_async_copy(
            ins[piece.array].at[block, :, piece.cols(core)], acc[i].at[block], own_sem.at[i, block]
        )

    def block_at(order, phase, origin, rest):
        stride = order[phase][0]
        block = me + (origin - spot(order[phase])) * stride
        for s, z in order[:phase]:
            here = (me // s) % z
            block = block + (xor(here, z - 1 - rest % z, z) - here) * s
            rest = rest // z
        return block

    def rests(order, phase):
        count = 1
        for _, z in order[:phase]:
            count *= z
        return count

    def ready(pieces, block):
        for i, piece in pieces:
            own_copy(i, piece, block).wait()
            pair_copy(i, piece, block).wait_recv()
            add_into(acc[i], block, pair[i], block, acc[i].shape[1])

    def hop(i, phase, block, rest, slot, send, device):
        return pltpu.make_async_remote_copy(
            src_ref=acc[i].at[block],
            dst_ref=got[i][phase].at[rest, slot],
            send_sem=send,
            recv_sem=recv_sems[phase].at[i, rest * got[i][phase].shape[1] + slot],
            device_id=device,
            device_id_type=MESH,
        )

    def take(pieces, phase, block, rest, slot):
        for i, piece in pieces:
            hop(i, phase, block, rest, slot, send_sem.at[i, phase], (me, 1 - core)).wait_recv()
            add_into(acc[i], block, got[i][phase].at[rest], slot, acc[i].shape[1])

    def give(pieces, phase, block, rest, slot, device):
        for i, piece in pieces:
            hop(i, phase, block, rest, slot, send_sem.at[i, phase], device).start()

    def event(order, pieces, phase, e, first):
        stride, size = order[phase]
        rest_count = rests(order, phase)
        at = spot(order[phase])
        far, rest = size - 1 - e // rest_count, e % rest_count
        origin = xor(at, far, size)
        block = block_at(order, phase, origin, rest)
        if first:
            ready(pieces, block)
        if size == 1:
            return
        if size == 2:
            pl.when(far == 1)(
                lambda: give(pieces, phase, block, rest, 0, (me + (1 - 2 * at) * stride, core))
            )
            pl.when(far == 0)(lambda: take(pieces, phase, block, rest, 0))
            return

        @pl.when(far > 0)
        def _():
            up = (origin > at).astype(jnp.int32)
            behind = jnp.where(up == 1, at > 0, at < size - 1)
            pl.when(behind)(lambda: take(pieces, phase, block, rest, origin))
            step = 2 * up - 1
            landing = jnp.where((up == 0) & (origin == at - 1), size, origin)
            give(pieces, phase, block, rest, landing, (me + step * stride, core))

        @pl.when(far == 0)
        def _():
            pl.when(at > 0)(lambda: take(pieces, phase, block, rest, at))
            pl.when(at < size - 1)(lambda: take(pieces, phase, block, rest, size))

    for stage in range(2):
        for order, pieces in numbered:
            last = order[2]
            count = rests(order, 2)

            def begin(e, _, order=order, pieces=pieces):
                far, rest = order[2][1] - 1 - e // rests(order, 2), e % rests(order, 2)
                block = block_at(order, 2, xor(spot(order[2]), far, order[2][1]), rest)
                for i, piece in pieces:
                    pair_copy(i, piece, block).start()
                    own_copy(i, piece, block).start()
                return 0

            lead = (last[1] - 1) * count
            lax.fori_loop(0 if stage == 0 else lead, lead if stage == 0 else n, begin, 0)

    tasks = []
    for number, (order, pieces) in enumerate(numbered):
        lead = (order[2][1] - 1) * rests(order, 2)
        later = rests(order, 2)
        inner = rests(order, 1)
        tasks.append((number, order, pieces, lead, later, inner))

    def lead_event(order, pieces, e):
        event(order, pieces, 2, e, True)

    def later_event(order, pieces, e, lead, later, inner):
        event(order, pieces, 2, lead + e, True)
        event(order, pieces, 1, e, False)
        pl.when(e >= later - inner)(lambda: event(order, pieces, 0, e - (later - inner), False))

    def loop(count, fns):
        def go(e, _):
            for size, fn in fns:
                if size == count:
                    fn(e)
                else:
                    pl.when(e < size)(lambda fn=fn: fn(e))
            return 0

        lax.fori_loop(0, count, go, 0)

    light, heavy = tasks[:2], tasks[2:]
    loop(max(t[3] for t in heavy), [(t[3], functools.partial(lead_event, t[1], t[2])) for t in heavy])
    both = [(t[3], functools.partial(lead_event, t[1], t[2])) for t in light] + [
        (t[4], functools.partial(lambda e, t: later_event(t[1], t[2], e, *t[3:]), t=t)) for t in heavy
    ]
    loop(max(b[0] for b in both), both)
    loop(
        max(t[4] for t in light),
        [(t[4], functools.partial(lambda e, t: later_event(t[1], t[2], e, *t[3:]), t=t)) for t in light],
    )

    final = []
    for order, pieces in numbered:
        for i, piece in pieces:
            outs[piece.array][:, piece.cols(core)] = acc[i][me]
            if piece.half:
                final.append(
                    pltpu.make_async_remote_copy(
                        src_ref=acc[i].at[me],
                        dst_ref=outs[piece.array].at[:, piece.cols(core)],
                        send_sem=last_send.at[i],
                        recv_sem=last_recv.at[i],
                        device_id=(me, 1 - core),
                        device_id_type=MESH,
                    )
                )
                final[-1].start()
    for copy in final:
        copy.wait()

    def drain(i, phase, count):
        many = acc[i].at[pl.ds(0, count)]
        pltpu.make_async_remote_copy(
            src_ref=many, dst_ref=many, send_sem=send_sem.at[i, phase], recv_sem=last_recv.at[i],
            device_id=(me, 1 - core), device_id_type=MESH,
        ).wait_send()

    for order, pieces in numbered:
        for i, piece in pieces:
            for phase in range(3):
                if order[phase][1] > 1:
                    drain(i, phase, (order[phase][1] - 1) * rests(order, phase))
            many = acc[i].at[pl.ds(0, n)]
            pltpu.make_async_remote_copy(
                src_ref=many, dst_ref=many, send_sem=pair_send.at[i], recv_sem=last_recv.at[i],
                device_id=(me, 1 - core), device_id_type=MESH,
            ).wait_send()


def scatter_all(axes, n, arrays, collective_id):
    plan = colours(axes, [a.shape[2] for a in arrays])
    pieces = [(order, p) for order, ps in plan for p in ps]
    scratch = []
    for order, p in pieces:
        rows, dtype = arrays[p.array].shape[1], arrays[p.array].dtype
        scratch += [pltpu.VMEM((n, rows, p.width), dtype)] * 2
        count = 1
        for phase in range(3):
            size = order[phase][1]
            scratch.append(pltpu.VMEM((count, slots(size), rows, p.width), dtype))
            count *= size
    total = len(pieces)
    shapes = []
    for phase in range(3):
        most = 1
        for order, _ in plan:
            count = slots(order[phase][1])
            for a in order[:phase]:
                count *= a[1]
            most = max(most, count)
        shapes.append((total, most))
    dma = pltpu.SemaphoreType.DMA
    return pl.pallas_call(
        functools.partial(scatter_kernel, axes, plan, n),
        out_shape=[jax.ShapeDtypeStruct(a.shape[1:], a.dtype) for a in arrays],
        in_specs=[pl.BlockSpec(memory_space=ANY)] * len(arrays),
        out_specs=[pl.BlockSpec(memory_space=pltpu.VMEM)] * len(arrays),
        scratch_shapes=scratch
        + [dma((total, n)), dma((total,)), dma((total, n)), dma((total, 3))]
        + [dma(s) for s in shapes]
        + [dma((total,)), dma((total,))],
        compiler_params=pltpu.CompilerParams(
            collective_id=collective_id, has_side_effects=True, vmem_limit_bytes=60 * 1024 * 1024
        ),
        name="scatter_all",
    )(*arrays)


import math

from jax.sharding import PartitionSpec as P

D = 1024
HEADS = 16
HEAD_DIM = 64
SEQ_MAX = 1024
CAP = 128


EPSILON = 1e-06
EXACT_PRECISION = lax.Precision.HIGHEST


def normalize(values, gain):
    inverse = lax.rsqrt(jnp.mean(values * values, axis=-1, keepdims=True) + EPSILON)
    return (values * inverse * gain, inverse)


def rms_back(values, inverse, gain, grad_normed):
    scaled = gain * grad_normed
    grad_values = inverse * scaled - values * inverse**3 * jnp.mean(
        scaled * values, axis=-1, keepdims=True
    )
    grad_gain = jnp.sum(grad_normed * values * inverse, axis=(0, 1))
    return (grad_values, grad_gain)


def split_heads(packed, offset):
    return packed[..., offset : offset + D].reshape(packed.shape[:2] + (HEADS, HEAD_DIM))


def body(
    axes,
    tokens,
    cotangent,
    w_qkv,
    w_out,
    w_up,
    w_down,
    w_router,
    gain_attn,
    gain_mlp,
    lengths,
    routed,
    dealing,
):
    factor = 1.0 / math.sqrt(HEAD_DIM)
    group_seqs = tokens.shape[1]
    per_device = group_seqs // lax.axis_size("fsdp")
    first_seq = lax.axis_index("fsdp") * per_device
    my_ids = lax.dynamic_slice_in_dim(dealing[0], first_seq, per_device)
    picker = my_ids[:, None] == jnp.arange(group_seqs, dtype=jnp.int32)[None, :]
    seq_lengths = jnp.sum(jnp.where(picker, lengths[0][None, :], 0), axis=1)
    seq_routes = jnp.sum(jnp.where(picker[:, :, None], routed[0][None, :, :], 0), axis=1)
    whole_tokens, whole_cot = (
        lax.all_to_all(tokens, "fsdp", split_axis=1, concat_axis=2, tiled=True),
        lax.all_to_all(cotangent, "fsdp", split_axis=1, concat_axis=2, tiled=True),
    )
    sequence_tokens = whole_tokens[0]
    sequence_cotangent = whole_cot[0]
    positions = jnp.arange(SEQ_MAX, dtype=jnp.int32)
    slot_ids = jnp.arange(CAP, dtype=jnp.int32)
    valid_slot = slot_ids[None, :] < (seq_lengths // 8)[:, None]
    selected_slots = (seq_routes[:, :, None] == positions[None, None, :]) & valid_slot[:, :, None]
    one_hot_matrix = selected_slots.astype(jnp.bfloat16)
    touched = jnp.any(selected_slots, axis=1)
    living = positions[None, :] < seq_lengths[:, None]
    incoming_rows = jnp.einsum(
        "puf,pfy->puy", one_hot_matrix, sequence_tokens, preferred_element_type=jnp.float32
    )
    row_gradient = jnp.einsum(
        "puf,pfy->puy", one_hot_matrix, sequence_cotangent, preferred_element_type=jnp.float32
    )
    shards = lax.axis_size("fsdp")
    part = w_router.shape[0]
    vectors = jnp.pad(jnp.stack([w_router, gain_attn, gain_mlp]), ((0, 13), (0, 128 - part)))
    blocks = gather_all(axes, shards, [w_qkv, w_out, w_up, w_down, vectors], 0)
    small = blocks[4][:, :3, :part].transpose(1, 0, 2).reshape(3, D)
    gathered = tuple(b.reshape(-1, b.shape[2]) for b in blocks[:4]) + (small[0], small[1], small[2])
    rows_low = incoming_rows.astype(jnp.bfloat16)
    router_val = jnp.einsum("scd,d->sc", rows_low, gathered[4], preferred_element_type=jnp.float32)
    normed_attn, inverse_attn = normalize(incoming_rows, gathered[5].astype(jnp.float32))
    normed_low = normed_attn.astype(jnp.bfloat16)
    packed = jnp.einsum(
        "scd,de->sce", normed_low, gathered[0], preferred_element_type=jnp.float32
    ).astype(jnp.bfloat16)
    queries = split_heads(packed, 0)
    keys_heads = split_heads(packed, D)
    values_heads = split_heads(packed, 2 * D)
    scores = (
        jnp.einsum("sqhe,skhe->shqk", queries, keys_heads, preferred_element_type=jnp.float32)
        * factor
    )
    allowed = (slot_ids[None, :] <= slot_ids[:, None])[None, None] & valid_slot[:, None, None, :]
    scores = jnp.where(allowed, scores, -1e30)
    probs = jax.nn.softmax(scores, axis=-1)
    probs_low = probs.astype(jnp.bfloat16)
    attended = jnp.einsum(
        "shqk,skhe->sqhe", probs_low, values_heads, preferred_element_type=jnp.float32
    ).astype(jnp.bfloat16)
    attended = attended.reshape(incoming_rows.shape)
    branch_attn = jnp.einsum(
        "sce,ed->scd", attended, gathered[1], preferred_element_type=jnp.float32
    )
    middle = incoming_rows + branch_attn
    normed_mid, inverse_mid = normalize(middle, gathered[6].astype(jnp.float32))
    normed_mid_low = normed_mid.astype(jnp.bfloat16)
    upward = jnp.einsum(
        "scd,df->scf", normed_mid_low, gathered[2], preferred_element_type=jnp.float32
    )
    activated = jax.nn.gelu(upward).astype(jnp.bfloat16)
    branch_mlp = jnp.einsum(
        "scf,fd->scd", activated, gathered[3], preferred_element_type=jnp.float32
    )
    combined = branch_attn + branch_mlp
    refreshed_rows = (incoming_rows + router_val[..., None] * combined).astype(jnp.bfloat16)
    scattered = jnp.einsum(
        "jyv,jyi->jvi", one_hot_matrix, refreshed_rows, preferred_element_type=jnp.float32
    ).astype(jnp.bfloat16)
    output_seq = jnp.where(touched[..., None], scattered, sequence_tokens)
    output_seq = jnp.where(living[..., None], output_seq, jnp.zeros_like(output_seq))
    back_weights = gathered
    grad_comb = router_val[..., None] * row_gradient
    grad_router_val = jnp.sum(row_gradient * combined, axis=-1)
    total_gradient = row_gradient + grad_router_val[..., None] * back_weights[4].astype(jnp.float32)
    grad_mlp_low = grad_comb.astype(jnp.bfloat16)
    grad_act = jnp.einsum(
        "scd,fd->scf", grad_mlp_low, back_weights[3], preferred_element_type=jnp.float32
    )
    grad_downw = jnp.einsum(
        "scf,scd->fd", activated, grad_mlp_low, preferred_element_type=jnp.float32
    )
    unused, gelu_pull = jax.vjp(jax.nn.gelu, upward)
    grad_up_low = gelu_pull(grad_act)[0].astype(jnp.bfloat16)
    grad_normed_mid = jnp.einsum(
        "scf,df->scd", grad_up_low, back_weights[2], preferred_element_type=jnp.float32
    )
    grad_upw = jnp.einsum(
        "scd,scf->df", normed_mid_low, grad_up_low, preferred_element_type=jnp.float32
    )
    grad_middle, grad_gain_second = rms_back(
        middle, inverse_mid, back_weights[6].astype(jnp.float32), grad_normed_mid
    )
    grad_attn_low = (grad_comb + grad_middle).astype(jnp.bfloat16)
    total_gradient = total_gradient + grad_middle
    grad_attended = jnp.einsum(
        "scd,ed->sce", grad_attn_low, back_weights[1], preferred_element_type=jnp.float32
    ).astype(jnp.bfloat16)
    grad_outw = jnp.einsum(
        "sce,scd->ed", attended, grad_attn_low, preferred_element_type=jnp.float32
    )
    grad_att_heads = grad_attended.reshape(queries.shape)
    grad_probs = jnp.einsum(
        "sqhe,skhe->shqk", grad_att_heads, values_heads, preferred_element_type=jnp.float32
    )
    grad_values = jnp.einsum(
        "shqk,sqhe->skhe", probs_low, grad_att_heads, preferred_element_type=jnp.float32
    )
    grad_scores = probs * (grad_probs - jnp.sum(probs * grad_probs, axis=-1, keepdims=True))
    grad_scores_low = grad_scores.astype(jnp.bfloat16)
    grad_queries = (
        jnp.einsum(
            "shqk,skhe->sqhe", grad_scores_low, keys_heads, preferred_element_type=jnp.float32
        )
        * factor
    )
    grad_keys = (
        jnp.einsum("shqk,sqhe->skhe", grad_scores_low, queries, preferred_element_type=jnp.float32)
        * factor
    )
    flat_shape = incoming_rows.shape
    grad_packed = jnp.concatenate(
        [
            grad_queries.reshape(flat_shape),
            grad_keys.reshape(flat_shape),
            grad_values.reshape(flat_shape),
        ],
        axis=-1,
    ).astype(jnp.bfloat16)
    grad_qkvw = jnp.einsum(
        "scd,sce->de", normed_low, grad_packed, preferred_element_type=jnp.float32
    )
    grad_normed_attn = jnp.einsum(
        "sce,de->scd", grad_packed, back_weights[0], preferred_element_type=jnp.float32
    )
    grad_first_rows, grad_gain_first = rms_back(
        incoming_rows, inverse_attn, back_weights[5].astype(jnp.float32), grad_normed_attn
    )
    total_gradient = total_gradient + grad_first_rows
    grad_routerw = jnp.einsum(
        "scd,sc->d", incoming_rows, grad_router_val, precision=EXACT_PRECISION
    )
    spread_back = jnp.einsum(
        "jyv,jyi->jvi",
        selected_slots.astype(jnp.float32),
        total_gradient,
        precision=EXACT_PRECISION,
    )
    grad_seq = jnp.where(touched[..., None], spread_back, sequence_cotangent.astype(jnp.float32))
    grad_seq = jnp.where(living[..., None], grad_seq, jnp.zeros_like(grad_seq)).astype(jnp.bfloat16)
    small_grads = jnp.stack([grad_routerw, grad_gain_first, grad_gain_second])
    small_grads = small_grads.reshape(3, shards, part).transpose(1, 0, 2)
    small_grads = jnp.pad(small_grads, ((0, 0), (0, 5), (0, 128 - part)))
    partial = [
        g.astype(jnp.bfloat16).reshape(shards, -1, g.shape[1])
        for g in (grad_qkvw, grad_outw, grad_upw, grad_downw)
    ]
    shares = scatter_all(axes, shards, partial + [small_grads], 1)
    totals = tuple(t.astype(jnp.float32) for t in shares[:4]) + tuple(shares[4][j, :part] for j in range(3))
    back_out, back_grad = (
        lax.all_to_all(output_seq[None], "fsdp", split_axis=2, concat_axis=1, tiled=True),
        lax.all_to_all(grad_seq[None], "fsdp", split_axis=2, concat_axis=1, tiled=True),
    )
    return (
        back_out,
        back_grad,
        totals[0],
        totals[1],
        totals[2],
        totals[3],
        totals[4],
        totals[5],
        totals[6],
    )


def solution(mesh):
    placed = (
        P("rep", None, "fsdp", None),
        P("rep", None, "fsdp", None),
        P("fsdp", None),
        P("fsdp", None),
        P("fsdp", None),
        P("fsdp", None),
        P("fsdp"),
        P("fsdp"),
        P("fsdp"),
        P("rep", None),
        P("rep", None, None),
        P("rep", None),
    )
    return jax.shard_map(
        functools.partial(body, grid_axes(mesh)),
        mesh=mesh,
        in_specs=placed,
        out_specs=(
            P("rep", None, "fsdp", None),
            P("rep", None, "fsdp", None),
            P("fsdp", None),
            P("fsdp", None),
            P("fsdp", None),
            P("fsdp", None),
            P("fsdp"),
            P("fsdp"),
            P("fsdp"),
        ),
        check_vma=False,
    )
```

```python
import functools

import jax
import jax.numpy as jnp
from jax import lax
from jax.experimental import pallas as pl
from jax.experimental.pallas import tpu as pltpu

MESH = pl.DeviceIdType.MESH
ANY = pl.ANY


def grid_axes(mesh):
    devices = mesh.devices[:, 0]
    count = len(devices)
    axes = []
    spots = [getattr(d, "coords", None) for d in devices]
    if all(s is not None for s in spots) and len(set(map(tuple, spots))) == count:
        low = [min(s[k] for s in spots) for k in range(3)]
        at = {tuple(s[k] - low[k] for k in range(3)): f for f, s in enumerate(spots)}
        for k in range(3):
            size = max(s[k] for s in spots) - low[k] + 1
            one = tuple(int(j == k) for j in range(3))
            axes.append((at[one] if size > 1 else 1, size, k))
        ok = all(
            f == sum(stride * spot[k] for stride, _, k in axes) for spot, f in at.items()
        )
        axes = [a[:2] for a in axes] if ok else []
    if not axes:
        axes, left = [], count
        for size in (2, 2):
            size = size if left % size == 0 and left > 1 else 1
            axes.append((count // left, size))
            left //= size
        axes.append((count // left, left))
    return sorted(axes, key=lambda a: -a[1])


def xor(a, b, size):
    out, bit = 0, 1
    while bit < size:
        out = out + ((a // bit + b // bit) % 2) * bit
        bit *= 2
    return out


class Piece:
    def __init__(self, array, half, offset, width):
        self.array, self.half, self.offset, self.width = array, half, offset, width

    def cols(self, core):
        start = self.offset
        if self.half:
            start = core * self.half + start
            start = pl.multiple_of(start, 128)
        return pl.ds(start, self.width)


def colours(axes, widths):
    qkv, out, up, down = (w // 2 for w in widths[:4])
    a, b, c = axes
    third = qkv // 3
    return [
        ((b, c, a), [Piece(1, out, 0, out), Piece(4, 0, 0, widths[4])]),
        ((c, b, a), [Piece(0, qkv, 0, third)]),
        ((a, b, c), [Piece(2, up, 0, up), Piece(0, qkv, third, third)]),
        ((a, c, b), [Piece(3, down, 0, down), Piece(0, qkv, 2 * third, third)]),
    ]


def enter(n, me, core):
    barrier = pltpu.get_barrier_semaphore()

    def hello(i, _):
        pl.semaphore_signal(barrier, inc=1, device_id=((me + i) % n, core), device_id_type=MESH)
        return 0

    lax.fori_loop(1, n, hello, 0)
    pl.semaphore_signal(barrier, inc=1, device_id=(me, 1 - core), device_id_type=MESH)
    pl.semaphore_wait(barrier, n)


def rows_out(n, me, core, rows, landing, send_sem, recv_sem, own_sem):
    own = pltpu.make_async_copy(rows.at[me], landing.at[me], own_sem)
    own.start()

    def go(i, _):
        to = (me + i) % n
        pltpu.make_async_remote_copy(
            src_ref=rows.at[to], dst_ref=landing.at[me], send_sem=send_sem, recv_sem=recv_sem,
            device_id=(to, core), device_id_type=MESH,
        ).start()
        return 0

    lax.fori_loop(1, n, go, 0)
    return own


def rows_wait(n, me, core, rows, landing, send_sem, recv_sem, own):
    own.wait()
    for which in range(2):
        copy = pltpu.make_async_remote_copy(
            src_ref=rows.at[pl.ds(0, n - 1)], dst_ref=landing.at[pl.ds(0, n - 1)],
            send_sem=send_sem, recv_sem=recv_sem, device_id=(me, 1 - core), device_id_type=MESH,
        )
        copy.wait_recv() if which else copy.wait_send()


def gather_kernel(axes, plan, n, *refs):
    k = 5
    ins, rows, flag = refs[:k], refs[k], refs[k + 1]
    outs, landing, other = refs[k + 2 : 2 * k + 2], refs[2 * k + 2], refs[2 * k + 3]
    stages = refs[2 * k + 4 : 3 * k + 4]
    send_sem, recv_sem, pair_send, pair_recv, local_sem, row_sems = refs[3 * k + 4 :]
    me, core = lax.axis_index("fsdp"), lax.axis_index("rep")
    enter(n, me, core)
    told = pltpu.make_async_remote_copy(
        src_ref=flag, dst_ref=other, send_sem=row_sems.at[3], recv_sem=row_sems.at[4],
        device_id=(me, 1 - core), device_id_type=MESH,
    )
    told.start()
    numbered, number = [], 0
    for order, pieces in plan:
        numbered.append((order, [(number + i, p) for i, p in enumerate(pieces)]))
        number += len(pieces)

    def spot(axis):
        return (me // axis[0]) % axis[1]

    def dst(piece, block):
        return outs[piece.array].at[block, :, piece.cols(core)]

    def put(pieces, block, own, phase, way, device, pair=False):
        for i, piece in pieces:
            if pair and not piece.half:
                continue
            src = ins[piece.array].at[:, piece.cols(core)] if own else dst(piece, block)
            pltpu.make_async_remote_copy(
                src_ref=src,
                dst_ref=dst(piece, block),
                send_sem=pair_send.at[i] if pair else send_sem.at[i, phase, way],
                recv_sem=pair_recv.at[i] if pair else recv_sem.at[i, block],
                device_id=device,
                device_id_type=MESH,
            ).start()

    def along(pieces, order, block, own, phase, ways):
        stride, size = order[phase]
        at = spot(order[phase])
        if size == 1:
            return
        if size == 2:
            put(pieces, block, own, phase, 0, (me + (1 - 2 * at) * stride, core))
            return
        for way in ways:
            step = 1 - 2 * way
            pl.when(at < size - 1 if way == 0 else at > 0)(
                functools.partial(put, pieces, block, own, phase, way, (me + step * stride, core))
            )

    def arrived(pieces, order, block, phase, way):
        for i, piece in pieces:
            pltpu.make_async_remote_copy(
                src_ref=dst(piece, block),
                dst_ref=dst(piece, block),
                send_sem=send_sem.at[i, phase, way],
                recv_sem=recv_sem.at[i, block],
                device_id=(me, 1 - core),
                device_id_type=MESH,
            ).wait_recv()
        if order[phase][1] > 2:
            along(pieces, order, block, False, phase, (way,))
        for later in range(phase + 1, 3):
            along(pieces, order, block, False, later, (0, 1))
        put(pieces, block, False, 0, 0, (me, 1 - core), pair=True)

    for order, pieces in numbered:
        for phase in range(3):
            along(pieces, order, me, True, phase, (0, 1))
    own = rows_out(n, me, core, rows, landing, row_sems.at[0], row_sems.at[1], row_sems.at[2])
    local = []
    for j in range(k):
        local.append(pltpu.make_async_copy(ins[j], stages[j], local_sem.at[j]))
        local[-1].start()
    events = []
    for number, (order, pieces) in enumerate(numbered):
        heavy = number >= 2
        sizes = [a[1] for a in order]
        for phase in range(3):
            size = sizes[phase]
            rest = 1
            for s in sizes[:phase]:
                rest *= s
            for t in range(1, size):
                ways = (0,) if size == 2 else (0, 1)
                for way in ways:
                    for j in range(rest):
                        if heavy:
                            key = 20 * t if phase == 0 else 20 * phase + 20 * (j + (t - 1) * rest + 1)
                        else:
                            key = 5 if phase == 0 else 10 + 5 * j if phase == 1 else 15 + 40 * t + 5 * j
                        events.append((key, len(events), order, pieces, phase, t, way, j))
    events.sort(key=lambda e: e[:2])

    def run(order, pieces, phase, t, way, j):
        stride, size = order[phase]
        at = spot(order[phase])
        origin = 1 - at if size == 2 else at - (1 - 2 * way) * t
        block = me + (origin - at) * stride
        for s, z in order[:phase]:
            here = (me // s) % z
            block = block + (xor(here, j % z, z) - here) * s
            j = j // z
        if size == 2:
            arrived(pieces, order, block, phase, 0)
        else:
            pl.when((origin >= 0) & (origin < size))(
                functools.partial(arrived, pieces, order, block, phase, way)
            )

    def settle():
        for j in range(k):
            local[j].wait()
            local[j] = pltpu.make_async_copy(stages[j], outs[j].at[me], local_sem.at[j])
            local[j].start()

    for number, (_, _, order, pieces, phase, t, way, j) in enumerate(events):
        run(order, pieces, phase, t, way, j)
        if number == 3:
            settle()
    for copy in local:
        copy.wait()
    told.wait()
    rows_wait(n, me, core, rows, landing, row_sems.at[0], row_sems.at[1], own)

    def drain(i, piece, count, send, recv, which):
        many = outs[piece.array].at[pl.ds(0, count), :, piece.cols(core)]
        copy = pltpu.make_async_remote_copy(
            src_ref=many, dst_ref=many, send_sem=send, recv_sem=recv,
            device_id=(me, 1 - core), device_id_type=MESH,
        )
        if which == "send":
            copy.wait_send()
        else:
            copy.wait_recv()

    for order, pieces in numbered:
        rest = 1
        for phase in range(3):
            stride, size = order[phase]
            at = spot(order[phase])
            for i, piece in pieces:
                if size == 2:
                    drain(i, piece, rest, send_sem.at[i, phase, 0], recv_sem.at[i, 0], "send")
                elif size > 2:
                    for here in range(size):
                        def both(here=here, i=i, piece=piece, phase=phase, rest=rest, size=size):
                            if here < size - 1:
                                drain(i, piece, (here + 1) * rest, send_sem.at[i, phase, 0], recv_sem.at[i, 0], "send")
                            if here > 0:
                                drain(i, piece, (size - here) * rest, send_sem.at[i, phase, 1], recv_sem.at[i, 0], "send")
                        pl.when(at == here)(both)
            rest *= size
        for i, piece in pieces:
            if piece.half:
                drain(i, piece, n - 1, pair_send.at[i], pair_recv.at[i], "send")
                drain(i, piece, n - 1, pair_send.at[i], pair_recv.at[i], "recv")


def gather_all(axes, n, arrays, rows, flag, collective_id):
    plan = colours(axes, [a.shape[1] for a in arrays])
    pieces = sum(len(p) for _, p in plan)
    vmem = pl.BlockSpec(memory_space=pltpu.VMEM)
    anywhere = pl.BlockSpec(memory_space=ANY)
    dma = pltpu.SemaphoreType.DMA
    return pl.pallas_call(
        functools.partial(gather_kernel, axes, plan, n),
        out_shape=[jax.ShapeDtypeStruct((n,) + a.shape, a.dtype) for a in arrays]
        + [jax.ShapeDtypeStruct(a.shape, a.dtype) for a in (rows, flag)],
        in_specs=[anywhere] * len(arrays) + [vmem, vmem],
        out_specs=[anywhere] * (len(arrays) + 1) + [vmem],
        scratch_shapes=[pltpu.VMEM(a.shape, a.dtype) for a in arrays]
        + [dma((pieces, 3, 2)), dma((pieces, n)), dma((pieces,)), dma((pieces,)), dma((len(arrays),)), dma((5,))],
        compiler_params=pltpu.CompilerParams(collective_id=collective_id, has_side_effects=True),
        name="gather_all",
    )(*arrays, rows, flag)
def add_into(acc, a, got, g, rows):
    step = min(rows, 16)

    def go(i, _):
        at = pl.ds(pl.multiple_of(i * step, step), step)
        acc[a, at, :] = (acc[a, at, :].astype(jnp.float32) + got[g, at, :].astype(jnp.float32)).astype(acc.dtype)
        return 0

    lax.fori_loop(0, rows // step, go, 0)


def turn(at, t, size):
    if size == 2:
        return at + (1 - 2 * at) * (1 - t)
    up = size - 1 - at
    first_up = jnp.where(t < up, size - 1 - t, t - up)
    first_down = jnp.where(t < at, t, size - 1 - (t - at))
    return jnp.where(t == size - 1, at, jnp.where(2 * at < size, first_up, first_down))


def slots(size):
    return 1 if size <= 2 else size + 1


def scatter_kernel(axes, plan, n, *refs):
    k = 5
    ins, rows, outs, landing = refs[:k], refs[k], refs[k + 1 : 2 * k + 1], refs[2 * k + 1]
    total = sum(len(p) for _, p in plan)
    buffers = refs[2 * k + 2 : 2 * k + 2 + 5 * total]
    own_sem, pair_send, pair_recv, send_sem = refs[-10:-6]
    recv_sems, last_send, last_recv, row_sems = refs[-6:-3], refs[-3], refs[-2], refs[-1]
    me, core = lax.axis_index("fsdp"), lax.axis_index("rep")
    enter(n, me, core)
    numbered, number = [], 0
    for order, pieces in plan:
        numbered.append((order, [(number + i, p) for i, p in enumerate(pieces)]))
        number += len(pieces)
    acc = [buffers[5 * i] for i in range(total)]
    pair = [buffers[5 * i + 1] for i in range(total)]
    got = [buffers[5 * i + 2 : 5 * i + 5] for i in range(total)]

    def spot(axis):
        return (me // axis[0]) % axis[1]

    def pair_copy(i, piece, block):
        return pltpu.make_async_remote_copy(
            src_ref=ins[piece.array].at[block, :, piece.cols(1 - core)],
            dst_ref=pair[i].at[block],
            send_sem=pair_send.at[i],
            recv_sem=pair_recv.at[i, block],
            device_id=(me, 1 - core),
            device_id_type=MESH,
        )

    def own_copy(i, piece, block):
        return pltpu.make_async_copy(
            ins[piece.array].at[block, :, piece.cols(core)], acc[i].at[block], own_sem.at[i, block]
        )

    def block_at(order, phase, origin, turns):
        block = me + (origin - spot(order[phase])) * order[phase][0]
        for axis, t in zip(order[:phase], turns):
            block = block + (turn(spot(axis), t, axis[1]) - spot(axis)) * axis[0]
        return block

    def ready(pieces, block):
        for i, piece in pieces:
            own_copy(i, piece, block).wait()
            pair_copy(i, piece, block).wait_recv()
            add_into(acc[i], block, pair[i], block, acc[i].shape[1])

    def hop(i, phase, block, rest, slot, send, device):
        return pltpu.make_async_remote_copy(
            src_ref=acc[i].at[block],
            dst_ref=got[i][phase].at[rest, slot],
            send_sem=send,
            recv_sem=recv_sems[phase].at[i, rest * got[i][phase].shape[1] + slot],
            device_id=device,
            device_id_type=MESH,
        )

    def take(pieces, phase, block, rest, slot):
        for i, piece in pieces:
            hop(i, phase, block, rest, slot, send_sem.at[i, phase], (me, 1 - core)).wait_recv()
            add_into(acc[i], block, got[i][phase].at[rest], slot, acc[i].shape[1])

    def give(pieces, phase, block, rest, slot, device):
        for i, piece in pieces:
            hop(i, phase, block, rest, slot, send_sem.at[i, phase], device).start()

    def event(order, pieces, phase, t, turns, first):
        stride, size = order[phase]
        at = spot(order[phase])
        origin = turn(at, t, size)
        mine = t == size - 1
        block = block_at(order, phase, origin, turns)
        rest = 0
        for axis, away in zip(order[:phase], turns):
            rest = rest * axis[1] + away
        if first:
            ready(pieces, block)
        if size == 1:
            return
        if size == 2:
            pl.when(jnp.logical_not(mine))(
                lambda: give(pieces, phase, block, rest, 0, (me + (1 - 2 * at) * stride, core))
            )
            pl.when(mine)(lambda: take(pieces, phase, block, rest, 0))
            return

        @pl.when(jnp.logical_not(mine))
        def _():
            up = (origin > at).astype(jnp.int32)
            behind = jnp.where(up == 1, at > 0, at < size - 1)
            pl.when(behind)(lambda: take(pieces, phase, block, rest, origin))
            step = 2 * up - 1
            landing = jnp.where((up == 0) & (origin == at - 1), size, origin)
            give(pieces, phase, block, rest, landing, (me + step * stride, core))

        @pl.when(mine)
        def _():
            pl.when(at > 0)(lambda: take(pieces, phase, block, rest, at))
            pl.when(at < size - 1)(lambda: take(pieces, phase, block, rest, size))

    def each(count, fn):
        lax.fori_loop(0, count, lambda e, _: (fn(e), 0)[1], 0)

    def begin(order, pieces, s):
        _, (_, nq), (_, nr) = order

        def go(e):
            block = block_at(order, 2, turn(spot(order[2]), e // nq, nr), (s, e % nq))
            for i, piece in pieces:
                pair_copy(i, piece, block).start()
                own_copy(i, piece, block).start()

        each(nr * nq, go)

    def lead(order, pieces, s):
        _, (_, nq), (_, nr) = order
        each((nr - 1) * nq, lambda e: event(order, pieces, 2, e // nq, (s, e % nq), True))

    def later(order, pieces, s, low, high):
        def go(e):
            event(order, pieces, 2, order[2][1] - 1, (s, low + e), True)
            event(order, pieces, 1, low + e, (s,), False)

        each(high - low, go)

    def finish(order, pieces, s):
        event(order, pieces, 0, s, (), False)

    light, heavy = numbered[:2], numbered[2:]
    steps, few = heavy[0][0][0][1], max(c[0][0][1] for c in light)

    def begin_all(s):
        for colour in heavy:
            pl.when(s < steps)(lambda colour=colour: begin(*colour, s))
        for colour in light:
            pl.when(s < colour[0][0][1])(lambda colour=colour: begin(*colour, s))

    each(max(steps, few), begin_all)
    own = rows_out(n, me, core, rows, landing, row_sems.at[0], row_sems.at[1], row_sems.at[2])
    for colour in heavy + light:
        lead(*colour, 0)

    def step(s):
        for colour in heavy:
            pl.when(s < steps)(lambda colour=colour: later(*colour, s, 0, 1))
        for colour in heavy:
            pl.when(s + 1 < steps)(lambda colour=colour: lead(*colour, s + 1))
        for colour in heavy:
            pl.when((s >= 1) & (s < steps))(lambda colour=colour: finish(*colour, s - 1))
        for colour in light:
            size = colour[0][0][1]
            pl.when(s + 1 < size)(lambda colour=colour: lead(*colour, s + 1))
        for colour in heavy:
            pl.when(s < steps)(lambda colour=colour: later(*colour, s, 1, colour[0][1][1]))
        for colour in light:
            size = colour[0][0][1]

            @pl.when((s >= 1) & (s <= size))
            def _(colour=colour):
                later(*colour, s - 1, 0, colour[0][1][1])
                finish(*colour, s - 1)
        for colour in heavy:
            pl.when(s == steps - 1)(lambda colour=colour: finish(*colour, s))

    each(max(steps, few + 1), step)

    final = []
    for order, pieces in numbered:
        for i, piece in pieces:
            outs[piece.array][:, piece.cols(core)] = acc[i][me]
            if piece.half:
                final.append(
                    pltpu.make_async_remote_copy(
                        src_ref=acc[i].at[me],
                        dst_ref=outs[piece.array].at[:, piece.cols(core)],
                        send_sem=last_send.at[i],
                        recv_sem=last_recv.at[i],
                        device_id=(me, 1 - core),
                        device_id_type=MESH,
                    )
                )
                final[-1].start()
    for copy in final:
        copy.wait()
    rows_wait(n, me, core, rows, landing, row_sems.at[0], row_sems.at[1], own)

    def drain(i, phase, count):
        many = acc[i].at[pl.ds(0, count)]
        pltpu.make_async_remote_copy(
            src_ref=many, dst_ref=many, send_sem=send_sem.at[i, phase], recv_sem=last_recv.at[i],
            device_id=(me, 1 - core), device_id_type=MESH,
        ).wait_send()

    for order, pieces in numbered:
        for i, piece in pieces:
            for phase in range(3):
                if order[phase][1] > 1:
                    count = order[phase][1] - 1
                    for axis in order[:phase]:
                        count *= axis[1]
                    drain(i, phase, count)
            many = acc[i].at[pl.ds(0, n)]
            pltpu.make_async_remote_copy(
                src_ref=many, dst_ref=many, send_sem=pair_send.at[i], recv_sem=last_recv.at[i],
                device_id=(me, 1 - core), device_id_type=MESH,
            ).wait_send()


def scatter_all(axes, n, arrays, rows, collective_id):
    plan = colours(axes, [a.shape[2] for a in arrays])
    pieces = [(order, p) for order, ps in plan for p in ps]
    scratch = []
    for order, p in pieces:
        deep, dtype = arrays[p.array].shape[1], arrays[p.array].dtype
        scratch += [pltpu.VMEM((n, deep, p.width), dtype)] * 2
        count = 1
        for phase in range(3):
            size = order[phase][1]
            scratch.append(pltpu.VMEM((count, slots(size), deep, p.width), dtype))
            count *= size
    total = len(pieces)
    shapes = []
    for phase in range(3):
        most = 1
        for order, _ in plan:
            count = slots(order[phase][1])
            for a in order[:phase]:
                count *= a[1]
            most = max(most, count)
        shapes.append((total, most))
    dma = pltpu.SemaphoreType.DMA
    return pl.pallas_call(
        functools.partial(scatter_kernel, axes, plan, n),
        out_shape=[jax.ShapeDtypeStruct(a.shape[1:], a.dtype) for a in arrays]
        + [jax.ShapeDtypeStruct(rows.shape, rows.dtype)],
        in_specs=[pl.BlockSpec(memory_space=ANY)] * len(arrays) + [pl.BlockSpec(memory_space=pltpu.VMEM)],
        out_specs=[pl.BlockSpec(memory_space=pltpu.VMEM)] * len(arrays) + [pl.BlockSpec(memory_space=ANY)],
        scratch_shapes=scratch
        + [dma((total, n)), dma((total,)), dma((total, n)), dma((total, 3))]
        + [dma(s) for s in shapes]
        + [dma((total,)), dma((total,)), dma((3,))],
        compiler_params=pltpu.CompilerParams(
            collective_id=collective_id, has_side_effects=True, vmem_limit_bytes=60 * 1024 * 1024
        ),
        name="scatter_all",
    )(*arrays, rows)


import math

from jax.sharding import PartitionSpec as P

D = 1024
HEADS = 16
HEAD_DIM = 64
SEQ_MAX = 1024
CAP = 128
PAST = 1 << 24


EPSILON = 1e-06
EXACT_PRECISION = lax.Precision.HIGHEST


def normalize(values, gain):
    inverse = lax.rsqrt(jnp.mean(values * values, axis=-1, keepdims=True) + EPSILON)
    return (values * inverse * gain, inverse)


def rms_back(values, inverse, gain, grad_normed):
    scaled = gain * grad_normed
    grad_values = inverse * scaled - values * inverse**3 * jnp.mean(
        scaled * values, axis=-1, keepdims=True
    )
    grad_gain = jnp.sum(grad_normed * values * inverse, axis=(0, 1))
    return (grad_values, grad_gain)


def split_heads(packed, offset):
    return packed[..., offset : offset + D].reshape(packed.shape[:2] + (HEADS, HEAD_DIM))


def body(
    axes,
    tokens,
    cotangent,
    w_qkv,
    w_out,
    w_up,
    w_down,
    w_router,
    gain_attn,
    gain_mlp,
    lengths,
    routed,
    dealing,
):
    factor = 1.0 / math.sqrt(HEAD_DIM)
    shards, place = lax.axis_size("fsdp"), lax.axis_index("fsdp")
    group_seqs, width = tokens.shape[1], tokens.shape[2]
    cap = min(24, width)
    slot_ids = jnp.arange(CAP, dtype=jnp.int32)
    picker = dealing[0][:, None] == jnp.arange(group_seqs, dtype=jnp.int32)[None, :]
    row_lengths = jnp.sum(jnp.where(picker, lengths[0][None, :], 0), axis=1)
    row_routes = jnp.sum(jnp.where(picker[:, :, None], routed[0][None, :, :], 0), axis=1)
    row_routes = jnp.where(slot_ids[None, :] < (row_lengths // 8)[:, None], row_routes, PAST)
    here = place * width + jnp.arange(width, dtype=jnp.int32)
    below = jnp.sum((row_routes[:, :, None] < here[None, None, :]).astype(jnp.int32), axis=1)
    upto = jnp.sum((row_routes[:, :, None] <= here[None, None, :]).astype(jnp.int32), axis=1)
    touched = upto > below
    living = here[None, :] < row_lengths[:, None]
    rank = jnp.where(touched, below - below[:, :1], -1)
    select = (rank[:, None, :] == jnp.arange(cap, dtype=jnp.int32)[None, :, None]).astype(jnp.bfloat16)
    shard_of = row_routes // width
    crowd = jnp.sum(
        (shard_of[:, :, None] == jnp.arange(shards, dtype=jnp.int32)[None, None, :]).astype(jnp.int32), axis=1
    )
    flag = jnp.broadcast_to((jnp.max(crowd) > cap).astype(jnp.float32), (8, 128))
    packed_rows = jnp.concatenate(
        [
            jnp.einsum("jip,jpd->jid", select, t[0], preferred_element_type=jnp.float32).astype(jnp.bfloat16)
            for t in (tokens, cotangent)
        ],
        axis=1,
    )
    seq_lengths = lax.dynamic_slice_in_dim(row_lengths, place, 1)
    routes = lax.dynamic_slice_in_dim(row_routes, place, 1)[0]
    valid_slot = slot_ids[None, :] < (seq_lengths // 8)[:, None]
    seq_shard = routes // width
    seq_rank = slot_ids - jnp.sum((routes[None, :] < (seq_shard * width)[:, None]).astype(jnp.int32), axis=1)
    fits = valid_slot[0] & (seq_rank < cap)
    landing = jnp.where(fits, seq_shard * (2 * cap) + seq_rank, -1)
    cells = jnp.arange(shards * 2 * cap, dtype=jnp.int32)
    pick = jnp.concatenate([landing[:, None] == cells[None, :], (landing[:, None] == (cells - cap)[None, :]) & fits[:, None]])
    pick = pick.astype(jnp.bfloat16)
    part = w_router.shape[0]
    vectors = jnp.pad(jnp.stack([w_router, gain_attn, gain_mlp]), ((0, 13), (0, 128 - part)))
    blocks = gather_all(axes, shards, [w_qkv, w_out, w_up, w_down, vectors], packed_rows, flag, 0)
    crowded = jnp.maximum(flag, blocks[6])[0, 0] > 0
    got_rows = jnp.einsum(
        "cs,sd->cd", pick, blocks[5].reshape(-1, D), preferred_element_type=jnp.float32
    ).astype(jnp.bfloat16)

    def all_rows(got):
        positions = jnp.arange(SEQ_MAX, dtype=jnp.int32)
        onehot = (routes[:, None] == positions[None, :]).astype(jnp.bfloat16)
        return jnp.concatenate(
            [
                jnp.dot(
                    onehot,
                    lax.all_to_all(t, "fsdp", split_axis=1, concat_axis=2, tiled=True)[0, 0],
                    preferred_element_type=jnp.float32,
                ).astype(jnp.bfloat16)
                for t in (tokens, cotangent)
            ]
        )

    if cap < width:
        got_rows = lax.cond(crowded, all_rows, lambda got: got, got_rows)
    rows_low = got_rows[None, :CAP]
    incoming_rows = rows_low.astype(jnp.float32)
    row_gradient = got_rows[None, CAP:].astype(jnp.float32)
    small = blocks[4][:, :3, :part].transpose(1, 0, 2).reshape(3, D)
    gathered = tuple(b.reshape(-1, b.shape[2]) for b in blocks[:4]) + (small[0], small[1], small[2])
    router_val = jnp.einsum("scd,d->sc", rows_low, gathered[4], preferred_element_type=jnp.float32)
    normed_attn, inverse_attn = normalize(incoming_rows, gathered[5].astype(jnp.float32))
    normed_low = normed_attn.astype(jnp.bfloat16)
    packed = jnp.einsum(
        "scd,de->sce", normed_low, gathered[0], preferred_element_type=jnp.float32
    ).astype(jnp.bfloat16)
    queries = split_heads(packed, 0)
    keys_heads = split_heads(packed, D)
    values_heads = split_heads(packed, 2 * D)
    scores = (
        jnp.einsum("sqhe,skhe->shqk", queries, keys_heads, preferred_element_type=jnp.float32)
        * factor
    )
    allowed = (slot_ids[None, :] <= slot_ids[:, None])[None, None] & valid_slot[:, None, None, :]
    scores = jnp.where(allowed, scores, -1e30)
    probs = jax.nn.softmax(scores, axis=-1)
    probs_low = probs.astype(jnp.bfloat16)
    attended = jnp.einsum(
        "shqk,skhe->sqhe", probs_low, values_heads, preferred_element_type=jnp.float32
    ).astype(jnp.bfloat16)
    attended = attended.reshape(incoming_rows.shape)
    branch_attn = jnp.einsum(
        "sce,ed->scd", attended, gathered[1], preferred_element_type=jnp.float32
    )
    middle = incoming_rows + branch_attn
    normed_mid, inverse_mid = normalize(middle, gathered[6].astype(jnp.float32))
    normed_mid_low = normed_mid.astype(jnp.bfloat16)
    upward = jnp.einsum(
        "scd,df->scf", normed_mid_low, gathered[2], preferred_element_type=jnp.float32
    )
    activated = jax.nn.gelu(upward).astype(jnp.bfloat16)
    branch_mlp = jnp.einsum(
        "scf,fd->scd", activated, gathered[3], preferred_element_type=jnp.float32
    )
    combined = branch_attn + branch_mlp
    refreshed_rows = (incoming_rows + router_val[..., None] * combined).astype(jnp.bfloat16)
    back_weights = gathered
    grad_comb = router_val[..., None] * row_gradient
    grad_router_val = jnp.sum(row_gradient * combined, axis=-1)
    total_gradient = row_gradient + grad_router_val[..., None] * back_weights[4].astype(jnp.float32)
    grad_mlp_low = grad_comb.astype(jnp.bfloat16)
    grad_act = jnp.einsum(
        "scd,fd->scf", grad_mlp_low, back_weights[3], preferred_element_type=jnp.float32
    )
    grad_downw = jnp.einsum(
        "scf,scd->fd", activated, grad_mlp_low, preferred_element_type=jnp.float32
    )
    unused, gelu_pull = jax.vjp(jax.nn.gelu, upward)
    grad_up_low = gelu_pull(grad_act)[0].astype(jnp.bfloat16)
    grad_normed_mid = jnp.einsum(
        "scf,df->scd", grad_up_low, back_weights[2], preferred_element_type=jnp.float32
    )
    grad_upw = jnp.einsum(
        "scd,scf->df", normed_mid_low, grad_up_low, preferred_element_type=jnp.float32
    )
    grad_middle, grad_gain_second = rms_back(
        middle, inverse_mid, back_weights[6].astype(jnp.float32), grad_normed_mid
    )
    grad_attn_low = (grad_comb + grad_middle).astype(jnp.bfloat16)
    total_gradient = total_gradient + grad_middle
    grad_attended = jnp.einsum(
        "scd,ed->sce", grad_attn_low, back_weights[1], preferred_element_type=jnp.float32
    ).astype(jnp.bfloat16)
    grad_outw = jnp.einsum(
        "sce,scd->ed", attended, grad_attn_low, preferred_element_type=jnp.float32
    )
    grad_att_heads = grad_attended.reshape(queries.shape)
    grad_probs = jnp.einsum(
        "sqhe,skhe->shqk", grad_att_heads, values_heads, preferred_element_type=jnp.float32
    )
    grad_values = jnp.einsum(
        "shqk,sqhe->skhe", probs_low, grad_att_heads, preferred_element_type=jnp.float32
    )
    grad_scores = probs * (grad_probs - jnp.sum(probs * grad_probs, axis=-1, keepdims=True))
    grad_scores_low = grad_scores.astype(jnp.bfloat16)
    grad_queries = (
        jnp.einsum(
            "shqk,skhe->sqhe", grad_scores_low, keys_heads, preferred_element_type=jnp.float32
        )
        * factor
    )
    grad_keys = (
        jnp.einsum("shqk,sqhe->skhe", grad_scores_low, queries, preferred_element_type=jnp.float32)
        * factor
    )
    flat_shape = incoming_rows.shape
    grad_packed = jnp.concatenate(
        [
            grad_queries.reshape(flat_shape),
            grad_keys.reshape(flat_shape),
            grad_values.reshape(flat_shape),
        ],
        axis=-1,
    ).astype(jnp.bfloat16)
    grad_qkvw = jnp.einsum(
        "scd,sce->de", normed_low, grad_packed, preferred_element_type=jnp.float32
    )
    grad_normed_attn = jnp.einsum(
        "sce,de->scd", grad_packed, back_weights[0], preferred_element_type=jnp.float32
    )
    grad_first_rows, grad_gain_first = rms_back(
        incoming_rows, inverse_attn, back_weights[5].astype(jnp.float32), grad_normed_attn
    )
    total_gradient = total_gradient + grad_first_rows
    grad_routerw = jnp.einsum(
        "scd,sc->d", incoming_rows, grad_router_val, precision=EXACT_PRECISION
    )
    new_rows = jnp.concatenate([refreshed_rows[0], total_gradient[0].astype(jnp.bfloat16)])
    sent_rows = (
        jnp.einsum("cs,cd->sd", pick, new_rows, preferred_element_type=jnp.float32)
        .astype(jnp.bfloat16)
        .reshape(shards, 2 * cap, D)
    )
    small_grads = jnp.stack([grad_routerw, grad_gain_first, grad_gain_second])
    small_grads = small_grads.reshape(3, shards, part).transpose(1, 0, 2)
    small_grads = jnp.pad(small_grads, ((0, 0), (0, 5), (0, 128 - part)))
    partial = [
        g.astype(jnp.bfloat16).reshape(shards, -1, g.shape[1])
        for g in (grad_qkvw, grad_outw, grad_upw, grad_downw)
    ]
    shares = scatter_all(axes, shards, partial + [small_grads], sent_rows, 1)
    totals = tuple(t.astype(jnp.float32) for t in shares[:4]) + tuple(shares[4][j, :part] for j in range(3))
    def place_rows(rows, held):
        spread = jnp.einsum("jip,jid->jpd", select, rows, preferred_element_type=jnp.float32).astype(jnp.bfloat16)
        kept = jnp.where(touched[..., None], spread, held[0])
        return jnp.where(living[..., None], kept, jnp.zeros_like(kept))[None]

    def compact(landed, rows):
        return place_rows(landed[:, :cap], tokens), place_rows(landed[:, cap:], cotangent)

    def entire(landed, rows):
        positions = jnp.arange(SEQ_MAX, dtype=jnp.int32)
        onehot = (routes[:, None] == positions[None, :]).astype(jnp.bfloat16)
        placed = []
        for r, held in ((rows[:CAP], tokens), (rows[CAP:], cotangent)):
            spread = jnp.einsum("cp,cd->pd", onehot, r, preferred_element_type=jnp.float32)
            spread = lax.all_to_all(
                spread.astype(jnp.bfloat16)[None, None], "fsdp", split_axis=2, concat_axis=1, tiled=True
            )
            kept = jnp.where(touched[..., None], spread[0], held[0])
            placed.append(jnp.where(living[..., None], kept, jnp.zeros_like(kept))[None])
        return tuple(placed)

    if cap < width:
        back_out, back_grad = lax.cond(crowded, entire, compact, shares[5], new_rows)
    else:
        back_out, back_grad = compact(shares[5], new_rows)
    return (
        back_out,
        back_grad,
        totals[0],
        totals[1],
        totals[2],
        totals[3],
        totals[4],
        totals[5],
        totals[6],
    )


def solution(mesh):
    placed = (
        P("rep", None, "fsdp", None),
        P("rep", None, "fsdp", None),
        P("fsdp", None),
        P("fsdp", None),
        P("fsdp", None),
        P("fsdp", None),
        P("fsdp"),
        P("fsdp"),
        P("fsdp"),
        P("rep", None),
        P("rep", None, None),
        P("rep", None),
    )
    return jax.shard_map(
        functools.partial(body, grid_axes(mesh)),
        mesh=mesh,
        in_specs=placed,
        out_specs=(
            P("rep", None, "fsdp", None),
            P("rep", None, "fsdp", None),
            P("fsdp", None),
            P("fsdp", None),
            P("fsdp", None),
            P("fsdp", None),
            P("fsdp"),
            P("fsdp"),
            P("fsdp"),
        ),
        check_vma=False,
    )
```

```python
import math
import functools

import jax
import jax.numpy as jnp
from jax import lax
from jax.experimental import pallas as pl
from jax.experimental.pallas import tpu as pltpu
from jax.sharding import PartitionSpec as P

D = 1024
HEADS = 16
HEAD_DIM = 64
SEQ_MAX = 1024
CAP = 128
PAST = 1 << 24


EPSILON = 1e-06
EXACT_PRECISION = lax.Precision.HIGHEST

MESH = pl.DeviceIdType.MESH
ANY = pl.ANY


def grid_axes(mesh):
    devices = mesh.devices[:, 0]
    count = len(devices)
    axes = []
    spots = [getattr(d, "coords", None) for d in devices]
    if all(s is not None for s in spots) and len(set(map(tuple, spots))) == count:
        low = [min(s[k] for s in spots) for k in range(3)]
        at = {tuple(s[k] - low[k] for k in range(3)): f for f, s in enumerate(spots)}
        for k in range(3):
            size = max(s[k] for s in spots) - low[k] + 1
            one = tuple(int(j == k) for j in range(3))
            axes.append((at[one] if size > 1 else 1, size, k))
        ok = all(
            f == sum(stride * spot[k] for stride, _, k in axes) for spot, f in at.items()
        )
        axes = [a[:2] for a in axes] if ok else []
    if not axes:
        axes, left = [], count
        for size in (2, 2):
            size = size if left % size == 0 and left > 1 else 1
            axes.append((count // left, size))
            left //= size
        axes.append((count // left, left))
    return sorted(axes, key=lambda a: -a[1])


def xor(a, b, size):
    out, bit = 0, 1
    while bit < size:
        out = out + ((a // bit + b // bit) % 2) * bit
        bit *= 2
    return out


class Piece:
    def __init__(self, array, half, offset, width):
        self.array, self.half, self.offset, self.width = array, half, offset, width

    def cols(self, core):
        start = self.offset
        if self.half:
            start = core * self.half + start
            start = pl.multiple_of(start, 128)
        return pl.ds(start, self.width)


def colours(axes, widths):
    qkv, out, up, down = (w // 2 for w in widths[:4])
    a, b, c = axes
    third = qkv // 3
    return [
        ((b, c, a), [Piece(1, out, 0, out), Piece(4, 0, 0, widths[4])]),
        ((c, b, a), [Piece(0, qkv, 0, third)]),
        ((a, b, c), [Piece(2, up, 0, up), Piece(0, qkv, third, third)]),
        ((a, c, b), [Piece(3, down, 0, down), Piece(0, qkv, 2 * third, third)]),
    ]


def enter(n, me, core):
    barrier = pltpu.get_barrier_semaphore()

    def hello(i, _):
        pl.semaphore_signal(barrier, inc=1, device_id=((me + i) % n, core), device_id_type=MESH)
        return 0

    lax.fori_loop(1, n, hello, 0)
    pl.semaphore_signal(barrier, inc=1, device_id=(me, 1 - core), device_id_type=MESH)
    pl.semaphore_wait(barrier, n)


def rows_out(n, me, core, rows, landing, send_sem, recv_sem, own_sem):
    own = pltpu.make_async_copy(rows.at[me], landing.at[me], own_sem)
    own.start()

    def go(i, _):
        to = (me + i) % n
        pltpu.make_async_remote_copy(
            src_ref=rows.at[to], dst_ref=landing.at[me], send_sem=send_sem, recv_sem=recv_sem,
            device_id=(to, core), device_id_type=MESH,
        ).start()
        return 0

    lax.fori_loop(1, n, go, 0)
    return own


def rows_wait(n, me, core, rows, landing, send_sem, recv_sem, own):
    own.wait()
    for which in range(2):
        copy = pltpu.make_async_remote_copy(
            src_ref=rows.at[pl.ds(0, n - 1)], dst_ref=landing.at[pl.ds(0, n - 1)],
            send_sem=send_sem, recv_sem=recv_sem, device_id=(me, 1 - core), device_id_type=MESH,
        )
        copy.wait_recv() if which else copy.wait_send()


def gather_kernel(axes, plan, n, *refs):
    k = 5
    ins, rows, flag = refs[:k], refs[k], refs[k + 1]
    outs, landing, other = refs[k + 2 : 2 * k + 2], refs[2 * k + 2], refs[2 * k + 3]
    stages = refs[2 * k + 4 : 3 * k + 4]
    send_sem, recv_sem, pair_send, pair_recv, local_sem, row_sems = refs[3 * k + 4 :]
    me, core = lax.axis_index("fsdp"), lax.axis_index("rep")
    enter(n, me, core)
    told = pltpu.make_async_remote_copy(
        src_ref=flag, dst_ref=other, send_sem=row_sems.at[3], recv_sem=row_sems.at[4],
        device_id=(me, 1 - core), device_id_type=MESH,
    )
    told.start()
    numbered, number = [], 0
    for order, pieces in plan:
        numbered.append((order, [(number + i, p) for i, p in enumerate(pieces)]))
        number += len(pieces)

    def spot(axis):
        return (me // axis[0]) % axis[1]

    def dst(piece, block):
        return outs[piece.array].at[block, :, piece.cols(core)]

    def put(pieces, block, own, phase, way, device, pair=False):
        for i, piece in pieces:
            if pair and not piece.half:
                continue
            src = ins[piece.array].at[:, piece.cols(core)] if own else dst(piece, block)
            pltpu.make_async_remote_copy(
                src_ref=src,
                dst_ref=dst(piece, block),
                send_sem=pair_send.at[i] if pair else send_sem.at[i, phase, way],
                recv_sem=pair_recv.at[i] if pair else recv_sem.at[i, block],
                device_id=device,
                device_id_type=MESH,
            ).start()

    def along(pieces, order, block, own, phase, ways):
        stride, size = order[phase]
        at = spot(order[phase])
        if size == 1:
            return
        if size == 2:
            put(pieces, block, own, phase, 0, (me + (1 - 2 * at) * stride, core))
            return
        for way in ways:
            step = 1 - 2 * way
            pl.when(at < size - 1 if way == 0 else at > 0)(
                functools.partial(put, pieces, block, own, phase, way, (me + step * stride, core))
            )

    def arrived(pieces, order, block, phase, way):
        for i, piece in pieces:
            pltpu.make_async_remote_copy(
                src_ref=dst(piece, block),
                dst_ref=dst(piece, block),
                send_sem=send_sem.at[i, phase, way],
                recv_sem=recv_sem.at[i, block],
                device_id=(me, 1 - core),
                device_id_type=MESH,
            ).wait_recv()
        if order[phase][1] > 2:
            along(pieces, order, block, False, phase, (way,))
        for later in range(phase + 1, 3):
            along(pieces, order, block, False, later, (0, 1))
        put(pieces, block, False, 0, 0, (me, 1 - core), pair=True)

    for order, pieces in numbered:
        for phase in range(3):
            along(pieces, order, me, True, phase, (0, 1))
    own = rows_out(n, me, core, rows, landing, row_sems.at[0], row_sems.at[1], row_sems.at[2])
    local = []
    for j in range(k):
        local.append(pltpu.make_async_copy(ins[j], stages[j], local_sem.at[j]))
        local[-1].start()
    events = []
    for number, (order, pieces) in enumerate(numbered):
        heavy = number >= 2
        sizes = [a[1] for a in order]
        for phase in range(3):
            size = sizes[phase]
            rest = 1
            for s in sizes[:phase]:
                rest *= s
            for t in range(1, size):
                ways = (0,) if size == 2 else (0, 1)
                for way in ways:
                    for j in range(rest):
                        if heavy:
                            key = 20 * t if phase == 0 else 20 * phase + 20 * (j + (t - 1) * rest + 1)
                        else:
                            key = 5 if phase == 0 else 10 + 5 * j if phase == 1 else 15 + 40 * t + 5 * j
                        events.append((key, len(events), order, pieces, phase, t, way, j))
    events.sort(key=lambda e: e[:2])

    def run(order, pieces, phase, t, way, j):
        stride, size = order[phase]
        at = spot(order[phase])
        origin = 1 - at if size == 2 else at - (1 - 2 * way) * t
        block = me + (origin - at) * stride
        for s, z in order[:phase]:
            here = (me // s) % z
            block = block + (xor(here, j % z, z) - here) * s
            j = j // z
        if size == 2:
            arrived(pieces, order, block, phase, 0)
        else:
            pl.when((origin >= 0) & (origin < size))(
                functools.partial(arrived, pieces, order, block, phase, way)
            )

    def settle():
        for j in range(k):
            local[j].wait()
            local[j] = pltpu.make_async_copy(stages[j], outs[j].at[me], local_sem.at[j])
            local[j].start()

    for number, (_, _, order, pieces, phase, t, way, j) in enumerate(events):
        run(order, pieces, phase, t, way, j)
        if number == 3:
            settle()
    for copy in local:
        copy.wait()
    told.wait()
    rows_wait(n, me, core, rows, landing, row_sems.at[0], row_sems.at[1], own)

    def drain(i, piece, count, send, recv, which):
        many = outs[piece.array].at[pl.ds(0, count), :, piece.cols(core)]
        copy = pltpu.make_async_remote_copy(
            src_ref=many, dst_ref=many, send_sem=send, recv_sem=recv,
            device_id=(me, 1 - core), device_id_type=MESH,
        )
        if which == "send":
            copy.wait_send()
        else:
            copy.wait_recv()

    for order, pieces in numbered:
        rest = 1
        for phase in range(3):
            stride, size = order[phase]
            at = spot(order[phase])
            for i, piece in pieces:
                if size == 2:
                    drain(i, piece, rest, send_sem.at[i, phase, 0], recv_sem.at[i, 0], "send")
                elif size > 2:
                    for here in range(size):
                        def both(here=here, i=i, piece=piece, phase=phase, rest=rest, size=size):
                            if here < size - 1:
                                drain(i, piece, (here + 1) * rest, send_sem.at[i, phase, 0], recv_sem.at[i, 0], "send")
                            if here > 0:
                                drain(i, piece, (size - here) * rest, send_sem.at[i, phase, 1], recv_sem.at[i, 0], "send")
                        pl.when(at == here)(both)
            rest *= size
        for i, piece in pieces:
            if piece.half:
                drain(i, piece, n - 1, pair_send.at[i], pair_recv.at[i], "send")
                drain(i, piece, n - 1, pair_send.at[i], pair_recv.at[i], "recv")


def gather_all(axes, n, arrays, rows, flag, collective_id):
    plan = colours(axes, [a.shape[1] for a in arrays])
    pieces = sum(len(p) for _, p in plan)
    vmem = pl.BlockSpec(memory_space=pltpu.VMEM)
    anywhere = pl.BlockSpec(memory_space=ANY)
    dma = pltpu.SemaphoreType.DMA
    return pl.pallas_call(
        functools.partial(gather_kernel, axes, plan, n),
        out_shape=[jax.ShapeDtypeStruct((n,) + a.shape, a.dtype) for a in arrays]
        + [jax.ShapeDtypeStruct(a.shape, a.dtype) for a in (rows, flag)],
        in_specs=[anywhere] * len(arrays) + [vmem, vmem],
        out_specs=[anywhere] * (len(arrays) + 1) + [vmem],
        scratch_shapes=[pltpu.VMEM(a.shape, a.dtype) for a in arrays]
        + [dma((pieces, 3, 2)), dma((pieces, n)), dma((pieces,)), dma((pieces,)), dma((len(arrays),)), dma((5,))],
        compiler_params=pltpu.CompilerParams(collective_id=collective_id, has_side_effects=True),
        name="gather_all",
    )(*arrays, rows, flag)
def add_into(acc, a, got, g, rows):
    step = min(rows, 16)

    def go(i, _):
        at = pl.ds(pl.multiple_of(i * step, step), step)
        acc[a, at, :] = (acc[a, at, :].astype(jnp.float32) + got[g, at, :].astype(jnp.float32)).astype(acc.dtype)
        return 0

    lax.fori_loop(0, rows // step, go, 0)


def turn(at, t, size):
    if size == 2:
        return at + (1 - 2 * at) * (1 - t)
    up = size - 1 - at
    first_up = jnp.where(t < up, size - 1 - t, t - up)
    first_down = jnp.where(t < at, t, size - 1 - (t - at))
    return jnp.where(t == size - 1, at, jnp.where(2 * at < size, first_up, first_down))


def slots(size):
    return 1 if size <= 2 else size + 1


def scatter_kernel(axes, plan, n, *refs):
    k = 5
    ins, rows, outs, landing = refs[:k], refs[k], refs[k + 1 : 2 * k + 1], refs[2 * k + 1]
    total = sum(len(p) for _, p in plan)
    buffers = refs[2 * k + 2 : 2 * k + 2 + 5 * total]
    own_sem, pair_send, pair_recv, send_sem = refs[-10:-6]
    recv_sems, last_send, last_recv, row_sems = refs[-6:-3], refs[-3], refs[-2], refs[-1]
    me, core = lax.axis_index("fsdp"), lax.axis_index("rep")
    enter(n, me, core)
    numbered, number = [], 0
    for order, pieces in plan:
        numbered.append((order, [(number + i, p) for i, p in enumerate(pieces)]))
        number += len(pieces)
    acc = [buffers[5 * i] for i in range(total)]
    pair = [buffers[5 * i + 1] for i in range(total)]
    got = [buffers[5 * i + 2 : 5 * i + 5] for i in range(total)]

    def spot(axis):
        return (me // axis[0]) % axis[1]

    def pair_copy(i, piece, block):
        return pltpu.make_async_remote_copy(
            src_ref=ins[piece.array].at[block, :, piece.cols(1 - core)],
            dst_ref=pair[i].at[block],
            send_sem=pair_send.at[i],
            recv_sem=pair_recv.at[i, block],
            device_id=(me, 1 - core),
            device_id_type=MESH,
        )

    def own_copy(i, piece, block):
        return pltpu.make_async_copy(
            ins[piece.array].at[block, :, piece.cols(core)], acc[i].at[block], own_sem.at[i, block]
        )

    def block_at(order, phase, origin, turns):
        block = me + (origin - spot(order[phase])) * order[phase][0]
        for axis, t in zip(order[:phase], turns):
            block = block + (turn(spot(axis), t, axis[1]) - spot(axis)) * axis[0]
        return block

    def ready(pieces, block):
        for i, piece in pieces:
            own_copy(i, piece, block).wait()
            pair_copy(i, piece, block).wait_recv()
            add_into(acc[i], block, pair[i], block, acc[i].shape[1])

    def hop(i, phase, block, rest, slot, send, device):
        return pltpu.make_async_remote_copy(
            src_ref=acc[i].at[block],
            dst_ref=got[i][phase].at[rest, slot],
            send_sem=send,
            recv_sem=recv_sems[phase].at[i, rest * got[i][phase].shape[1] + slot],
            device_id=device,
            device_id_type=MESH,
        )

    def take(pieces, phase, block, rest, slot):
        for i, piece in pieces:
            hop(i, phase, block, rest, slot, send_sem.at[i, phase], (me, 1 - core)).wait_recv()
            add_into(acc[i], block, got[i][phase].at[rest], slot, acc[i].shape[1])

    def give(pieces, phase, block, rest, slot, device):
        for i, piece in pieces:
            hop(i, phase, block, rest, slot, send_sem.at[i, phase], device).start()

    def event(order, pieces, phase, t, turns, first):
        stride, size = order[phase]
        at = spot(order[phase])
        origin = turn(at, t, size)
        mine = t == size - 1
        block = block_at(order, phase, origin, turns)
        rest = 0
        for axis, away in zip(order[:phase], turns):
            rest = rest * axis[1] + away
        if first:
            ready(pieces, block)
        if size == 1:
            return
        if size == 2:
            pl.when(jnp.logical_not(mine))(
                lambda: give(pieces, phase, block, rest, 0, (me + (1 - 2 * at) * stride, core))
            )
            pl.when(mine)(lambda: take(pieces, phase, block, rest, 0))
            return

        @pl.when(jnp.logical_not(mine))
        def _():
            up = (origin > at).astype(jnp.int32)
            behind = jnp.where(up == 1, at > 0, at < size - 1)
            pl.when(behind)(lambda: take(pieces, phase, block, rest, origin))
            step = 2 * up - 1
            landing = jnp.where((up == 0) & (origin == at - 1), size, origin)
            give(pieces, phase, block, rest, landing, (me + step * stride, core))

        @pl.when(mine)
        def _():
            pl.when(at > 0)(lambda: take(pieces, phase, block, rest, at))
            pl.when(at < size - 1)(lambda: take(pieces, phase, block, rest, size))

    def each(count, fn):
        lax.fori_loop(0, count, lambda e, _: (fn(e), 0)[1], 0)

    def begin(order, pieces, s):
        _, (_, nq), (_, nr) = order

        def go(e):
            block = block_at(order, 2, turn(spot(order[2]), e // nq, nr), (s, e % nq))
            for i, piece in pieces:
                pair_copy(i, piece, block).start()
                own_copy(i, piece, block).start()

        each(nr * nq, go)

    def lead(order, pieces, s):
        _, (_, nq), (_, nr) = order
        each((nr - 1) * nq, lambda e: event(order, pieces, 2, e // nq, (s, e % nq), True))

    def later(order, pieces, s, low, high):
        def go(e):
            event(order, pieces, 2, order[2][1] - 1, (s, low + e), True)
            event(order, pieces, 1, low + e, (s,), False)

        each(high - low, go)

    def finish(order, pieces, s):
        event(order, pieces, 0, s, (), False)

    light, heavy = numbered[:2], numbered[2:]
    steps, few = heavy[0][0][0][1], max(c[0][0][1] for c in light)

    def begin_all(s):
        for colour in heavy:
            pl.when(s < steps)(lambda colour=colour: begin(*colour, s))
        for colour in light:
            pl.when(s < colour[0][0][1])(lambda colour=colour: begin(*colour, s))

    each(max(steps, few), begin_all)
    own = rows_out(n, me, core, rows, landing, row_sems.at[0], row_sems.at[1], row_sems.at[2])
    for colour in heavy + light:
        lead(*colour, 0)

    def step(s):
        for colour in heavy:
            pl.when(s < steps)(lambda colour=colour: later(*colour, s, 0, 1))
        for colour in heavy:
            pl.when(s + 1 < steps)(lambda colour=colour: lead(*colour, s + 1))
        for colour in heavy:
            pl.when((s >= 1) & (s < steps))(lambda colour=colour: finish(*colour, s - 1))
        for colour in light:
            size = colour[0][0][1]
            pl.when(s + 1 < size)(lambda colour=colour: lead(*colour, s + 1))
        for colour in heavy:
            pl.when(s < steps)(lambda colour=colour: later(*colour, s, 1, colour[0][1][1]))
        for colour in light:
            size = colour[0][0][1]

            @pl.when((s >= 1) & (s <= size))
            def _(colour=colour):
                later(*colour, s - 1, 0, colour[0][1][1])
                finish(*colour, s - 1)
        for colour in heavy:
            pl.when(s == steps - 1)(lambda colour=colour: finish(*colour, s))

    each(max(steps, few + 1), step)

    final = []
    for order, pieces in numbered:
        for i, piece in pieces:
            outs[piece.array][:, piece.cols(core)] = acc[i][me]
            if piece.half:
                final.append(
                    pltpu.make_async_remote_copy(
                        src_ref=acc[i].at[me],
                        dst_ref=outs[piece.array].at[:, piece.cols(core)],
                        send_sem=last_send.at[i],
                        recv_sem=last_recv.at[i],
                        device_id=(me, 1 - core),
                        device_id_type=MESH,
                    )
                )
                final[-1].start()
    for copy in final:
        copy.wait()
    rows_wait(n, me, core, rows, landing, row_sems.at[0], row_sems.at[1], own)

    def drain(i, phase, count):
        many = acc[i].at[pl.ds(0, count)]
        pltpu.make_async_remote_copy(
            src_ref=many, dst_ref=many, send_sem=send_sem.at[i, phase], recv_sem=last_recv.at[i],
            device_id=(me, 1 - core), device_id_type=MESH,
        ).wait_send()

    for order, pieces in numbered:
        for i, piece in pieces:
            for phase in range(3):
                if order[phase][1] > 1:
                    count = order[phase][1] - 1
                    for axis in order[:phase]:
                        count *= axis[1]
                    drain(i, phase, count)
            many = acc[i].at[pl.ds(0, n)]
            pltpu.make_async_remote_copy(
                src_ref=many, dst_ref=many, send_sem=pair_send.at[i], recv_sem=last_recv.at[i],
                device_id=(me, 1 - core), device_id_type=MESH,
            ).wait_send()


def scatter_all(axes, n, arrays, rows, collective_id):
    plan = colours(axes, [a.shape[2] for a in arrays])
    pieces = [(order, p) for order, ps in plan for p in ps]
    scratch = []
    for order, p in pieces:
        deep, dtype = arrays[p.array].shape[1], arrays[p.array].dtype
        scratch += [pltpu.VMEM((n, deep, p.width), dtype)] * 2
        count = 1
        for phase in range(3):
            size = order[phase][1]
            scratch.append(pltpu.VMEM((count, slots(size), deep, p.width), dtype))
            count *= size
    total = len(pieces)
    shapes = []
    for phase in range(3):
        most = 1
        for order, _ in plan:
            count = slots(order[phase][1])
            for a in order[:phase]:
                count *= a[1]
            most = max(most, count)
        shapes.append((total, most))
    dma = pltpu.SemaphoreType.DMA
    return pl.pallas_call(
        functools.partial(scatter_kernel, axes, plan, n),
        out_shape=[jax.ShapeDtypeStruct(a.shape[1:], a.dtype) for a in arrays]
        + [jax.ShapeDtypeStruct(rows.shape, rows.dtype)],
        in_specs=[pl.BlockSpec(memory_space=ANY)] * len(arrays) + [pl.BlockSpec(memory_space=pltpu.VMEM)],
        out_specs=[pl.BlockSpec(memory_space=pltpu.VMEM)] * len(arrays) + [pl.BlockSpec(memory_space=ANY)],
        scratch_shapes=scratch
        + [dma((total, n)), dma((total,)), dma((total, n)), dma((total, 3))]
        + [dma(s) for s in shapes]
        + [dma((total,)), dma((total,)), dma((3,))],
        compiler_params=pltpu.CompilerParams(
            collective_id=collective_id, has_side_effects=True, vmem_limit_bytes=60 * 1024 * 1024
        ),
        name="scatter_all",
    )(*arrays, rows)


SQRT_2_PI = math.sqrt(2.0 / math.pi)
NN = (((1,), (0,)), ((), ()))
NT = (((1,), (1,)), ((), ()))
TN = (((0,), (0,)), ((), ()))


def mm(a, b, dims=NN):
    return lax.dot_general(a, b, dims, preferred_element_type=jnp.float32)


def each(count, fn):
    lax.fori_loop(0, count, lambda e, _: (fn(e), 0)[1], 0)


class Part:
    def __init__(self, array, offset, width):
        self.array, self.offset, self.width = array, offset, width

    def of(self, ref, block):
        return ref.at[block, :, pl.ds(self.offset, self.width)]


EARLY, AT0, AT1, CUT, SPLIT = 60, 4, 85, 70, False


def first_shares(axes, vectors):
    a, b, c = axes
    half = D // 2
    return [
        ((b, c, a), [Part(1, 0, D // 8), Part(4, 0, vectors)]),
        ((c, b, a), [Part(0, 0, D // 8)]),
        ((a, b, c), [Part(0, D // 8, half + 3 * D // 8)]),
        ((a, c, b), [Part(0, D, half), Part(1, D // 8, 3 * D // 8)]),
    ]


def second_shares(axes):
    a, b, c = axes
    return [
        ((b, c, a), [Part(2, 0, 3 * D // 8)]),
        ((c, b, a), [Part(3, 0, D // 4)]),
        ((a, b, c), [Part(2, 3 * D // 8, 13 * D // 8)]),
        ((a, c, b), [Part(3, D // 4, 3 * D // 4)]),
    ]


def number_parts(plan):
    numbered, number = [], 0
    for order, parts in plan:
        numbered.append((order, [(number + i, p) for i, p in enumerate(parts)]))
        number += len(parts)
    return numbered


def send(src, dst, send_sem, recv_sem, device):
    return pltpu.make_async_remote_copy(
        src_ref=src, dst_ref=dst, send_sem=send_sem, recv_sem=recv_sem, device_id=device, device_id_type=MESH
    )


class Gather:
    def __init__(self, n, me, core, numbered, whole, sems):
        self.n, self.me, self.core, self.numbered, self.whole = n, me, core, numbered, whole
        self.send_sem, self.recv_sem = sems

    def spot(self, axis):
        return (self.me // axis[0]) % axis[1]

    def put(self, parts, block, phase, way, step):
        for i, part in parts:
            dst = part.of(self.whole[part.array], block)
            send(
                dst, dst, self.send_sem.at[i, phase, way], self.recv_sem.at[i, block], (self.me + step, self.core)
            ).start()

    def along(self, parts, order, block, phase, ways):
        stride, size = order[phase]
        at = self.spot(order[phase])
        if size == 2:
            self.put(parts, block, phase, 0, (1 - 2 * at) * stride)
        elif size > 2:
            for way in ways:
                step = (1 - 2 * way) * stride
                pl.when(at < size - 1 if way == 0 else at > 0)(
                    functools.partial(self.put, parts, block, phase, way, step)
                )

    def arrived(self, parts, order, block, phase, way):
        for i, part in parts:
            dst = part.of(self.whole[part.array], block)
            send(
                dst, dst, self.send_sem.at[i, phase, way], self.recv_sem.at[i, block], (self.me, 1 - self.core)
            ).wait_recv()
        if order[phase][1] > 2:
            self.along(parts, order, block, phase, (way,))
        for later in range(phase + 1, 3):
            self.along(parts, order, block, later, (0, 1))

    def start(self):
        for order, parts in self.numbered:
            for phase in range(3):
                self.along(parts, order, self.me, phase, (0, 1))

    def events(self):
        found = []
        for number, (order, parts) in enumerate(self.numbered):
            heavy = number >= 2
            sizes = [a[1] for a in order]
            for phase in range(3):
                size, rest = sizes[phase], math.prod(sizes[:phase])
                for t in range(1, size):
                    for way in (0,) if size == 2 else (0, 1):
                        for j in range(rest):
                            if heavy:
                                key = 20 * t if phase == 0 else 20 * phase + 20 * (j + (t - 1) * rest + 1)
                            else:
                                key = 5 if phase == 0 else 10 + 5 * j if phase == 1 else 15 + 40 * t + 5 * j
                            found.append((key, len(found), order, parts, phase, t, way, j))
        found.sort(key=lambda e: e[:2])
        return [functools.partial(self.run, *e[2:]) for e in found]

    def run(self, order, parts, phase, t, way, j):
        stride, size = order[phase]
        at = self.spot(order[phase])
        origin = 1 - at if size == 2 else at - (1 - 2 * way) * t
        block = self.me + (origin - at) * stride
        for s, z in order[:phase]:
            here = (self.me // s) % z
            block = block + (xor(here, j % z, z) - here) * s
            j = j // z
        if size == 2:
            self.arrived(parts, order, block, phase, 0)
        else:
            pl.when((origin >= 0) & (origin < size))(
                functools.partial(self.arrived, parts, order, block, phase, way)
            )

    def drain(self):
        for order, parts in self.numbered:
            rest = 1
            for phase in range(3):
                size = order[phase][1]
                at = self.spot(order[phase])
                for i, part in parts:
                    def gone(count, way, i=i, part=part, phase=phase):
                        many = part.of(self.whole[part.array], pl.ds(0, count))
                        send(
                            many, many, self.send_sem.at[i, phase, way], self.recv_sem.at[i, 0], (self.me, 1 - self.core)
                        ).wait_send()

                    if size == 2:
                        gone(rest, 0)
                    elif size > 2:
                        for here in range(size):
                            def both(here=here, gone=gone, rest=rest, size=size):
                                if here < size - 1:
                                    gone((here + 1) * rest, 0)
                                if here > 0:
                                    gone((size - here) * rest, 1)
                            pl.when(at == here)(both)
                rest *= size


class Scatter:
    def __init__(self, me, core, numbered, acc, got, sems):
        self.me, self.core, self.numbered, self.acc, self.got = me, core, numbered, acc, got
        self.send_sem, self.recv_sems, self.drain_sem = sems

    def spot(self, axis):
        return (self.me // axis[0]) % axis[1]

    def block_at(self, order, phase, origin, turns):
        block = self.me + (origin - self.spot(order[phase])) * order[phase][0]
        for axis, t in zip(order[:phase], turns):
            block = block + (turn(self.spot(axis), t, axis[1]) - self.spot(axis)) * axis[0]
        return block

    def hop(self, i, part, phase, block, rest, slot, device):
        return send(
            part.of(self.acc[part.array], block),
            self.got[i][phase].at[rest, slot],
            self.send_sem.at[i, phase],
            self.recv_sems[phase].at[i, rest * self.got[i][phase].shape[1] + slot],
            device,
        )

    def take(self, parts, phase, block, rest, slot):
        for i, part in parts:
            self.hop(i, part, phase, block, rest, slot, (self.me, 1 - self.core)).wait_recv()
            acc, got = self.acc[part.array], self.got[i][phase]
            rows = acc.shape[1]
            step = min(rows, 16)
            cols = pl.ds(part.offset, part.width)

            def go(e, acc=acc, got=got, step=step, cols=cols):
                at = pl.ds(pl.multiple_of(e * step, step), step)
                acc[block, at, cols] = acc[block, at, cols] + got[rest, slot, at, :]

            each(rows // step, go)

    def give(self, parts, phase, block, rest, slot, step):
        for i, part in parts:
            self.hop(i, part, phase, block, rest, slot, (self.me + step, self.core)).start()

    def event(self, order, parts, phase, t, turns):
        stride, size = order[phase]
        at = self.spot(order[phase])
        origin = turn(at, t, size)
        mine = t == size - 1
        block = self.block_at(order, phase, origin, turns)
        rest = 0
        for axis, away in zip(order[:phase], turns):
            rest = rest * axis[1] + away
        if size == 1:
            return
        if size == 2:
            pl.when(jnp.logical_not(mine))(
                lambda: self.give(parts, phase, block, rest, 0, (1 - 2 * at) * stride)
            )
            pl.when(mine)(lambda: self.take(parts, phase, block, rest, 0))
            return

        @pl.when(jnp.logical_not(mine))
        def _():
            up = (origin > at).astype(jnp.int32)
            behind = jnp.where(up == 1, at > 0, at < size - 1)
            pl.when(behind)(lambda: self.take(parts, phase, block, rest, origin))
            landing = jnp.where((up == 0) & (origin == at - 1), size, origin)
            self.give(parts, phase, block, rest, landing, (2 * up - 1) * stride)

        @pl.when(mine)
        def _():
            pl.when(at > 0)(lambda: self.take(parts, phase, block, rest, at))
            pl.when(at < size - 1)(lambda: self.take(parts, phase, block, rest, size))

    def lead(self, order, parts, s):
        _, (_, nq), (_, nr) = order
        each((nr - 1) * nq, lambda e: self.event(order, parts, 2, e // nq, (s, e % nq)))

    def later(self, order, parts, s, low, high):
        def go(e):
            self.event(order, parts, 2, order[2][1] - 1, (s, low + e))
            self.event(order, parts, 1, low + e, (s,))

        each(high - low, go)

    def finish(self, order, parts, s):
        self.event(order, parts, 0, s, ())

    def stages(self):
        light, heavy = self.numbered[:2], self.numbered[2:]
        steps, few = heavy[0][0][0][1], max(c[0][0][1] for c in light)
        found = [functools.partial(self.lead, *colour, 0) for colour in heavy + light]
        for s in range(max(steps, few + 1)):
            if s < steps:
                found += [functools.partial(self.later, *colour, s, 0, 1) for colour in heavy]
            if s + 1 < steps:
                found += [functools.partial(self.lead, *colour, s + 1) for colour in heavy]
            if 1 <= s < steps:
                found += [functools.partial(self.finish, *colour, s - 1) for colour in heavy]
            found += [functools.partial(self.lead, *c, s + 1) for c in light if s + 1 < c[0][0][1]]
            if s < steps:
                found += [functools.partial(self.later, *c, s, 1, c[0][1][1]) for c in heavy]
            for c in light:
                if 1 <= s <= c[0][0][1]:
                    found += [
                        functools.partial(self.later, *c, s - 1, e, e + 1) for e in range(c[0][1][1])
                    ]
                    found.append(functools.partial(self.finish, *c, s - 1))
            if s == steps - 1:
                found += [functools.partial(self.finish, *colour, s) for colour in heavy]
        return found

    def drain(self):
        for order, parts in self.numbered:
            for i, part in parts:
                for phase in range(3):
                    if order[phase][1] > 1:
                        count = (order[phase][1] - 1) * math.prod([a[1] for a in order[:phase]])
                        many = part.of(self.acc[part.array], pl.ds(0, count))
                        send(
                            many, many, self.send_sem.at[i, phase], self.drain_sem, (self.me, 1 - self.core)
                        ).wait_send()


class Refs:
    pass


def block_kernel(axes, n, cap, *refs):
    names = (
        "wq", "wo", "wu", "wd", "vec", "rows_in", "pick", "extra", "notes", "gq", "go", "gu", "gd", "gs",
        "landed", "new", "Wq", "Wo", "Wu", "Wd", "V", "Wo2", "Aq", "Ao", "Au", "Ad", "As", "As2", "land",
        "rows_out", "X", "DY", "N1", "QKV", "PROBS", "ATT", "PART", "SENT", "GOT1", "GOT2", "GOT3", "GOT4",
        "BA", "N2", "ACT", "GM", "GU", "M1", "GA", "GATT", "GQKV", "GR", "NOTE", "FQ", "FO", "FU", "FD",
    )
    r = Refs()
    for name, ref in zip(names, refs):
        setattr(r, name, ref)
    got_refs, sems = refs[len(names) : -8], refs[-8:]
    g_send, g_recv, g_local, s_send, s_recv0, s_recv1, s_recv2, misc = sems
    R = D // n
    me, core = lax.axis_index("fsdp"), lax.axis_index("rep")
    half = D // 2
    pair = (me, 1 - core)
    units = r.wd.shape[0] // 2
    blocks = [r.Wq, r.Wo, r.Wu, r.Wd, r.V]

    def stage(src, dst, k):
        pltpu.make_async_copy(src, dst, g_local.at[k]).start()

    def column(f, size, start):
        return pl.ds(pl.multiple_of(f * size + start, 128), size)

    for k in range(3):
        stage(r.wq.at[:, pl.ds(pl.multiple_of(k * D + core * half, 128), half)], r.Wq.at[me, :, pl.ds(k * half, half)], 0)
    stage(r.wo.at[:, column(core, half, 0)], r.Wo.at[me], 1)
    each(
        n, lambda f: stage(r.wu.at[:, column(2 * f + core, units, 0)], r.Wu.at[me, :, column(f, units, 0)], 2)
    )
    stage(r.wd.at[pl.ds(pl.multiple_of(core * units, 16), units)], r.Wd.at[me], 3)
    stage(r.vec, r.V.at[me], 4)
    enter(n, me, core)
    for k, whole in enumerate(blocks):
        pltpu.make_async_copy(whole.at[me], whole.at[me], g_local.at[k]).wait()
    counter = [0]

    def to_pair(src, dst):
        k = counter[0]
        counter[0] += 2
        copy = send(src, dst, misc.at[k], misc.at[k + 1], pair)
        copy.start()
        return copy

    numbered = number_parts(first_shares(axes, 128) + second_shares(axes))
    g_sems = (g_send, g_recv)
    gathers = [Gather(n, me, core, part, blocks, g_sems) for part in (numbered[:4], numbered[4:])]
    gathers[0].start()
    row_sems = [misc.at[40 + k] for k in range(6)]
    own_rows = rows_out(n, me, core, r.rows_in, r.land, *row_sems[:3])
    note = to_pair(r.notes, r.NOTE)
    events = gathers[0].events()
    early = len(events) * EARLY // 100
    for event in events[:early]:
        event()
    gathers[1].start()
    for event in events[early:]:
        event()
    mine, theirs = pl.ds(0, CAP), pl.ds(CAP, CAP)
    STEP = 64
    TILE = 256
    flying = Refs()

    def cols(e, size=TILE):
        return pl.ds(pl.multiple_of(e * size, size), size)

    def flat(ref, at):
        return ref[:, :, at].reshape(-1, at.size)

    def vector(v):
        per = 128 // R
        tiles = []
        for t in range(D // 128):
            total = r.V[t * per].astype(jnp.float32)[v : v + 1, :]
            for j in range(1, per):
                total = total + r.V[t * per + j].astype(jnp.float32)[v : v + 1, :]
            tiles.append(total)
        return jnp.concatenate(tiles, axis=1)

    w_router, gain1, gain2 = vector(0), vector(1), vector(2)

    def inverse(v):
        return lax.rsqrt(jnp.mean(v * v, axis=1, keepdims=True) + EPSILON)

    def rows_here():
        rows_wait(n, me, core, r.rows_in, r.land, row_sems[0], row_sems[1], own_rows)
        flying.out_half = to_pair(r.Wo.at[pl.ds((1 - core) * (n // 2), n // 2)], r.Wo2)

    def extract(k, ref):
        def go(e):
            at = pl.ds(k * CAP, CAP)
            ref[:CAP, cols(e)] = (
                mm(r.pick[at, :], r.land[:, :, cols(e)].reshape(-1, TILE)) + r.extra[at, cols(e)].astype(jnp.float32)
            ).astype(jnp.bfloat16)

        each(D // TILE, go)

    def swap_rows():
        flying.both = [to_pair(ref.at[mine], ref.at[theirs]) for ref in (r.X, r.DY)] + [note]

    def first(e):
        at = pl.ds(pl.multiple_of(e * STEP, STEP), STEP)
        x = r.X[at, :].astype(jnp.float32)
        r.N1[at, :] = (x * inverse(x) * gain1).astype(jnp.bfloat16)
        router = jnp.sum(x * w_router, axis=1, keepdims=True)
        r.GM[at, :] = (router * r.DY[at, :].astype(jnp.float32)).astype(jnp.bfloat16)

    def first_rows():
        for copy in flying.both:
            copy.wait()
        each(2 * CAP // STEP, first)

    def project(e):
        r.QKV[:, cols(e)] = mm(r.N1[...], flat(r.Wq, cols(e))).astype(jnp.bfloat16)

    factor = 1.0 / math.sqrt(HEAD_DIM)
    pairs = half // 128
    lane = lax.broadcasted_iota(jnp.int32, (CAP, 128), 1) // HEAD_DIM
    zero = jnp.zeros((CAP, 128), jnp.bfloat16)
    causal = lax.broadcasted_iota(jnp.int32, (CAP, CAP), 1) <= lax.broadcasted_iota(jnp.int32, (CAP, CAP), 0)

    def heads(e):
        s, p = e // pairs, e % pairs
        rows = pl.ds(pl.multiple_of(s * CAP, CAP), CAP)
        q, k, v = (r.QKV[rows, cols(p + j * pairs, 128)] for j in range(3))
        return s, p, rows, q, k, v

    def attend(e):
        s, p, rows, q, k, v = heads(e)
        valid = jnp.where(s == 0, r.notes[0:1, :], r.NOTE[0:1, :]) > 0
        parts = []
        for h in range(2):
            score = mm(jnp.where(lane == h, q, zero), k, NT) * factor
            score = jnp.where(causal & valid, score, -1e30)
            top = jnp.exp(score - jnp.max(score, axis=1, keepdims=True))
            probs = top / jnp.sum(top, axis=1, keepdims=True)
            r.PROBS[2 * e + h] = probs
            parts.append(mm(probs.astype(jnp.bfloat16), v))
        r.ATT[rows, cols(p, 128)] = jnp.where(lane == 0, parts[0], parts[1]).astype(jnp.bfloat16)

    near = pl.ds(pl.multiple_of(core * half, half), half)
    away = pl.ds(pl.multiple_of((1 - core) * half, half), half)
    own_heads = pl.ds(core * (n // 2), n // 2)

    def wo_near():
        return r.Wo[own_heads].reshape(half, half)

    def wo_away():
        return r.Wo2[...].reshape(half, half)

    def project_out(where):
        if where == 0:
            r.BA[:, near] = mm(r.ATT[...], wo_near())
        else:
            flying.out_half.wait()
            r.BA[:, away] = mm(r.ATT[...], wo_away())

    def pass_on(part, got):
        for a, b in ((mine, theirs), (theirs, mine)):
            r.SENT[a, :] = part[b, :].astype(jnp.bfloat16)
        flying.gone = to_pair(r.SENT, got)

    def second(e):
        at = pl.ds(pl.multiple_of(e * STEP, STEP), STEP)
        branch = r.BA[at, :] + r.GOT1[at, :].astype(jnp.float32)
        r.BA[at, :] = branch
        middle = r.X[at, :].astype(jnp.float32) + branch
        r.N2[at, :] = (middle * inverse(middle) * gain2).astype(jnp.bfloat16)

    def second_rows():
        flying.gone.wait()
        each(2 * CAP // STEP, second)

    def some(fn, low, high):
        return lambda: lax.fori_loop(low, high, lambda e, _: (fn(e), 0)[1], 0)

    def spread(items, chunks, low, high):
        done = 0
        for number, item in enumerate(items):
            item()
            want = len(chunks) * (number + 1 - low) // max(high - low, 1)
            while done < min(max(want, 0), len(chunks)):
                chunks[done]()
                done += 1
        for chunk in chunks[done:]:
            chunk()

    forward = [rows_here, functools.partial(extract, 0, r.X), functools.partial(extract, 1, r.DY), swap_rows, first_rows]
    forward += [some(project, e, e + 1) for e in range(3 * half // TILE)]
    forward += [some(attend, e, e + 2) for e in range(0, 2 * pairs, 2)]
    forward += [
        functools.partial(project_out, 0), functools.partial(project_out, 1),
        lambda: pass_on(r.BA, r.GOT1), second_rows,
    ]
    events = gathers[1].events()
    spread(events, forward, len(events) * AT0 // 100, len(events) * AT1 // 100)
    hidden = r.Wd.shape[1]
    per = TILE // hidden if hidden < TILE else 1

    def down_rows(e):
        return pl.ds(e * per, per)

    def hidden_units(e):
        up = mm(r.N2[...], flat(r.Wu, cols(e)))
        inner = jnp.tanh(SQRT_2_PI * (up + 0.044715 * up * up * up))
        act = (0.5 * up * (1.0 + inner)).astype(jnp.bfloat16)
        slope = 0.5 * (1.0 + inner) + 0.5 * up * (1.0 - inner * inner) * (
            SQRT_2_PI * (1.0 + 3 * 0.044715 * up * up)
        )
        r.ACT[:, cols(e)] = act
        down = r.Wd[down_rows(e)].reshape(TILE, D)
        grad_act = mm(r.GM[...], down, NT)
        r.GU[:, cols(e)] = (slope * grad_act).astype(jnp.bfloat16)
        r.Ad[down_rows(e)] = mm(act, r.GM[...], TN).astype(jnp.bfloat16).reshape(per, hidden, D)

    tiles = 2 * D // TILE
    each(tiles, hidden_units)

    def up_grads(e):
        r.Au[:, :, cols(e)] = mm(r.N2[...], r.GU[:, cols(e)], TN).astype(jnp.bfloat16).reshape(n, R, TILE)

    total = sum(len(p) for _, p in numbered)
    got = [got_refs[3 * i : 3 * i + 3] for i in range(total)]
    s_sems = (s_send, (s_recv0, s_recv1, s_recv2), misc.at[46])
    acc = [r.Aq, r.Ao, r.Au, r.Ad, r.As]
    late, soon = (Scatter(me, core, part, acc, got, s_sems) for part in (numbered[:4], numbered[4:]))
    many = TILE // R

    def back_up(e):
        block = r.Wu[pl.ds(e * many, many)].reshape(TILE, 2 * D)
        r.PART[:, cols(e)] = mm(r.GU[...], block, NT)

    def mlp(e):
        r.M1[:, cols(e)] = mm(r.ACT[...], r.Wd[:, :, cols(e)].reshape(2 * D, TILE))

    def mlp_out():
        flying.gone.wait()
        r.SENT[mine, :] = r.M1[theirs, :].astype(jnp.bfloat16)
        flying.gone = to_pair(r.SENT.at[mine], r.GOT3)

    zeros = jnp.zeros((1, D), jnp.float32)

    def third(e, total):
        at = pl.ds(pl.multiple_of(e * STEP, STEP), STEP)
        x = r.X[at, :].astype(jnp.float32)
        dy = r.DY[at, :].astype(jnp.float32)
        middle = x + r.BA[at, :]
        inv = inverse(middle)
        grad = r.PART[at, :] + r.GOT2[at, :].astype(jnp.float32)
        scaled = gain2 * grad
        grad_middle = inv * scaled - middle * inv**3 * jnp.mean(scaled * middle, axis=1, keepdims=True)
        router = jnp.sum(x * w_router, axis=1, keepdims=True)
        r.GA[at, :] = (router * dy + grad_middle).astype(jnp.bfloat16)
        r.PART[at, :] = grad_middle
        counted = jnp.where(e < CAP // STEP, 1.0, 0.0)
        return total + counted * jnp.sum(grad * middle * inv, axis=0, keepdims=True)

    def third_rows():
        flying.gain2 = lax.fori_loop(0, 2 * CAP // STEP, third, zeros)

    def out_grads():
        r.Ao[own_heads] = mm(r.ATT[...], r.GA[:, near], TN).astype(jnp.bfloat16).reshape(n // 2, R, half)

    def attended_grads():
        r.GATT[...] = (mm(r.GA[:, near], wo_near(), NT) + mm(r.GA[:, away], wo_away(), NT)).astype(jnp.bfloat16)

    def other_out_grads():
        flying.gone.wait()
        r.Wo2[...] = mm(r.ATT[...], r.GA[:, away], TN).astype(jnp.bfloat16).reshape(n // 2, R, half)
        flying.out = to_pair(r.Wo2, r.Ao.at[own_heads])

    def attend_back(e):
        s, p, rows, q, k, v = heads(e)
        grad = r.GATT[rows, cols(p, 128)]
        gq, gk, gv = [], [], []
        for h in range(2):
            grad_h, q_h = jnp.where(lane == h, grad, zero), jnp.where(lane == h, q, zero)
            probs = r.PROBS[2 * e + h]
            grad_probs = mm(grad_h, v, NT)
            gv.append(mm(probs.astype(jnp.bfloat16), grad_h, TN))
            grad_scores = probs * (grad_probs - jnp.sum(probs * grad_probs, axis=1, keepdims=True))
            grad_scores = grad_scores.astype(jnp.bfloat16)
            gq.append(mm(grad_scores, k))
            gk.append(mm(grad_scores, q_h, TN))
        r.GQKV[rows, cols(p, 128)] = (jnp.where(lane == 0, gq[0], gq[1]) * factor).astype(jnp.bfloat16)
        r.GQKV[rows, cols(p + pairs, 128)] = ((gk[0] + gk[1]) * factor).astype(jnp.bfloat16)
        r.GQKV[rows, cols(p + 2 * pairs, 128)] = (gv[0] + gv[1]).astype(jnp.bfloat16)

    def qkv_grads(e):
        r.Aq[:, :, cols(e)] = mm(r.N1[...], r.GQKV[:, cols(e)], TN).astype(jnp.bfloat16).reshape(n, R, TILE)

    def back_qkv(e):
        block = r.Wq[pl.ds(e * many, many)].reshape(TILE, 3 * half)
        r.M1[:, cols(e)] = mm(r.GQKV[...], block, NT)

    def fourth(e, total):
        at = pl.ds(pl.multiple_of(e * STEP, STEP), STEP)
        x = r.X[at, :].astype(jnp.float32)
        dy = r.DY[at, :].astype(jnp.float32)
        combined = r.BA[at, :] + r.M1[at, :] + r.GOT3[at, :].astype(jnp.float32)
        router = jnp.sum(x * w_router, axis=1, keepdims=True)
        r.new[at, :] = (x + router * combined).astype(jnp.bfloat16)
        grad_router = jnp.sum(dy * combined, axis=1, keepdims=True)
        r.GR[at, :] = dy + grad_router * w_router + r.PART[at, :]
        return total + jnp.sum(grad_router * x, axis=0, keepdims=True)

    def fourth_rows():
        flying.router = lax.fori_loop(0, CAP // STEP, fourth, zeros)

    def last_out():
        r.SENT[theirs, :] = r.M1[theirs, :].astype(jnp.bfloat16)
        flying.gone = to_pair(r.SENT.at[theirs], r.GOT4)

    def fifth(e, total):
        at = pl.ds(pl.multiple_of(e * STEP, STEP), STEP)
        x = r.X[at, :].astype(jnp.float32)
        grad = r.M1[at, :] + r.GOT4[at, :].astype(jnp.float32)
        inv = inverse(x)
        scaled = gain1 * grad
        grad_x = inv * scaled - x * inv**3 * jnp.mean(scaled * x, axis=1, keepdims=True)
        below = pl.ds(pl.multiple_of(CAP + e * STEP, STEP), STEP)
        r.new[below, :] = (r.GR[at, :] + grad_x).astype(jnp.bfloat16)
        return total + jnp.sum(grad * x * inv, axis=0, keepdims=True)

    def fifth_rows():
        flying.gone.wait()
        gain1_grad = lax.fori_loop(0, CAP // STEP, fifth, zeros)
        small = jnp.concatenate([flying.router, gain1_grad, flying.gain2, jnp.zeros((5, D), jnp.float32)], axis=0)
        for block in range(n):
            tile = block * R // 128
            r.As[block] = small[:, tile * 128 : tile * 128 + 128]
        flying.small = to_pair(r.As, r.As2)

    def place(e):
        sent = mm(r.pick[...], r.new[:, cols(e)], TN).astype(jnp.bfloat16)
        r.rows_out[:, :, cols(e)] = sent.reshape(n, -1, TILE)

    def send_late():
        flying.rows = rows_out(n, me, core, r.rows_out, r.landed, *row_sems[3:])
        flying.small.wait()
        flying.out.wait()
        r.As[...] = r.As[...] + r.As2[...]

    backward = [some(up_grads, e, e + 2) for e in range(0, tiles, 2)] if SPLIT else []
    backward += [some(back_up, e, e + 1) for e in range(D // TILE)]
    backward += [lambda: pass_on(r.PART, r.GOT2)]
    backward += [some(mlp, e, e + 1) for e in range(D // TILE)]
    backward += [mlp_out, third_rows, out_grads, attended_grads, other_out_grads]
    backward += [some(attend_back, e, e + 1) for e in range(2 * pairs)]
    backward += [fourth_rows]
    backward += [some(back_qkv, e, e + 1) for e in range(D // TILE)]
    backward += [last_out]
    backward += [some(qkv_grads, e, e + 1) for e in range(3 * half // TILE)]
    backward += [fifth_rows, some(place, 0, D // TILE), send_late]
    each(tiles, up_grads)
    stages = soon.stages()
    cut = len(stages) * CUT // 100
    spread(stages[:cut], backward, 1, cut)
    rest, more = stages[cut:], late.stages()
    while rest or more:
        if more:
            more.pop(0)()
        if rest:
            rest.pop(0)()
    for gather in gathers:
        gather.drain()
    final = [to_pair(acc[k].at[me], ref) for k, ref in enumerate((r.FQ, r.FO, r.FU, r.FD))]

    def give(k, side, ref):
        value = ref[...].astype(jnp.float32)
        if k == 0:
            for j in range(3):
                r.gq[:, pl.ds(pl.multiple_of(j * D + side * half, 128), half)] = value[:, j * half : (j + 1) * half]
        elif k == 1:
            r.go[:, column(side, half, 0)] = value
        elif k == 2:
            for f in range(n):
                r.gu[:, column(2 * f + side, units, 0)] = value[:, f * units : (f + 1) * units]
        else:
            r.gd[pl.ds(pl.multiple_of(side * units, 8), units), :] = value

    for k in range(4):
        give(k, core, acc[k].at[me])
    r.gs[...] = r.As[me]
    for k, ref in enumerate((r.FQ, r.FO, r.FU, r.FD)):
        final[k].wait()
        give(k, 1 - core, ref)
    rows_wait(n, me, core, r.rows_out, r.landed, row_sems[3], row_sems[4], flying.rows)
    late.drain()
    soon.drain()


def whole_block(axes, n, cap, weights, vec, rows_in, pick, extra, notes):
    plan = first_shares(axes, 128) + second_shares(axes)
    bf, f32 = jnp.bfloat16, jnp.float32
    shards = weights
    weights = [
        jax.ShapeDtypeStruct((w.shape[0] // (2 if k == 3 else 1), w.shape[1] // (1 if k == 3 else 2)), bf)
        for k, w in enumerate(shards)
    ]
    R, F = weights[0].shape[0], weights[3].shape[0]
    vmem = pl.BlockSpec(memory_space=pltpu.VMEM)
    anywhere = pl.BlockSpec(memory_space=ANY)
    out = [jax.ShapeDtypeStruct(w.shape, f32) for w in shards]
    out += [
        jax.ShapeDtypeStruct((8, 128), f32),
        jax.ShapeDtypeStruct(rows_in.shape, bf),
        jax.ShapeDtypeStruct((2 * CAP, D), bf),
    ]
    rows = 2 * CAP
    half = D // 2
    V = pltpu.VMEM
    scratch = [V((n,) + w.shape, bf) for w in weights]
    scratch += [V((n,) + vec.shape, bf), V((n // 2, R, half), bf)]
    scratch += [V((n,) + w.shape, bf) for w in weights]
    scratch += [V((n, 8, 128), f32)] * 2
    scratch += [V((n, 2 * cap, D), bf), V((n, 2 * cap, D), bf)]
    scratch += [V((rows, D), bf)] * 3
    scratch += [V((rows, 3 * half), bf), V((HEADS, CAP, CAP), f32), V((rows, half), bf)]
    scratch += [V((rows, D), f32), V((rows, D), bf), V((rows, D), bf), V((rows, D), bf), V((CAP, D), bf), V((CAP, D), bf)]
    scratch += [V((rows, D), f32), V((rows, D), bf)]
    scratch += [V((rows, 2 * D), bf), V((rows, D), bf), V((rows, 2 * D), bf)]
    scratch += [V((rows, D), f32), V((rows, D), bf), V((rows, half), bf), V((rows, 3 * half), bf)]
    scratch += [V((CAP, D), f32), V((8, 128), f32)]
    scratch += [V(w.shape, bf) for w in weights]
    most = [1, 1, 1]
    total = 0
    deep = [R, R, R, F, 8]
    for order, parts in plan:
        total += len(parts)
        for p in parts:
            count = 1
            for phase in range(3):
                size = order[phase][1]
                kind = f32 if p.array == 4 else bf
                scratch.append(V((count, slots(size), deep[p.array], p.width), kind))
                most[phase] = max(most[phase], count * slots(size))
                count *= size
    dma = pltpu.SemaphoreType.DMA
    scratch += [dma((total, 3, 2)), dma((total, n)), dma((5,)), dma((total, 3))]
    scratch += [dma((total, m)) for m in most]
    scratch += [dma((48,))]
    return pl.pallas_call(
        functools.partial(block_kernel, axes, n, cap),
        out_shape=out,
        in_specs=[anywhere] * 6 + [vmem] * 3,
        out_specs=[vmem] * 5 + [anywhere, vmem],
        scratch_shapes=scratch,
        compiler_params=pltpu.CompilerParams(
            collective_id=2, has_side_effects=True, vmem_limit_bytes=67043328
        ),
        name="whole_block",
    )(*shards, vec, rows_in, pick, extra, notes)


def normalize(values, gain):
    inverse = lax.rsqrt(jnp.mean(values * values, axis=-1, keepdims=True) + EPSILON)
    return (values * inverse * gain, inverse)


def rms_back(values, inverse, gain, grad_normed):
    scaled = gain * grad_normed
    grad_values = inverse * scaled - values * inverse**3 * jnp.mean(
        scaled * values, axis=-1, keepdims=True
    )
    grad_gain = jnp.sum(grad_normed * values * inverse, axis=(0, 1))
    return (grad_values, grad_gain)


def split_heads(packed, offset):
    return packed[..., offset : offset + D].reshape(packed.shape[:2] + (HEADS, HEAD_DIM))


def narrow_body(
    axes,
    tokens,
    cotangent,
    w_qkv,
    w_out,
    w_up,
    w_down,
    w_router,
    gain_attn,
    gain_mlp,
    lengths,
    routed,
    dealing,
):
    factor = 1.0 / math.sqrt(HEAD_DIM)
    shards, place = lax.axis_size("fsdp"), lax.axis_index("fsdp")
    group_seqs, width = tokens.shape[1], tokens.shape[2]
    cap = min(24, width)
    slot_ids = jnp.arange(CAP, dtype=jnp.int32)
    picker = dealing[0][:, None] == jnp.arange(group_seqs, dtype=jnp.int32)[None, :]
    row_lengths = jnp.sum(jnp.where(picker, lengths[0][None, :], 0), axis=1)
    row_routes = jnp.sum(jnp.where(picker[:, :, None], routed[0][None, :, :], 0), axis=1)
    row_routes = jnp.where(slot_ids[None, :] < (row_lengths // 8)[:, None], row_routes, PAST)
    here = place * width + jnp.arange(width, dtype=jnp.int32)
    below = jnp.sum((row_routes[:, :, None] < here[None, None, :]).astype(jnp.int32), axis=1)
    upto = jnp.sum((row_routes[:, :, None] <= here[None, None, :]).astype(jnp.int32), axis=1)
    touched = upto > below
    living = here[None, :] < row_lengths[:, None]
    rank = jnp.where(touched, below - below[:, :1], -1)
    select = (rank[:, None, :] == jnp.arange(cap, dtype=jnp.int32)[None, :, None]).astype(jnp.bfloat16)
    shard_of = row_routes // width
    crowd = jnp.sum(
        (shard_of[:, :, None] == jnp.arange(shards, dtype=jnp.int32)[None, None, :]).astype(jnp.int32), axis=1
    )
    flag = jnp.broadcast_to((jnp.max(crowd) > cap).astype(jnp.float32), (8, 128))
    packed_rows = jnp.concatenate(
        [
            jnp.einsum("jip,jpd->jid", select, t[0], preferred_element_type=jnp.float32).astype(jnp.bfloat16)
            for t in (tokens, cotangent)
        ],
        axis=1,
    )
    seq_lengths = lax.dynamic_slice_in_dim(row_lengths, place, 1)
    routes = lax.dynamic_slice_in_dim(row_routes, place, 1)[0]
    valid_slot = slot_ids[None, :] < (seq_lengths // 8)[:, None]
    seq_shard = routes // width
    seq_rank = slot_ids - jnp.sum((routes[None, :] < (seq_shard * width)[:, None]).astype(jnp.int32), axis=1)
    fits = valid_slot[0] & (seq_rank < cap)
    landing = jnp.where(fits, seq_shard * (2 * cap) + seq_rank, -1)
    cells = jnp.arange(shards * 2 * cap, dtype=jnp.int32)
    pick = jnp.concatenate([landing[:, None] == cells[None, :], (landing[:, None] == (cells - cap)[None, :]) & fits[:, None]])
    pick = pick.astype(jnp.bfloat16)
    part = w_router.shape[0]
    vectors = jnp.pad(jnp.stack([w_router, gain_attn, gain_mlp]), ((0, 13), (0, 128 - part)))
    blocks = gather_all(axes, shards, [w_qkv, w_out, w_up, w_down, vectors], packed_rows, flag, 0)
    crowded = jnp.maximum(flag, blocks[6])[0, 0] > 0
    got_rows = jnp.einsum(
        "cs,sd->cd", pick, blocks[5].reshape(-1, D), preferred_element_type=jnp.float32
    ).astype(jnp.bfloat16)

    def all_rows(got):
        positions = jnp.arange(SEQ_MAX, dtype=jnp.int32)
        onehot = (routes[:, None] == positions[None, :]).astype(jnp.bfloat16)
        return jnp.concatenate(
            [
                jnp.dot(
                    onehot,
                    lax.all_to_all(t, "fsdp", split_axis=1, concat_axis=2, tiled=True)[0, 0],
                    preferred_element_type=jnp.float32,
                ).astype(jnp.bfloat16)
                for t in (tokens, cotangent)
            ]
        )

    if cap < width:
        got_rows = lax.cond(crowded, all_rows, lambda got: got, got_rows)
    rows_low = got_rows[None, :CAP]
    incoming_rows = rows_low.astype(jnp.float32)
    row_gradient = got_rows[None, CAP:].astype(jnp.float32)
    small = blocks[4][:, :3, :part].transpose(1, 0, 2).reshape(3, D)
    gathered = tuple(b.reshape(-1, b.shape[2]) for b in blocks[:4]) + (small[0], small[1], small[2])
    router_val = jnp.einsum("scd,d->sc", rows_low, gathered[4], preferred_element_type=jnp.float32)
    normed_attn, inverse_attn = normalize(incoming_rows, gathered[5].astype(jnp.float32))
    normed_low = normed_attn.astype(jnp.bfloat16)
    packed = jnp.einsum(
        "scd,de->sce", normed_low, gathered[0], preferred_element_type=jnp.float32
    ).astype(jnp.bfloat16)
    queries = split_heads(packed, 0)
    keys_heads = split_heads(packed, D)
    values_heads = split_heads(packed, 2 * D)
    scores = (
        jnp.einsum("sqhe,skhe->shqk", queries, keys_heads, preferred_element_type=jnp.float32)
        * factor
    )
    allowed = (slot_ids[None, :] <= slot_ids[:, None])[None, None] & valid_slot[:, None, None, :]
    scores = jnp.where(allowed, scores, -1e30)
    probs = jax.nn.softmax(scores, axis=-1)
    probs_low = probs.astype(jnp.bfloat16)
    attended = jnp.einsum(
        "shqk,skhe->sqhe", probs_low, values_heads, preferred_element_type=jnp.float32
    ).astype(jnp.bfloat16)
    attended = attended.reshape(incoming_rows.shape)
    branch_attn = jnp.einsum(
        "sce,ed->scd", attended, gathered[1], preferred_element_type=jnp.float32
    )
    middle = incoming_rows + branch_attn
    normed_mid, inverse_mid = normalize(middle, gathered[6].astype(jnp.float32))
    normed_mid_low = normed_mid.astype(jnp.bfloat16)
    upward = jnp.einsum(
        "scd,df->scf", normed_mid_low, gathered[2], preferred_element_type=jnp.float32
    )
    activated = jax.nn.gelu(upward).astype(jnp.bfloat16)
    branch_mlp = jnp.einsum(
        "scf,fd->scd", activated, gathered[3], preferred_element_type=jnp.float32
    )
    combined = branch_attn + branch_mlp
    refreshed_rows = (incoming_rows + router_val[..., None] * combined).astype(jnp.bfloat16)
    back_weights = gathered
    grad_comb = router_val[..., None] * row_gradient
    grad_router_val = jnp.sum(row_gradient * combined, axis=-1)
    total_gradient = row_gradient + grad_router_val[..., None] * back_weights[4].astype(jnp.float32)
    grad_mlp_low = grad_comb.astype(jnp.bfloat16)
    grad_act = jnp.einsum(
        "scd,fd->scf", grad_mlp_low, back_weights[3], preferred_element_type=jnp.float32
    )
    grad_downw = jnp.einsum(
        "scf,scd->fd", activated, grad_mlp_low, preferred_element_type=jnp.float32
    )
    unused, gelu_pull = jax.vjp(jax.nn.gelu, upward)
    grad_up_low = gelu_pull(grad_act)[0].astype(jnp.bfloat16)
    grad_normed_mid = jnp.einsum(
        "scf,df->scd", grad_up_low, back_weights[2], preferred_element_type=jnp.float32
    )
    grad_upw = jnp.einsum(
        "scd,scf->df", normed_mid_low, grad_up_low, preferred_element_type=jnp.float32
    )
    grad_middle, grad_gain_second = rms_back(
        middle, inverse_mid, back_weights[6].astype(jnp.float32), grad_normed_mid
    )
    grad_attn_low = (grad_comb + grad_middle).astype(jnp.bfloat16)
    total_gradient = total_gradient + grad_middle
    grad_attended = jnp.einsum(
        "scd,ed->sce", grad_attn_low, back_weights[1], preferred_element_type=jnp.float32
    ).astype(jnp.bfloat16)
    grad_outw = jnp.einsum(
        "sce,scd->ed", attended, grad_attn_low, preferred_element_type=jnp.float32
    )
    grad_att_heads = grad_attended.reshape(queries.shape)
    grad_probs = jnp.einsum(
        "sqhe,skhe->shqk", grad_att_heads, values_heads, preferred_element_type=jnp.float32
    )
    grad_values = jnp.einsum(
        "shqk,sqhe->skhe", probs_low, grad_att_heads, preferred_element_type=jnp.float32
    )
    grad_scores = probs * (grad_probs - jnp.sum(probs * grad_probs, axis=-1, keepdims=True))
    grad_scores_low = grad_scores.astype(jnp.bfloat16)
    grad_queries = (
        jnp.einsum(
            "shqk,skhe->sqhe", grad_scores_low, keys_heads, preferred_element_type=jnp.float32
        )
        * factor
    )
    grad_keys = (
        jnp.einsum("shqk,sqhe->skhe", grad_scores_low, queries, preferred_element_type=jnp.float32)
        * factor
    )
    flat_shape = incoming_rows.shape
    grad_packed = jnp.concatenate(
        [
            grad_queries.reshape(flat_shape),
            grad_keys.reshape(flat_shape),
            grad_values.reshape(flat_shape),
        ],
        axis=-1,
    ).astype(jnp.bfloat16)
    grad_qkvw = jnp.einsum(
        "scd,sce->de", normed_low, grad_packed, preferred_element_type=jnp.float32
    )
    grad_normed_attn = jnp.einsum(
        "sce,de->scd", grad_packed, back_weights[0], preferred_element_type=jnp.float32
    )
    grad_first_rows, grad_gain_first = rms_back(
        incoming_rows, inverse_attn, back_weights[5].astype(jnp.float32), grad_normed_attn
    )
    total_gradient = total_gradient + grad_first_rows
    grad_routerw = jnp.einsum(
        "scd,sc->d", incoming_rows, grad_router_val, precision=EXACT_PRECISION
    )
    new_rows = jnp.concatenate([refreshed_rows[0], total_gradient[0].astype(jnp.bfloat16)])
    sent_rows = (
        jnp.einsum("cs,cd->sd", pick, new_rows, preferred_element_type=jnp.float32)
        .astype(jnp.bfloat16)
        .reshape(shards, 2 * cap, D)
    )
    small_grads = jnp.stack([grad_routerw, grad_gain_first, grad_gain_second])
    small_grads = small_grads.reshape(3, shards, part).transpose(1, 0, 2)
    small_grads = jnp.pad(small_grads, ((0, 0), (0, 5), (0, 128 - part)))
    partial = [
        g.astype(jnp.bfloat16).reshape(shards, -1, g.shape[1])
        for g in (grad_qkvw, grad_outw, grad_upw, grad_downw)
    ]
    shares = scatter_all(axes, shards, partial + [small_grads], sent_rows, 1)
    totals = tuple(t.astype(jnp.float32) for t in shares[:4]) + tuple(shares[4][j, :part] for j in range(3))
    def place_rows(rows, held):
        spread = jnp.einsum("jip,jid->jpd", select, rows, preferred_element_type=jnp.float32).astype(jnp.bfloat16)
        kept = jnp.where(touched[..., None], spread, held[0])
        return jnp.where(living[..., None], kept, jnp.zeros_like(kept))[None]

    def compact(landed, rows):
        return place_rows(landed[:, :cap], tokens), place_rows(landed[:, cap:], cotangent)

    def entire(landed, rows):
        positions = jnp.arange(SEQ_MAX, dtype=jnp.int32)
        onehot = (routes[:, None] == positions[None, :]).astype(jnp.bfloat16)
        placed = []
        for r, held in ((rows[:CAP], tokens), (rows[CAP:], cotangent)):
            spread = jnp.einsum("cp,cd->pd", onehot, r, preferred_element_type=jnp.float32)
            spread = lax.all_to_all(
                spread.astype(jnp.bfloat16)[None, None], "fsdp", split_axis=2, concat_axis=1, tiled=True
            )
            kept = jnp.where(touched[..., None], spread[0], held[0])
            placed.append(jnp.where(living[..., None], kept, jnp.zeros_like(kept))[None])
        return tuple(placed)

    if cap < width:
        back_out, back_grad = lax.cond(crowded, entire, compact, shares[5], new_rows)
    else:
        back_out, back_grad = compact(shares[5], new_rows)
    return (
        back_out,
        back_grad,
        totals[0],
        totals[1],
        totals[2],
        totals[3],
        totals[4],
        totals[5],
        totals[6],
    )


def wide_body(
    axes,
    tokens,
    cotangent,
    w_qkv,
    w_out,
    w_up,
    w_down,
    w_router,
    gain_attn,
    gain_mlp,
    lengths,
    routed,
    dealing,
):
    factor = 1.0 / math.sqrt(HEAD_DIM)
    shards, place = lax.axis_size("fsdp"), lax.axis_index("fsdp")
    group_seqs, width = tokens.shape[1], tokens.shape[2]
    cap = min(24, width)
    slot_ids = jnp.arange(CAP, dtype=jnp.int32)
    picker = dealing[0][:, None] == jnp.arange(group_seqs, dtype=jnp.int32)[None, :]
    row_lengths = jnp.sum(jnp.where(picker, lengths[0][None, :], 0), axis=1)
    row_routes = jnp.sum(jnp.where(picker[:, :, None], routed[0][None, :, :], 0), axis=1)
    row_routes = jnp.where(slot_ids[None, :] < (row_lengths // 8)[:, None], row_routes, PAST)
    here = place * width + jnp.arange(width, dtype=jnp.int32)
    below = jnp.sum((row_routes[:, :, None] < here[None, None, :]).astype(jnp.int32), axis=1)
    upto = jnp.sum((row_routes[:, :, None] <= here[None, None, :]).astype(jnp.int32), axis=1)
    touched = upto > below
    living = here[None, :] < row_lengths[:, None]
    rank = jnp.where(touched, below - below[:, :1], -1)
    select = (rank[:, None, :] == jnp.arange(cap, dtype=jnp.int32)[None, :, None]).astype(jnp.bfloat16)
    shard_of = row_routes // width
    crowd = jnp.sum(
        (shard_of[:, :, None] == jnp.arange(shards, dtype=jnp.int32)[None, None, :]).astype(jnp.int32), axis=1
    )
    flag = jnp.broadcast_to((jnp.max(crowd) > cap).astype(jnp.float32), (8, 128))
    packed_rows = jnp.concatenate(
        [
            jnp.einsum("jip,jpd->jid", select, t[0], preferred_element_type=jnp.float32).astype(jnp.bfloat16)
            for t in (tokens, cotangent)
        ],
        axis=1,
    )
    seq_lengths = lax.dynamic_slice_in_dim(row_lengths, place, 1)
    routes = lax.dynamic_slice_in_dim(row_routes, place, 1)[0]
    valid_slot = slot_ids[None, :] < (seq_lengths // 8)[:, None]
    seq_shard = routes // width
    seq_rank = slot_ids - jnp.sum((routes[None, :] < (seq_shard * width)[:, None]).astype(jnp.int32), axis=1)
    fits = valid_slot[0] & (seq_rank < cap)
    landing = jnp.where(fits, seq_shard * (2 * cap) + seq_rank, -1)
    cells = jnp.arange(shards * 2 * cap, dtype=jnp.int32)
    pick = jnp.concatenate([landing[:, None] == cells[None, :], (landing[:, None] == (cells - cap)[None, :]) & fits[:, None]])
    pick = pick.astype(jnp.bfloat16)
    part = w_router.shape[0]
    mine = jnp.max(flag)
    other = lax.ppermute(flag, "rep", [(0, 1), (1, 0)])
    crowded = jnp.maximum(mine, jnp.max(other)) > 0
    positions = jnp.arange(SEQ_MAX, dtype=jnp.int32)

    def all_rows():
        onehot = (routes[:, None] == positions[None, :]).astype(jnp.bfloat16)
        return jnp.concatenate(
            [
                jnp.dot(
                    onehot,
                    lax.all_to_all(t, "fsdp", split_axis=1, concat_axis=2, tiled=True)[0, 0],
                    preferred_element_type=jnp.float32,
                ).astype(jnp.bfloat16)
                for t in (tokens, cotangent)
            ]
        )

    extra = jnp.zeros((2 * CAP, D), jnp.bfloat16)
    if cap < width:
        extra = lax.cond(crowded, all_rows, lambda: jnp.zeros((2 * CAP, D), jnp.bfloat16))
        pick = jnp.where(crowded, jnp.zeros_like(pick), pick)
    weights = [w_qkv, w_out, w_up, w_down]
    lanes = (place * part) % 128
    vectors = jnp.pad(jnp.stack([w_router, gain_attn, gain_mlp]), ((0, 13), (0, 0)))
    vectors = lax.dynamic_update_slice(jnp.zeros((16, 128), jnp.bfloat16), vectors, (0, lanes))
    notes = jnp.broadcast_to(valid_slot.astype(jnp.float32), (8, CAP))
    gq, go, gu, gd, gs, landed, new_rows = whole_block(
        axes, shards, cap, weights, vectors, packed_rows, pick, extra, notes
    )
    small = lax.dynamic_slice(gs, (0, lanes), (8, part))
    totals = (gq, go, gu, gd, small[0], small[1], small[2])

    def place_rows(rows, held):
        spread = jnp.einsum("jip,jid->jpd", select, rows, preferred_element_type=jnp.float32).astype(jnp.bfloat16)
        kept = jnp.where(touched[..., None], spread, held[0])
        return jnp.where(living[..., None], kept, jnp.zeros_like(kept))[None]

    def compact(landed, rows):
        return place_rows(landed[:, :cap], tokens), place_rows(landed[:, cap:], cotangent)

    def entire(landed, rows):
        positions = jnp.arange(SEQ_MAX, dtype=jnp.int32)
        onehot = (routes[:, None] == positions[None, :]).astype(jnp.bfloat16)
        placed = []
        for r, held in ((rows[:CAP], tokens), (rows[CAP:], cotangent)):
            spread = jnp.einsum("cp,cd->pd", onehot, r, preferred_element_type=jnp.float32)
            spread = lax.all_to_all(
                spread.astype(jnp.bfloat16)[None, None], "fsdp", split_axis=2, concat_axis=1, tiled=True
            )
            kept = jnp.where(touched[..., None], spread[0], held[0])
            placed.append(jnp.where(living[..., None], kept, jnp.zeros_like(kept))[None])
        return tuple(placed)

    if cap < width:
        back_out, back_grad = lax.cond(crowded, entire, compact, landed, new_rows)
    else:
        back_out, back_grad = compact(landed, new_rows)
    return (
        back_out,
        back_grad,
        totals[0],
        totals[1],
        totals[2],
        totals[3],
        totals[4],
        totals[5],
        totals[6],
    )


def body(axes, *arrays):
    run = wide_body if arrays[2].shape[0] % 16 == 0 else narrow_body
    return run(axes, *arrays)


def solution(mesh):
    placed = (
        P("rep", None, "fsdp", None),
        P("rep", None, "fsdp", None),
        P("fsdp", None),
        P("fsdp", None),
        P("fsdp", None),
        P("fsdp", None),
        P("fsdp"),
        P("fsdp"),
        P("fsdp"),
        P("rep", None),
        P("rep", None, None),
        P("rep", None),
    )
    return jax.shard_map(
        functools.partial(body, grid_axes(mesh)),
        mesh=mesh,
        in_specs=placed,
        out_specs=(
            P("rep", None, "fsdp", None),
            P("rep", None, "fsdp", None),
            P("fsdp", None),
            P("fsdp", None),
            P("fsdp", None),
            P("fsdp", None),
            P("fsdp"),
            P("fsdp"),
            P("fsdp"),
        ),
        check_vma=False,
    )
```

```python
import math
import functools

import jax
import jax.numpy as jnp
from jax import lax
from jax.experimental import pallas as pl
from jax.experimental.pallas import tpu as pltpu
from jax.sharding import PartitionSpec as P

D = 1024
HEADS = 16
HEAD_DIM = 64
SEQ_MAX = 1024
CAP = 128
PAST = 1 << 24


EPSILON = 1e-06
EXACT_PRECISION = lax.Precision.HIGHEST

MESH = pl.DeviceIdType.MESH
ANY = pl.ANY


def grid_axes(mesh):
    devices = mesh.devices[:, 0]
    count = len(devices)
    axes = []
    spots = [getattr(d, "coords", None) for d in devices]
    if all(s is not None for s in spots) and len(set(map(tuple, spots))) == count:
        low = [min(s[k] for s in spots) for k in range(3)]
        at = {tuple(s[k] - low[k] for k in range(3)): f for f, s in enumerate(spots)}
        for k in range(3):
            size = max(s[k] for s in spots) - low[k] + 1
            one = tuple(int(j == k) for j in range(3))
            axes.append((at[one] if size > 1 else 1, size, k))
        ok = all(
            f == sum(stride * spot[k] for stride, _, k in axes) for spot, f in at.items()
        )
        axes = [a[:2] for a in axes] if ok else []
    if not axes:
        axes, left = [], count
        for size in (2, 2):
            size = size if left % size == 0 and left > 1 else 1
            axes.append((count // left, size))
            left //= size
        axes.append((count // left, left))
    return sorted(axes, key=lambda a: -a[1])


def xor(a, b, size):
    out, bit = 0, 1
    while bit < size:
        out = out + ((a // bit + b // bit) % 2) * bit
        bit *= 2
    return out


class Piece:
    def __init__(self, array, half, offset, width):
        self.array, self.half, self.offset, self.width = array, half, offset, width

    def cols(self, core):
        start = self.offset
        if self.half:
            start = core * self.half + start
            start = pl.multiple_of(start, 128)
        return pl.ds(start, self.width)


def colours(axes, widths):
    qkv, out, up, down = (w // 2 for w in widths[:4])
    a, b, c = axes
    third = qkv // 3
    return [
        ((b, c, a), [Piece(1, out, 0, out), Piece(4, 0, 0, widths[4])]),
        ((c, b, a), [Piece(0, qkv, 0, third)]),
        ((a, b, c), [Piece(2, up, 0, up), Piece(0, qkv, third, third)]),
        ((a, c, b), [Piece(3, down, 0, down), Piece(0, qkv, 2 * third, third)]),
    ]


def enter(n, me, core):
    barrier = pltpu.get_barrier_semaphore()

    def hello(i, _):
        pl.semaphore_signal(barrier, inc=1, device_id=((me + i) % n, core), device_id_type=MESH)
        return 0

    lax.fori_loop(1, n, hello, 0)
    pl.semaphore_signal(barrier, inc=1, device_id=(me, 1 - core), device_id_type=MESH)
    pl.semaphore_wait(barrier, n)


def rows_out(n, me, core, rows, landing, send_sem, recv_sem, own_sem):
    own = pltpu.make_async_copy(rows.at[me], landing.at[me], own_sem)
    own.start()

    def go(i, _):
        to = (me + i) % n
        pltpu.make_async_remote_copy(
            src_ref=rows.at[to], dst_ref=landing.at[me], send_sem=send_sem, recv_sem=recv_sem,
            device_id=(to, core), device_id_type=MESH,
        ).start()
        return 0

    lax.fori_loop(1, n, go, 0)
    return own


def rows_each(n, me, core, rows, landing, send_sem, recv_sem, own_sem):
    own = pltpu.make_async_copy(rows.at[me], landing.at[me], own_sem)
    own.start()

    def go(i):
        to = (me + i) % n
        pltpu.make_async_remote_copy(
            src_ref=rows.at[to], dst_ref=landing.at[me], send_sem=send_sem, recv_sem=recv_sem,
            device_id=(to, core), device_id_type=MESH,
        ).start()

    return own, [functools.partial(go, i) for i in (ORDER or range(1, n))]


def rows_wait(n, me, core, rows, landing, send_sem, recv_sem, own):
    own.wait()
    for which in range(2):
        copy = pltpu.make_async_remote_copy(
            src_ref=rows.at[pl.ds(0, n - 1)], dst_ref=landing.at[pl.ds(0, n - 1)],
            send_sem=send_sem, recv_sem=recv_sem, device_id=(me, 1 - core), device_id_type=MESH,
        )
        copy.wait_recv() if which else copy.wait_send()


def gather_kernel(axes, plan, n, *refs):
    k = 5
    ins, rows, flag = refs[:k], refs[k], refs[k + 1]
    outs, landing, other = refs[k + 2 : 2 * k + 2], refs[2 * k + 2], refs[2 * k + 3]
    stages = refs[2 * k + 4 : 3 * k + 4]
    send_sem, recv_sem, pair_send, pair_recv, local_sem, row_sems = refs[3 * k + 4 :]
    me, core = lax.axis_index("fsdp"), lax.axis_index("rep")
    enter(n, me, core)
    told = pltpu.make_async_remote_copy(
        src_ref=flag, dst_ref=other, send_sem=row_sems.at[3], recv_sem=row_sems.at[4],
        device_id=(me, 1 - core), device_id_type=MESH,
    )
    told.start()
    numbered, number = [], 0
    for order, pieces in plan:
        numbered.append((order, [(number + i, p) for i, p in enumerate(pieces)]))
        number += len(pieces)

    def spot(axis):
        return (me // axis[0]) % axis[1]

    def dst(piece, block):
        return outs[piece.array].at[block, :, piece.cols(core)]

    def put(pieces, block, own, phase, way, device, pair=False):
        for i, piece in pieces:
            if pair and not piece.half:
                continue
            src = ins[piece.array].at[:, piece.cols(core)] if own else dst(piece, block)
            pltpu.make_async_remote_copy(
                src_ref=src,
                dst_ref=dst(piece, block),
                send_sem=pair_send.at[i] if pair else send_sem.at[i, phase, way],
                recv_sem=pair_recv.at[i] if pair else recv_sem.at[i, block],
                device_id=device,
                device_id_type=MESH,
            ).start()

    def along(pieces, order, block, own, phase, ways):
        stride, size = order[phase]
        at = spot(order[phase])
        if size == 1:
            return
        if size == 2:
            put(pieces, block, own, phase, 0, (me + (1 - 2 * at) * stride, core))
            return
        for way in ways:
            step = 1 - 2 * way
            pl.when(at < size - 1 if way == 0 else at > 0)(
                functools.partial(put, pieces, block, own, phase, way, (me + step * stride, core))
            )

    def arrived(pieces, order, block, phase, way):
        for i, piece in pieces:
            pltpu.make_async_remote_copy(
                src_ref=dst(piece, block),
                dst_ref=dst(piece, block),
                send_sem=send_sem.at[i, phase, way],
                recv_sem=recv_sem.at[i, block],
                device_id=(me, 1 - core),
                device_id_type=MESH,
            ).wait_recv()
        if order[phase][1] > 2:
            along(pieces, order, block, False, phase, (way,))
        for later in range(phase + 1, 3):
            along(pieces, order, block, False, later, (0, 1))
        put(pieces, block, False, 0, 0, (me, 1 - core), pair=True)

    for order, pieces in numbered:
        for phase in range(3):
            along(pieces, order, me, True, phase, (0, 1))
    own = rows_out(n, me, core, rows, landing, row_sems.at[0], row_sems.at[1], row_sems.at[2])
    local = []
    for j in range(k):
        local.append(pltpu.make_async_copy(ins[j], stages[j], local_sem.at[j]))
        local[-1].start()
    events = []
    for number, (order, pieces) in enumerate(numbered):
        heavy = number >= 2
        sizes = [a[1] for a in order]
        for phase in range(3):
            size = sizes[phase]
            rest = 1
            for s in sizes[:phase]:
                rest *= s
            for t in range(1, size):
                ways = (0,) if size == 2 else (0, 1)
                for way in ways:
                    for j in range(rest):
                        if heavy:
                            key = 20 * t if phase == 0 else 20 * phase + 20 * (j + (t - 1) * rest + 1)
                        else:
                            key = 5 if phase == 0 else 10 + 5 * j if phase == 1 else 15 + 40 * t + 5 * j
                        events.append((key, len(events), order, pieces, phase, t, way, j))
    events.sort(key=lambda e: e[:2])

    def run(order, pieces, phase, t, way, j):
        stride, size = order[phase]
        at = spot(order[phase])
        origin = 1 - at if size == 2 else at - (1 - 2 * way) * t
        block = me + (origin - at) * stride
        for s, z in order[:phase]:
            here = (me // s) % z
            block = block + (xor(here, j % z, z) - here) * s
            j = j // z
        if size == 2:
            arrived(pieces, order, block, phase, 0)
        else:
            pl.when((origin >= 0) & (origin < size))(
                functools.partial(arrived, pieces, order, block, phase, way)
            )

    def settle():
        for j in range(k):
            local[j].wait()
            local[j] = pltpu.make_async_copy(stages[j], outs[j].at[me], local_sem.at[j])
            local[j].start()

    for number, (_, _, order, pieces, phase, t, way, j) in enumerate(events):
        run(order, pieces, phase, t, way, j)
        if number == 3:
            settle()
    for copy in local:
        copy.wait()
    told.wait()
    rows_wait(n, me, core, rows, landing, row_sems.at[0], row_sems.at[1], own)

    def drain(i, piece, count, send, recv, which):
        many = outs[piece.array].at[pl.ds(0, count), :, piece.cols(core)]
        copy = pltpu.make_async_remote_copy(
            src_ref=many, dst_ref=many, send_sem=send, recv_sem=recv,
            device_id=(me, 1 - core), device_id_type=MESH,
        )
        if which == "send":
            copy.wait_send()
        else:
            copy.wait_recv()

    for order, pieces in numbered:
        rest = 1
        for phase in range(3):
            stride, size = order[phase]
            at = spot(order[phase])
            for i, piece in pieces:
                if size == 2:
                    drain(i, piece, rest, send_sem.at[i, phase, 0], recv_sem.at[i, 0], "send")
                elif size > 2:
                    for here in range(size):
                        def both(here=here, i=i, piece=piece, phase=phase, rest=rest, size=size):
                            if here < size - 1:
                                drain(i, piece, (here + 1) * rest, send_sem.at[i, phase, 0], recv_sem.at[i, 0], "send")
                            if here > 0:
                                drain(i, piece, (size - here) * rest, send_sem.at[i, phase, 1], recv_sem.at[i, 0], "send")
                        pl.when(at == here)(both)
            rest *= size
        for i, piece in pieces:
            if piece.half:
                drain(i, piece, n - 1, pair_send.at[i], pair_recv.at[i], "send")
                drain(i, piece, n - 1, pair_send.at[i], pair_recv.at[i], "recv")


def gather_all(axes, n, arrays, rows, flag, collective_id):
    plan = colours(axes, [a.shape[1] for a in arrays])
    pieces = sum(len(p) for _, p in plan)
    vmem = pl.BlockSpec(memory_space=pltpu.VMEM)
    anywhere = pl.BlockSpec(memory_space=ANY)
    dma = pltpu.SemaphoreType.DMA
    return pl.pallas_call(
        functools.partial(gather_kernel, axes, plan, n),
        out_shape=[jax.ShapeDtypeStruct((n,) + a.shape, a.dtype) for a in arrays]
        + [jax.ShapeDtypeStruct(a.shape, a.dtype) for a in (rows, flag)],
        in_specs=[anywhere] * len(arrays) + [vmem, vmem],
        out_specs=[anywhere] * (len(arrays) + 1) + [vmem],
        scratch_shapes=[pltpu.VMEM(a.shape, a.dtype) for a in arrays]
        + [dma((pieces, 3, 2)), dma((pieces, n)), dma((pieces,)), dma((pieces,)), dma((len(arrays),)), dma((5,))],
        compiler_params=pltpu.CompilerParams(collective_id=collective_id, has_side_effects=True),
        name="gather_all",
    )(*arrays, rows, flag)
def add_into(acc, a, got, g, rows):
    step = min(rows, 16)

    def go(i, _):
        at = pl.ds(pl.multiple_of(i * step, step), step)
        acc[a, at, :] = (acc[a, at, :].astype(jnp.float32) + got[g, at, :].astype(jnp.float32)).astype(acc.dtype)
        return 0

    lax.fori_loop(0, rows // step, go, 0)


def turn(at, t, size):
    if size == 2:
        return at + (1 - 2 * at) * (1 - t)
    up = size - 1 - at
    first_up = jnp.where(t < up, size - 1 - t, t - up)
    first_down = jnp.where(t < at, t, size - 1 - (t - at))
    return jnp.where(t == size - 1, at, jnp.where(2 * at < size, first_up, first_down))


def slots(size):
    return 1 if size <= 2 else size + 1


def scatter_kernel(axes, plan, n, *refs):
    k = 5
    ins, rows, outs, landing = refs[:k], refs[k], refs[k + 1 : 2 * k + 1], refs[2 * k + 1]
    total = sum(len(p) for _, p in plan)
    buffers = refs[2 * k + 2 : 2 * k + 2 + 5 * total]
    own_sem, pair_send, pair_recv, send_sem = refs[-10:-6]
    recv_sems, last_send, last_recv, row_sems = refs[-6:-3], refs[-3], refs[-2], refs[-1]
    me, core = lax.axis_index("fsdp"), lax.axis_index("rep")
    enter(n, me, core)
    numbered, number = [], 0
    for order, pieces in plan:
        numbered.append((order, [(number + i, p) for i, p in enumerate(pieces)]))
        number += len(pieces)
    acc = [buffers[5 * i] for i in range(total)]
    pair = [buffers[5 * i + 1] for i in range(total)]
    got = [buffers[5 * i + 2 : 5 * i + 5] for i in range(total)]

    def spot(axis):
        return (me // axis[0]) % axis[1]

    def pair_copy(i, piece, block):
        return pltpu.make_async_remote_copy(
            src_ref=ins[piece.array].at[block, :, piece.cols(1 - core)],
            dst_ref=pair[i].at[block],
            send_sem=pair_send.at[i],
            recv_sem=pair_recv.at[i, block],
            device_id=(me, 1 - core),
            device_id_type=MESH,
        )

    def own_copy(i, piece, block):
        return pltpu.make_async_copy(
            ins[piece.array].at[block, :, piece.cols(core)], acc[i].at[block], own_sem.at[i, block]
        )

    def block_at(order, phase, origin, turns):
        block = me + (origin - spot(order[phase])) * order[phase][0]
        for axis, t in zip(order[:phase], turns):
            block = block + (turn(spot(axis), t, axis[1]) - spot(axis)) * axis[0]
        return block

    def ready(pieces, block):
        for i, piece in pieces:
            own_copy(i, piece, block).wait()
            pair_copy(i, piece, block).wait_recv()
            add_into(acc[i], block, pair[i], block, acc[i].shape[1])

    def hop(i, phase, block, rest, slot, send, device):
        return pltpu.make_async_remote_copy(
            src_ref=acc[i].at[block],
            dst_ref=got[i][phase].at[rest, slot],
            send_sem=send,
            recv_sem=recv_sems[phase].at[i, rest * got[i][phase].shape[1] + slot],
            device_id=device,
            device_id_type=MESH,
        )

    def take(pieces, phase, block, rest, slot):
        for i, piece in pieces:
            hop(i, phase, block, rest, slot, send_sem.at[i, phase], (me, 1 - core)).wait_recv()
            add_into(acc[i], block, got[i][phase].at[rest], slot, acc[i].shape[1])

    def give(pieces, phase, block, rest, slot, device):
        for i, piece in pieces:
            hop(i, phase, block, rest, slot, send_sem.at[i, phase], device).start()

    def event(order, pieces, phase, t, turns, first):
        stride, size = order[phase]
        at = spot(order[phase])
        origin = turn(at, t, size)
        mine = t == size - 1
        block = block_at(order, phase, origin, turns)
        rest = 0
        for axis, away in zip(order[:phase], turns):
            rest = rest * axis[1] + away
        if first:
            ready(pieces, block)
        if size == 1:
            return
        if size == 2:
            pl.when(jnp.logical_not(mine))(
                lambda: give(pieces, phase, block, rest, 0, (me + (1 - 2 * at) * stride, core))
            )
            pl.when(mine)(lambda: take(pieces, phase, block, rest, 0))
            return

        @pl.when(jnp.logical_not(mine))
        def _():
            up = (origin > at).astype(jnp.int32)
            behind = jnp.where(up == 1, at > 0, at < size - 1)
            pl.when(behind)(lambda: take(pieces, phase, block, rest, origin))
            step = 2 * up - 1
            landing = jnp.where((up == 0) & (origin == at - 1), size, origin)
            give(pieces, phase, block, rest, landing, (me + step * stride, core))

        @pl.when(mine)
        def _():
            pl.when(at > 0)(lambda: take(pieces, phase, block, rest, at))
            pl.when(at < size - 1)(lambda: take(pieces, phase, block, rest, size))

    def each(count, fn):
        lax.fori_loop(0, count, lambda e, _: (fn(e), 0)[1], 0)

    def begin(order, pieces, s):
        _, (_, nq), (_, nr) = order

        def go(e):
            block = block_at(order, 2, turn(spot(order[2]), e // nq, nr), (s, e % nq))
            for i, piece in pieces:
                pair_copy(i, piece, block).start()
                own_copy(i, piece, block).start()

        each(nr * nq, go)

    def lead(order, pieces, s):
        _, (_, nq), (_, nr) = order
        each((nr - 1) * nq, lambda e: event(order, pieces, 2, e // nq, (s, e % nq), True))

    def later(order, pieces, s, low, high):
        def go(e):
            event(order, pieces, 2, order[2][1] - 1, (s, low + e), True)
            event(order, pieces, 1, low + e, (s,), False)

        each(high - low, go)

    def finish(order, pieces, s):
        event(order, pieces, 0, s, (), False)

    light, heavy = numbered[:2], numbered[2:]
    steps, few = heavy[0][0][0][1], max(c[0][0][1] for c in light)

    def begin_all(s):
        for colour in heavy:
            pl.when(s < steps)(lambda colour=colour: begin(*colour, s))
        for colour in light:
            pl.when(s < colour[0][0][1])(lambda colour=colour: begin(*colour, s))

    each(max(steps, few), begin_all)
    own = rows_out(n, me, core, rows, landing, row_sems.at[0], row_sems.at[1], row_sems.at[2])
    for colour in heavy + light:
        lead(*colour, 0)

    def step(s):
        for colour in heavy:
            pl.when(s < steps)(lambda colour=colour: later(*colour, s, 0, 1))
        for colour in heavy:
            pl.when(s + 1 < steps)(lambda colour=colour: lead(*colour, s + 1))
        for colour in heavy:
            pl.when((s >= 1) & (s < steps))(lambda colour=colour: finish(*colour, s - 1))
        for colour in light:
            size = colour[0][0][1]
            pl.when(s + 1 < size)(lambda colour=colour: lead(*colour, s + 1))
        for colour in heavy:
            pl.when(s < steps)(lambda colour=colour: later(*colour, s, 1, colour[0][1][1]))
        for colour in light:
            size = colour[0][0][1]

            @pl.when((s >= 1) & (s <= size))
            def _(colour=colour):
                later(*colour, s - 1, 0, colour[0][1][1])
                finish(*colour, s - 1)
        for colour in heavy:
            pl.when(s == steps - 1)(lambda colour=colour: finish(*colour, s))

    each(max(steps, few + 1), step)

    final = []
    for order, pieces in numbered:
        for i, piece in pieces:
            outs[piece.array][:, piece.cols(core)] = acc[i][me]
            if piece.half:
                final.append(
                    pltpu.make_async_remote_copy(
                        src_ref=acc[i].at[me],
                        dst_ref=outs[piece.array].at[:, piece.cols(core)],
                        send_sem=last_send.at[i],
                        recv_sem=last_recv.at[i],
                        device_id=(me, 1 - core),
                        device_id_type=MESH,
                    )
                )
                final[-1].start()
    for copy in final:
        copy.wait()
    rows_wait(n, me, core, rows, landing, row_sems.at[0], row_sems.at[1], own)

    def drain(i, phase, count):
        many = acc[i].at[pl.ds(0, count)]
        pltpu.make_async_remote_copy(
            src_ref=many, dst_ref=many, send_sem=send_sem.at[i, phase], recv_sem=last_recv.at[i],
            device_id=(me, 1 - core), device_id_type=MESH,
        ).wait_send()

    for order, pieces in numbered:
        for i, piece in pieces:
            for phase in range(3):
                if order[phase][1] > 1:
                    count = order[phase][1] - 1
                    for axis in order[:phase]:
                        count *= axis[1]
                    drain(i, phase, count)
            many = acc[i].at[pl.ds(0, n)]
            pltpu.make_async_remote_copy(
                src_ref=many, dst_ref=many, send_sem=pair_send.at[i], recv_sem=last_recv.at[i],
                device_id=(me, 1 - core), device_id_type=MESH,
            ).wait_send()


def scatter_all(axes, n, arrays, rows, collective_id):
    plan = colours(axes, [a.shape[2] for a in arrays])
    pieces = [(order, p) for order, ps in plan for p in ps]
    scratch = []
    for order, p in pieces:
        deep, dtype = arrays[p.array].shape[1], arrays[p.array].dtype
        scratch += [pltpu.VMEM((n, deep, p.width), dtype)] * 2
        count = 1
        for phase in range(3):
            size = order[phase][1]
            scratch.append(pltpu.VMEM((count, slots(size), deep, p.width), dtype))
            count *= size
    total = len(pieces)
    shapes = []
    for phase in range(3):
        most = 1
        for order, _ in plan:
            count = slots(order[phase][1])
            for a in order[:phase]:
                count *= a[1]
            most = max(most, count)
        shapes.append((total, most))
    dma = pltpu.SemaphoreType.DMA
    return pl.pallas_call(
        functools.partial(scatter_kernel, axes, plan, n),
        out_shape=[jax.ShapeDtypeStruct(a.shape[1:], a.dtype) for a in arrays]
        + [jax.ShapeDtypeStruct(rows.shape, rows.dtype)],
        in_specs=[pl.BlockSpec(memory_space=ANY)] * len(arrays) + [pl.BlockSpec(memory_space=pltpu.VMEM)],
        out_specs=[pl.BlockSpec(memory_space=pltpu.VMEM)] * len(arrays) + [pl.BlockSpec(memory_space=ANY)],
        scratch_shapes=scratch
        + [dma((total, n)), dma((total,)), dma((total, n)), dma((total, 3))]
        + [dma(s) for s in shapes]
        + [dma((total,)), dma((total,)), dma((3,))],
        compiler_params=pltpu.CompilerParams(
            collective_id=collective_id, has_side_effects=True, vmem_limit_bytes=60 * 1024 * 1024
        ),
        name="scatter_all",
    )(*arrays, rows)


SQRT_2_PI = math.sqrt(2.0 / math.pi)
NN = (((1,), (0,)), ((), ()))
NT = (((1,), (1,)), ((), ()))
TN = (((0,), (0,)), ((), ()))


def mm(a, b, dims=NN):
    return lax.dot_general(a, b, dims, preferred_element_type=jnp.float32)


def each(count, fn):
    lax.fori_loop(0, count, lambda e, _: (fn(e), 0)[1], 0)


class Part:
    def __init__(self, array, offset, width):
        self.array, self.offset, self.width = array, offset, width

    def of(self, ref, block):
        return ref.at[block, :, pl.ds(self.offset, self.width)]


EARLY, AT0, AT1, CUT, SPLIT = 30, 4, 85, 50, False
AHEAD = 2
ROWS_IN, ROWS_OUT, ORDER = (0, 100), 4, ()


def first_shares(axes, vectors):
    a, b, c = axes
    half = D // 2
    return [
        ((b, c, a), [Part(1, 0, D // 8), Part(4, 0, vectors)]),
        ((c, b, a), [Part(0, 0, D // 8)]),
        ((a, b, c), [Part(0, D // 8, half + 3 * D // 8)]),
        ((a, c, b), [Part(0, D, half), Part(1, D // 8, 3 * D // 8)]),
    ]


def second_shares(axes):
    a, b, c = axes
    return [
        ((b, c, a), [Part(2, 0, 3 * D // 8)]),
        ((c, b, a), [Part(3, 0, D // 4)]),
        ((a, b, c), [Part(2, 3 * D // 8, 13 * D // 8)]),
        ((a, c, b), [Part(3, D // 4, 3 * D // 4)]),
    ]


def number_parts(plan):
    numbered, number = [], 0
    for order, parts in plan:
        numbered.append((order, [(number + i, p) for i, p in enumerate(parts)]))
        number += len(parts)
    return numbered


def send(src, dst, send_sem, recv_sem, device):
    return pltpu.make_async_remote_copy(
        src_ref=src, dst_ref=dst, send_sem=send_sem, recv_sem=recv_sem, device_id=device, device_id_type=MESH
    )


class Gather:
    def __init__(self, n, me, core, numbered, whole, sems):
        self.n, self.me, self.core, self.numbered, self.whole = n, me, core, numbered, whole
        self.send_sem, self.recv_sem = sems

    def spot(self, axis):
        return (self.me // axis[0]) % axis[1]

    def put(self, parts, block, phase, way, step):
        for i, part in parts:
            dst = part.of(self.whole[part.array], block)
            send(
                dst, dst, self.send_sem.at[i, phase, way], self.recv_sem.at[i, block], (self.me + step, self.core)
            ).start()

    def along(self, parts, order, block, phase, ways):
        stride, size = order[phase]
        at = self.spot(order[phase])
        if size == 2:
            self.put(parts, block, phase, 0, (1 - 2 * at) * stride)
        elif size > 2:
            for way in ways:
                step = (1 - 2 * way) * stride
                pl.when(at < size - 1 if way == 0 else at > 0)(
                    functools.partial(self.put, parts, block, phase, way, step)
                )

    def arrived(self, parts, order, block, phase, way):
        for i, part in parts:
            dst = part.of(self.whole[part.array], block)
            send(
                dst, dst, self.send_sem.at[i, phase, way], self.recv_sem.at[i, block], (self.me, 1 - self.core)
            ).wait_recv()
        if order[phase][1] > 2:
            self.along(parts, order, block, phase, (way,))
        for later in range(phase + 1, 3):
            self.along(parts, order, block, later, (0, 1))

    def start(self):
        for order, parts in self.numbered:
            for phase in range(3):
                self.along(parts, order, self.me, phase, (0, 1))

    def events(self):
        found = []
        for number, (order, parts) in enumerate(self.numbered):
            heavy = number >= 2
            sizes = [a[1] for a in order]
            for phase in range(3):
                size, rest = sizes[phase], math.prod(sizes[:phase])
                for t in range(1, size):
                    for way in (0,) if size == 2 else (0, 1):
                        for j in range(rest):
                            if heavy:
                                key = 20 * t if phase == 0 else 20 * phase + 20 * (j + (t - 1) * rest + 1)
                            else:
                                key = 5 if phase == 0 else 10 + 5 * j if phase == 1 else 15 + 40 * t + 5 * j
                            found.append((key, len(found), order, parts, phase, t, way, j))
        found.sort(key=lambda e: e[:2])
        return [functools.partial(self.run, *e[2:]) for e in found]

    def run(self, order, parts, phase, t, way, j):
        stride, size = order[phase]
        at = self.spot(order[phase])
        origin = 1 - at if size == 2 else at - (1 - 2 * way) * t
        block = self.me + (origin - at) * stride
        for s, z in order[:phase]:
            here = (self.me // s) % z
            block = block + (xor(here, j % z, z) - here) * s
            j = j // z
        if size == 2:
            self.arrived(parts, order, block, phase, 0)
        else:
            pl.when((origin >= 0) & (origin < size))(
                functools.partial(self.arrived, parts, order, block, phase, way)
            )

    def drain(self):
        for order, parts in self.numbered:
            rest = 1
            for phase in range(3):
                size = order[phase][1]
                at = self.spot(order[phase])
                for i, part in parts:
                    def gone(count, way, i=i, part=part, phase=phase):
                        many = part.of(self.whole[part.array], pl.ds(0, count))
                        send(
                            many, many, self.send_sem.at[i, phase, way], self.recv_sem.at[i, 0], (self.me, 1 - self.core)
                        ).wait_send()

                    if size == 2:
                        gone(rest, 0)
                    elif size > 2:
                        for here in range(size):
                            def both(here=here, gone=gone, rest=rest, size=size):
                                if here < size - 1:
                                    gone((here + 1) * rest, 0)
                                if here > 0:
                                    gone((size - here) * rest, 1)
                            pl.when(at == here)(both)
                rest *= size


class Scatter:
    def __init__(self, me, core, numbered, acc, got, sems):
        self.me, self.core, self.numbered, self.acc, self.got = me, core, numbered, acc, got
        self.send_sem, self.recv_sems, self.drain_sem = sems

    def spot(self, axis):
        return (self.me // axis[0]) % axis[1]

    def block_at(self, order, phase, origin, turns):
        block = self.me + (origin - self.spot(order[phase])) * order[phase][0]
        for axis, t in zip(order[:phase], turns):
            block = block + (turn(self.spot(axis), t, axis[1]) - self.spot(axis)) * axis[0]
        return block

    def hop(self, i, part, phase, block, rest, slot, device):
        return send(
            part.of(self.acc[part.array], block),
            self.got[i][phase].at[rest, slot],
            self.send_sem.at[i, phase],
            self.recv_sems[phase].at[i, rest * self.got[i][phase].shape[1] + slot],
            device,
        )

    def take(self, parts, phase, block, rest, slot):
        for i, part in parts:
            self.hop(i, part, phase, block, rest, slot, (self.me, 1 - self.core)).wait_recv()
            acc, got = self.acc[part.array], self.got[i][phase]
            rows = acc.shape[1]
            step = min(rows, 16)
            cols = pl.ds(part.offset, part.width)

            def go(e, acc=acc, got=got, step=step, cols=cols):
                at = pl.ds(pl.multiple_of(e * step, step), step)
                acc[block, at, cols] = acc[block, at, cols] + got[rest, slot, at, :]

            each(rows // step, go)

    def give(self, parts, phase, block, rest, slot, step):
        for i, part in parts:
            self.hop(i, part, phase, block, rest, slot, (self.me + step, self.core)).start()

    def event(self, order, parts, phase, t, turns):
        stride, size = order[phase]
        at = self.spot(order[phase])
        origin = turn(at, t, size)
        mine = t == size - 1
        block = self.block_at(order, phase, origin, turns)
        rest = 0
        for axis, away in zip(order[:phase], turns):
            rest = rest * axis[1] + away
        if size == 1:
            return
        if size == 2:
            pl.when(jnp.logical_not(mine))(
                lambda: self.give(parts, phase, block, rest, 0, (1 - 2 * at) * stride)
            )
            pl.when(mine)(lambda: self.take(parts, phase, block, rest, 0))
            return

        @pl.when(jnp.logical_not(mine))
        def _():
            up = (origin > at).astype(jnp.int32)
            behind = jnp.where(up == 1, at > 0, at < size - 1)
            pl.when(behind)(lambda: self.take(parts, phase, block, rest, origin))
            landing = jnp.where((up == 0) & (origin == at - 1), size, origin)
            self.give(parts, phase, block, rest, landing, (2 * up - 1) * stride)

        @pl.when(mine)
        def _():
            pl.when(at > 0)(lambda: self.take(parts, phase, block, rest, at))
            pl.when(at < size - 1)(lambda: self.take(parts, phase, block, rest, size))

    def lead(self, order, parts, s):
        _, (_, nq), (_, nr) = order
        each((nr - 1) * nq, lambda e: self.event(order, parts, 2, e // nq, (s, e % nq)))

    def later(self, order, parts, s, low, high):
        def go(e):
            self.event(order, parts, 2, order[2][1] - 1, (s, low + e))
            self.event(order, parts, 1, low + e, (s,))

        each(high - low, go)

    def finish(self, order, parts, s):
        self.event(order, parts, 0, s, ())

    def stages(self):
        light, heavy = self.numbered[:2], self.numbered[2:]
        steps, few = heavy[0][0][0][1], max(c[0][0][1] for c in light)
        found = [functools.partial(self.lead, *c, s) for c in heavy[::-1] for s in range(min(AHEAD, steps))]
        found += [functools.partial(self.lead, *colour, 0) for colour in light]
        for s in range(max(steps, few + 1)):
            if s < steps:
                found += [functools.partial(self.later, *colour, s, 0, 1) for colour in heavy]
            if s + AHEAD < steps:
                found += [functools.partial(self.lead, *colour, s + AHEAD) for colour in heavy]
            if 1 <= s < steps:
                found += [functools.partial(self.finish, *colour, s - 1) for colour in heavy]
            found += [functools.partial(self.lead, *c, s + 1) for c in light if s + 1 < c[0][0][1]]
            if s < steps:
                found += [functools.partial(self.later, *c, s, 1, c[0][1][1]) for c in heavy]
            for c in light:
                if 1 <= s <= c[0][0][1]:
                    found += [
                        functools.partial(self.later, *c, s - 1, e, e + 1) for e in range(c[0][1][1])
                    ]
                    found.append(functools.partial(self.finish, *c, s - 1))
            if s == steps - 1:
                found += [functools.partial(self.finish, *colour, s) for colour in heavy]
        return found

    def drain(self):
        for order, parts in self.numbered:
            for i, part in parts:
                for phase in range(3):
                    if order[phase][1] > 1:
                        count = (order[phase][1] - 1) * math.prod([a[1] for a in order[:phase]])
                        many = part.of(self.acc[part.array], pl.ds(0, count))
                        send(
                            many, many, self.send_sem.at[i, phase], self.drain_sem, (self.me, 1 - self.core)
                        ).wait_send()


class Refs:
    pass


def block_kernel(axes, n, cap, *refs):
    names = (
        "wq", "wo", "wu", "wd", "vec", "rows_in", "pick", "extra", "notes", "gq", "go", "gu", "gd", "gs",
        "landed", "new", "Wq", "Wo", "Wu", "Wd", "V", "Wo2", "Aq", "Ao", "Au", "Ad", "As", "As2", "land",
        "rows_out", "X", "DY", "N1", "QKV", "PROBS", "ATT", "PART", "SENT", "GOT1", "GOT2", "GOT3", "GOT4",
        "BA", "N2", "ACT", "GM", "GU", "M1", "GA", "GATT", "GQKV", "GR", "NOTE", "FQ", "FO", "FU", "FD",
    )
    r = Refs()
    for name, ref in zip(names, refs):
        setattr(r, name, ref)
    got_refs, sems = refs[len(names) : -8], refs[-8:]
    g_send, g_recv, g_local, s_send, s_recv0, s_recv1, s_recv2, misc = sems
    R = D // n
    me, core = lax.axis_index("fsdp"), lax.axis_index("rep")
    half = D // 2
    pair = (me, 1 - core)
    units = r.wd.shape[0] // 2
    blocks = [r.Wq, r.Wo, r.Wu, r.Wd, r.V]

    def stage(src, dst, k):
        pltpu.make_async_copy(src, dst, g_local.at[k]).start()

    def column(f, size, start):
        return pl.ds(pl.multiple_of(f * size + start, 128), size)

    for k in range(3):
        stage(r.wq.at[:, pl.ds(pl.multiple_of(k * D + core * half, 128), half)], r.Wq.at[me, :, pl.ds(k * half, half)], 0)
    stage(r.wo.at[:, column(core, half, 0)], r.Wo.at[me], 1)
    each(
        n, lambda f: stage(r.wu.at[:, column(2 * f + core, units, 0)], r.Wu.at[me, :, column(f, units, 0)], 2)
    )
    stage(r.wd.at[pl.ds(pl.multiple_of(core * units, 16), units)], r.Wd.at[me], 3)
    stage(r.vec, r.V.at[me], 4)
    enter(n, me, core)
    for k, whole in enumerate(blocks):
        pltpu.make_async_copy(whole.at[me], whole.at[me], g_local.at[k]).wait()
    counter = [0]

    def to_pair(src, dst):
        k = counter[0]
        counter[0] += 2
        copy = send(src, dst, misc.at[k], misc.at[k + 1], pair)
        copy.start()
        return copy

    numbered = number_parts(first_shares(axes, 128) + second_shares(axes))
    g_sems = (g_send, g_recv)
    gathers = [Gather(n, me, core, part, blocks, g_sems) for part in (numbered[:4], numbered[4:])]
    gathers[0].start()
    row_sems = [misc.at[40 + k] for k in range(6)]
    def spread(items, chunks, low, high):
        done = 0
        for number, item in enumerate(items):
            item()
            want = len(chunks) * (number + 1 - low) // max(high - low, 1) if number + 1 >= low else 0
            while done < min(max(want, 0), len(chunks)):
                chunks[done]()
                done += 1
        for chunk in chunks[done:]:
            chunk()

    own_rows, row_sends = rows_each(n, me, core, r.rows_in, r.land, *row_sems[:3])
    note = to_pair(r.notes, r.NOTE)
    events = gathers[0].events()
    events.insert(len(events) * EARLY // 100, gathers[1].start)
    behind = gathers[1].events()
    late_sends = []
    if ROWS_IN[1] > 100:
        late_sends = row_sends[(n - 1) * 100 // ROWS_IN[1]:]
        row_sends = row_sends[: (n - 1) * 100 // ROWS_IN[1]]
    spread(events, row_sends, len(events) * ROWS_IN[0] // 100, len(events) * min(ROWS_IN[1], 100) // 100)
    for number, chunk in enumerate(late_sends):
        behind.insert(2 * number, chunk)
    mine, theirs = pl.ds(0, CAP), pl.ds(CAP, CAP)
    STEP = 64
    TILE = 256
    flying = Refs()

    def cols(e, size=TILE):
        return pl.ds(pl.multiple_of(e * size, size), size)

    def flat(ref, at):
        return ref[:, :, at].reshape(-1, at.size)

    def vector(v):
        per = 128 // R
        tiles = []
        for t in range(D // 128):
            total = r.V[t * per].astype(jnp.float32)[v : v + 1, :]
            for j in range(1, per):
                total = total + r.V[t * per + j].astype(jnp.float32)[v : v + 1, :]
            tiles.append(total)
        return jnp.concatenate(tiles, axis=1)

    w_router, gain1, gain2 = vector(0), vector(1), vector(2)

    def inverse(v):
        return lax.rsqrt(jnp.mean(v * v, axis=1, keepdims=True) + EPSILON)

    def rows_here():
        rows_wait(n, me, core, r.rows_in, r.land, row_sems[0], row_sems[1], own_rows)
        flying.out_half = to_pair(r.Wo.at[pl.ds((1 - core) * (n // 2), n // 2)], r.Wo2)

    def extract(k, ref):
        def go(e):
            at = pl.ds(k * CAP, CAP)
            ref[:CAP, cols(e)] = (
                mm(r.pick[at, :], r.land[:, :, cols(e)].reshape(-1, TILE)) + r.extra[at, cols(e)].astype(jnp.float32)
            ).astype(jnp.bfloat16)

        each(D // TILE, go)

    def swap_rows():
        flying.both = [to_pair(ref.at[mine], ref.at[theirs]) for ref in (r.X, r.DY)] + [note]

    def first(e):
        at = pl.ds(pl.multiple_of(e * STEP, STEP), STEP)
        x = r.X[at, :].astype(jnp.float32)
        r.N1[at, :] = (x * inverse(x) * gain1).astype(jnp.bfloat16)
        router = jnp.sum(x * w_router, axis=1, keepdims=True)
        r.GM[at, :] = (router * r.DY[at, :].astype(jnp.float32)).astype(jnp.bfloat16)

    def first_rows():
        for copy in flying.both:
            copy.wait()
        each(2 * CAP // STEP, first)

    def project(e):
        r.QKV[:, cols(e)] = mm(r.N1[...], flat(r.Wq, cols(e))).astype(jnp.bfloat16)

    factor = 1.0 / math.sqrt(HEAD_DIM)
    pairs = half // 128
    lane = lax.broadcasted_iota(jnp.int32, (CAP, 128), 1) // HEAD_DIM
    zero = jnp.zeros((CAP, 128), jnp.bfloat16)
    causal = lax.broadcasted_iota(jnp.int32, (CAP, CAP), 1) <= lax.broadcasted_iota(jnp.int32, (CAP, CAP), 0)

    def heads(e):
        s, p = e // pairs, e % pairs
        rows = pl.ds(pl.multiple_of(s * CAP, CAP), CAP)
        q, k, v = (r.QKV[rows, cols(p + j * pairs, 128)] for j in range(3))
        return s, p, rows, q, k, v

    def attend(e):
        s, p, rows, q, k, v = heads(e)
        valid = jnp.where(s == 0, r.notes[0:1, :], r.NOTE[0:1, :]) > 0
        parts = []
        for h in range(2):
            score = mm(jnp.where(lane == h, q, zero), k, NT) * factor
            score = jnp.where(causal & valid, score, -1e30)
            top = jnp.exp(score - jnp.max(score, axis=1, keepdims=True))
            probs = top / jnp.sum(top, axis=1, keepdims=True)
            r.PROBS[2 * e + h] = probs
            parts.append(mm(probs.astype(jnp.bfloat16), v))
        r.ATT[rows, cols(p, 128)] = jnp.where(lane == 0, parts[0], parts[1]).astype(jnp.bfloat16)

    near = pl.ds(pl.multiple_of(core * half, half), half)
    away = pl.ds(pl.multiple_of((1 - core) * half, half), half)
    own_heads = pl.ds(core * (n // 2), n // 2)

    def wo_near():
        return r.Wo[own_heads].reshape(half, half)

    def wo_away():
        return r.Wo2[...].reshape(half, half)

    def project_out(where):
        if where == 0:
            r.BA[:, near] = mm(r.ATT[...], wo_near())
        else:
            flying.out_half.wait()
            r.BA[:, away] = mm(r.ATT[...], wo_away())

    def pass_on(part, got):
        for a, b in ((mine, theirs), (theirs, mine)):
            r.SENT[a, :] = part[b, :].astype(jnp.bfloat16)
        flying.gone = to_pair(r.SENT, got)

    def second(e):
        at = pl.ds(pl.multiple_of(e * STEP, STEP), STEP)
        branch = r.BA[at, :] + r.GOT1[at, :].astype(jnp.float32)
        r.BA[at, :] = branch
        middle = r.X[at, :].astype(jnp.float32) + branch
        r.N2[at, :] = (middle * inverse(middle) * gain2).astype(jnp.bfloat16)

    def second_rows():
        flying.gone.wait()
        each(2 * CAP // STEP, second)

    def some(fn, low, high):
        return lambda: lax.fori_loop(low, high, lambda e, _: (fn(e), 0)[1], 0)

    forward = [rows_here, functools.partial(extract, 0, r.X), functools.partial(extract, 1, r.DY), swap_rows, first_rows]
    forward += [some(project, e, e + 1) for e in range(3 * half // TILE)]
    forward += [some(attend, e, e + 2) for e in range(0, 2 * pairs, 2)]
    forward += [
        functools.partial(project_out, 0), functools.partial(project_out, 1),
        lambda: pass_on(r.BA, r.GOT1), second_rows,
    ]
    spread(behind, forward, len(behind) * AT0 // 100, len(behind) * AT1 // 100)
    hidden = r.Wd.shape[1]
    per = TILE // hidden if hidden < TILE else 1

    def down_rows(e):
        return pl.ds(e * per, per)

    def hidden_units(e):
        up = mm(r.N2[...], flat(r.Wu, cols(e)))
        inner = jnp.tanh(SQRT_2_PI * (up + 0.044715 * up * up * up))
        act = (0.5 * up * (1.0 + inner)).astype(jnp.bfloat16)
        slope = 0.5 * (1.0 + inner) + 0.5 * up * (1.0 - inner * inner) * (
            SQRT_2_PI * (1.0 + 3 * 0.044715 * up * up)
        )
        r.ACT[:, cols(e)] = act
        down = r.Wd[down_rows(e)].reshape(TILE, D)
        grad_act = mm(r.GM[...], down, NT)
        r.GU[:, cols(e)] = (slope * grad_act).astype(jnp.bfloat16)
        r.Ad[down_rows(e)] = mm(act, r.GM[...], TN).astype(jnp.bfloat16).reshape(per, hidden, D)

    tiles = 2 * D // TILE
    each(tiles, hidden_units)

    def up_grads(e):
        r.Au[:, :, cols(e)] = mm(r.N2[...], r.GU[:, cols(e)], TN).astype(jnp.bfloat16).reshape(n, R, TILE)

    total = sum(len(p) for _, p in numbered)
    got = [got_refs[3 * i : 3 * i + 3] for i in range(total)]
    s_sems = (s_send, (s_recv0, s_recv1, s_recv2), misc.at[46])
    acc = [r.Aq, r.Ao, r.Au, r.Ad, r.As]
    late, soon = (Scatter(me, core, part, acc, got, s_sems) for part in (numbered[:4], numbered[4:]))
    many = TILE // R

    def back_up(e):
        block = r.Wu[pl.ds(e * many, many)].reshape(TILE, 2 * D)
        r.PART[:, cols(e)] = mm(r.GU[...], block, NT)

    def mlp(e):
        r.M1[:, cols(e)] = mm(r.ACT[...], r.Wd[:, :, cols(e)].reshape(2 * D, TILE))

    def mlp_out():
        flying.gone.wait()
        r.SENT[mine, :] = r.M1[theirs, :].astype(jnp.bfloat16)
        flying.gone = to_pair(r.SENT.at[mine], r.GOT3)

    zeros = jnp.zeros((1, D), jnp.float32)

    def third(e, total):
        at = pl.ds(pl.multiple_of(e * STEP, STEP), STEP)
        x = r.X[at, :].astype(jnp.float32)
        dy = r.DY[at, :].astype(jnp.float32)
        middle = x + r.BA[at, :]
        inv = inverse(middle)
        grad = r.PART[at, :] + r.GOT2[at, :].astype(jnp.float32)
        scaled = gain2 * grad
        grad_middle = inv * scaled - middle * inv**3 * jnp.mean(scaled * middle, axis=1, keepdims=True)
        router = jnp.sum(x * w_router, axis=1, keepdims=True)
        r.GA[at, :] = (router * dy + grad_middle).astype(jnp.bfloat16)
        r.PART[at, :] = grad_middle
        counted = jnp.where(e < CAP // STEP, 1.0, 0.0)
        return total + counted * jnp.sum(grad * middle * inv, axis=0, keepdims=True)

    def third_rows():
        flying.gain2 = lax.fori_loop(0, 2 * CAP // STEP, third, zeros)

    def out_grads():
        r.Ao[own_heads] = mm(r.ATT[...], r.GA[:, near], TN).astype(jnp.bfloat16).reshape(n // 2, R, half)

    def attended_grads():
        r.GATT[...] = (mm(r.GA[:, near], wo_near(), NT) + mm(r.GA[:, away], wo_away(), NT)).astype(jnp.bfloat16)

    def other_out_grads():
        flying.gone.wait()
        r.Wo2[...] = mm(r.ATT[...], r.GA[:, away], TN).astype(jnp.bfloat16).reshape(n // 2, R, half)
        flying.out = to_pair(r.Wo2, r.Ao.at[own_heads])

    def attend_back(e):
        s, p, rows, q, k, v = heads(e)
        grad = r.GATT[rows, cols(p, 128)]
        gq, gk, gv = [], [], []
        for h in range(2):
            grad_h, q_h = jnp.where(lane == h, grad, zero), jnp.where(lane == h, q, zero)
            probs = r.PROBS[2 * e + h]
            grad_probs = mm(grad_h, v, NT)
            gv.append(mm(probs.astype(jnp.bfloat16), grad_h, TN))
            grad_scores = probs * (grad_probs - jnp.sum(probs * grad_probs, axis=1, keepdims=True))
            grad_scores = grad_scores.astype(jnp.bfloat16)
            gq.append(mm(grad_scores, k))
            gk.append(mm(grad_scores, q_h, TN))
        r.GQKV[rows, cols(p, 128)] = (jnp.where(lane == 0, gq[0], gq[1]) * factor).astype(jnp.bfloat16)
        r.GQKV[rows, cols(p + pairs, 128)] = ((gk[0] + gk[1]) * factor).astype(jnp.bfloat16)
        r.GQKV[rows, cols(p + 2 * pairs, 128)] = (gv[0] + gv[1]).astype(jnp.bfloat16)

    def qkv_grads(e):
        r.Aq[:, :, cols(e)] = mm(r.N1[...], r.GQKV[:, cols(e)], TN).astype(jnp.bfloat16).reshape(n, R, TILE)

    def back_qkv(e):
        block = r.Wq[pl.ds(e * many, many)].reshape(TILE, 3 * half)
        r.M1[:, cols(e)] = mm(r.GQKV[...], block, NT)

    def fourth(e, total):
        at = pl.ds(pl.multiple_of(e * STEP, STEP), STEP)
        x = r.X[at, :].astype(jnp.float32)
        dy = r.DY[at, :].astype(jnp.float32)
        combined = r.BA[at, :] + r.M1[at, :] + r.GOT3[at, :].astype(jnp.float32)
        router = jnp.sum(x * w_router, axis=1, keepdims=True)
        r.new[at, :] = (x + router * combined).astype(jnp.bfloat16)
        grad_router = jnp.sum(dy * combined, axis=1, keepdims=True)
        r.GR[at, :] = dy + grad_router * w_router + r.PART[at, :]
        return total + jnp.sum(grad_router * x, axis=0, keepdims=True)

    def fourth_rows():
        flying.router = lax.fori_loop(0, CAP // STEP, fourth, zeros)

    def last_out():
        r.SENT[theirs, :] = r.M1[theirs, :].astype(jnp.bfloat16)
        flying.gone = to_pair(r.SENT.at[theirs], r.GOT4)

    def fifth(e, total):
        at = pl.ds(pl.multiple_of(e * STEP, STEP), STEP)
        x = r.X[at, :].astype(jnp.float32)
        grad = r.M1[at, :] + r.GOT4[at, :].astype(jnp.float32)
        inv = inverse(x)
        scaled = gain1 * grad
        grad_x = inv * scaled - x * inv**3 * jnp.mean(scaled * x, axis=1, keepdims=True)
        below = pl.ds(pl.multiple_of(CAP + e * STEP, STEP), STEP)
        r.new[below, :] = (r.GR[at, :] + grad_x).astype(jnp.bfloat16)
        return total + jnp.sum(grad * x * inv, axis=0, keepdims=True)

    def fifth_rows():
        flying.gone.wait()
        gain1_grad = lax.fori_loop(0, CAP // STEP, fifth, zeros)
        small = jnp.concatenate([flying.router, gain1_grad, flying.gain2, jnp.zeros((5, D), jnp.float32)], axis=0)
        for block in range(n):
            tile = block * R // 128
            r.As[block] = small[:, tile * 128 : tile * 128 + 128]
        flying.small = to_pair(r.As, r.As2)

    def place(e):
        sent = mm(r.pick[...], r.new[:, cols(e)], TN).astype(jnp.bfloat16)
        r.rows_out[:, :, cols(e)] = sent.reshape(n, -1, TILE)

    def send_late():
        flying.rows, flying.sends = rows_each(n, me, core, r.rows_out, r.landed, *row_sems[3:])
        flying.small.wait()
        flying.out.wait()
        r.As[...] = r.As[...] + r.As2[...]

    backward = [some(up_grads, e, e + 2) for e in range(0, tiles, 2)] if SPLIT else []
    backward += [some(back_up, e, e + 1) for e in range(D // TILE)]
    backward += [lambda: pass_on(r.PART, r.GOT2)]
    backward += [some(mlp, e, e + 1) for e in range(D // TILE)]
    backward += [mlp_out, third_rows, out_grads, attended_grads, other_out_grads]
    backward += [some(attend_back, e, e + 1) for e in range(2 * pairs)]
    backward += [fourth_rows]
    backward += [some(back_qkv, e, e + 1) for e in range(D // TILE)]
    backward += [last_out]
    backward += [some(qkv_grads, e, e + 1) for e in range(3 * half // TILE)]
    backward += [fifth_rows, some(place, 0, D // TILE), send_late]
    stages = soon.stages()
    for stage in stages[:AHEAD]:
        stage()
    each(tiles, up_grads)
    stages = stages[AHEAD:]
    cut = len(stages) * CUT // 100
    spread(stages[:cut], backward, 1, cut)
    rest, more = stages[cut:], late.stages()
    for number, chunk in enumerate(flying.sends):
        more.insert((number + 1) * ROWS_OUT - 1 if ROWS_OUT else 0, chunk)
    while rest or more:
        if more:
            more.pop(0)()
        if rest:
            rest.pop(0)()
    for gather in gathers:
        gather.drain()
    final = [to_pair(acc[k].at[me], ref) for k, ref in enumerate((r.FQ, r.FO, r.FU, r.FD))]

    def give(k, side, ref):
        value = ref[...]
        if k == 0:
            for j in range(3):
                r.gq[:, pl.ds(pl.multiple_of(j * D + side * half, 128), half)] = value[:, j * half : (j + 1) * half]
        elif k == 1:
            r.go[:, column(side, half, 0)] = value
        elif k == 2:
            for f in range(n):
                r.gu[:, column(2 * f + side, units, 0)] = value[:, f * units : (f + 1) * units]
        else:
            r.gd[pl.ds(pl.multiple_of(side * units, 16), units), :] = value

    for k in range(4):
        give(k, core, acc[k].at[me])
    r.gs[...] = r.As[me]
    for k, ref in enumerate((r.FQ, r.FO, r.FU, r.FD)):
        final[k].wait()
        give(k, 1 - core, ref)
    rows_wait(n, me, core, r.rows_out, r.landed, row_sems[3], row_sems[4], flying.rows)
    late.drain()
    soon.drain()


def whole_block(axes, n, cap, weights, vec, rows_in, pick, extra, notes):
    plan = first_shares(axes, 128) + second_shares(axes)
    bf, f32 = jnp.bfloat16, jnp.float32
    shards = weights
    weights = [
        jax.ShapeDtypeStruct((w.shape[0] // (2 if k == 3 else 1), w.shape[1] // (1 if k == 3 else 2)), bf)
        for k, w in enumerate(shards)
    ]
    R, F = weights[0].shape[0], weights[3].shape[0]
    vmem = pl.BlockSpec(memory_space=pltpu.VMEM)
    anywhere = pl.BlockSpec(memory_space=ANY)
    out = [jax.ShapeDtypeStruct(w.shape, bf) for w in shards]
    out += [
        jax.ShapeDtypeStruct((8, 128), f32),
        jax.ShapeDtypeStruct(rows_in.shape, bf),
        jax.ShapeDtypeStruct((2 * CAP, D), bf),
    ]
    rows = 2 * CAP
    half = D // 2
    V = pltpu.VMEM
    scratch = [V((n,) + w.shape, bf) for w in weights]
    scratch += [V((n,) + vec.shape, bf), V((n // 2, R, half), bf)]
    scratch += [V((n,) + w.shape, bf) for w in weights]
    scratch += [V((n, 8, 128), f32)] * 2
    scratch += [V((n, 2 * cap, D), bf), V((n, 2 * cap, D), bf)]
    scratch += [V((rows, D), bf)] * 3
    scratch += [V((rows, 3 * half), bf), V((HEADS, CAP, CAP), f32), V((rows, half), bf)]
    scratch += [V((rows, D), f32), V((rows, D), bf), V((rows, D), bf), V((rows, D), bf), V((CAP, D), bf), V((CAP, D), bf)]
    scratch += [V((rows, D), f32), V((rows, D), bf)]
    scratch += [V((rows, 2 * D), bf), V((rows, D), bf), V((rows, 2 * D), bf)]
    scratch += [V((rows, D), f32), V((rows, D), bf), V((rows, half), bf), V((rows, 3 * half), bf)]
    scratch += [V((CAP, D), f32), V((8, 128), f32)]
    scratch += [V(w.shape, bf) for w in weights]
    most = [1, 1, 1]
    total = 0
    deep = [R, R, R, F, 8]
    for order, parts in plan:
        total += len(parts)
        for p in parts:
            count = 1
            for phase in range(3):
                size = order[phase][1]
                kind = f32 if p.array == 4 else bf
                scratch.append(V((count, slots(size), deep[p.array], p.width), kind))
                most[phase] = max(most[phase], count * slots(size))
                count *= size
    dma = pltpu.SemaphoreType.DMA
    scratch += [dma((total, 3, 2)), dma((total, n)), dma((5,)), dma((total, 3))]
    scratch += [dma((total, m)) for m in most]
    scratch += [dma((48,))]
    return pl.pallas_call(
        functools.partial(block_kernel, axes, n, cap),
        out_shape=out,
        in_specs=[anywhere] * 6 + [vmem] * 3,
        out_specs=[vmem] * 5 + [anywhere, vmem],
        scratch_shapes=scratch,
        compiler_params=pltpu.CompilerParams(
            collective_id=2, has_side_effects=True, vmem_limit_bytes=67043328
        ),
        name="whole_block",
    )(*shards, vec, rows_in, pick, extra, notes)


def normalize(values, gain):
    inverse = lax.rsqrt(jnp.mean(values * values, axis=-1, keepdims=True) + EPSILON)
    return (values * inverse * gain, inverse)


def rms_back(values, inverse, gain, grad_normed):
    scaled = gain * grad_normed
    grad_values = inverse * scaled - values * inverse**3 * jnp.mean(
        scaled * values, axis=-1, keepdims=True
    )
    grad_gain = jnp.sum(grad_normed * values * inverse, axis=(0, 1))
    return (grad_values, grad_gain)


def split_heads(packed, offset):
    return packed[..., offset : offset + D].reshape(packed.shape[:2] + (HEADS, HEAD_DIM))


def narrow_body(
    axes,
    tokens,
    cotangent,
    w_qkv,
    w_out,
    w_up,
    w_down,
    w_router,
    gain_attn,
    gain_mlp,
    lengths,
    routed,
    dealing,
):
    factor = 1.0 / math.sqrt(HEAD_DIM)
    shards, place = lax.axis_size("fsdp"), lax.axis_index("fsdp")
    group_seqs, width = tokens.shape[1], tokens.shape[2]
    cap = min(24, width)
    slot_ids = jnp.arange(CAP, dtype=jnp.int32)
    picker = dealing[0][:, None] == jnp.arange(group_seqs, dtype=jnp.int32)[None, :]
    row_lengths = jnp.sum(jnp.where(picker, lengths[0][None, :], 0), axis=1)
    row_routes = jnp.sum(jnp.where(picker[:, :, None], routed[0][None, :, :], 0), axis=1)
    row_routes = jnp.where(slot_ids[None, :] < (row_lengths // 8)[:, None], row_routes, PAST)
    here = place * width + jnp.arange(width, dtype=jnp.int32)
    below = jnp.sum((row_routes[:, :, None] < here[None, None, :]).astype(jnp.int32), axis=1)
    upto = jnp.sum((row_routes[:, :, None] <= here[None, None, :]).astype(jnp.int32), axis=1)
    touched = upto > below
    living = here[None, :] < row_lengths[:, None]
    rank = jnp.where(touched, below - below[:, :1], -1)
    select = (rank[:, None, :] == jnp.arange(cap, dtype=jnp.int32)[None, :, None]).astype(jnp.bfloat16)
    shard_of = row_routes // width
    crowd = jnp.sum(
        (shard_of[:, :, None] == jnp.arange(shards, dtype=jnp.int32)[None, None, :]).astype(jnp.int32), axis=1
    )
    flag = jnp.broadcast_to((jnp.max(crowd) > cap).astype(jnp.float32), (8, 128))
    packed_rows = jnp.concatenate(
        [
            jnp.einsum("jip,jpd->jid", select, t[0], preferred_element_type=jnp.float32).astype(jnp.bfloat16)
            for t in (tokens, cotangent)
        ],
        axis=1,
    )
    seq_lengths = lax.dynamic_slice_in_dim(row_lengths, place, 1)
    routes = lax.dynamic_slice_in_dim(row_routes, place, 1)[0]
    valid_slot = slot_ids[None, :] < (seq_lengths // 8)[:, None]
    seq_shard = routes // width
    seq_rank = slot_ids - jnp.sum((routes[None, :] < (seq_shard * width)[:, None]).astype(jnp.int32), axis=1)
    fits = valid_slot[0] & (seq_rank < cap)
    landing = jnp.where(fits, seq_shard * (2 * cap) + seq_rank, -1)
    cells = jnp.arange(shards * 2 * cap, dtype=jnp.int32)
    pick = jnp.concatenate([landing[:, None] == cells[None, :], (landing[:, None] == (cells - cap)[None, :]) & fits[:, None]])
    pick = pick.astype(jnp.bfloat16)
    part = w_router.shape[0]
    vectors = jnp.pad(jnp.stack([w_router, gain_attn, gain_mlp]), ((0, 13), (0, 128 - part)))
    blocks = gather_all(axes, shards, [w_qkv, w_out, w_up, w_down, vectors], packed_rows, flag, 0)
    crowded = jnp.maximum(flag, blocks[6])[0, 0] > 0
    got_rows = jnp.einsum(
        "cs,sd->cd", pick, blocks[5].reshape(-1, D), preferred_element_type=jnp.float32
    ).astype(jnp.bfloat16)

    def all_rows(got):
        positions = jnp.arange(SEQ_MAX, dtype=jnp.int32)
        onehot = (routes[:, None] == positions[None, :]).astype(jnp.bfloat16)
        return jnp.concatenate(
            [
                jnp.dot(
                    onehot,
                    lax.all_to_all(t, "fsdp", split_axis=1, concat_axis=2, tiled=True)[0, 0],
                    preferred_element_type=jnp.float32,
                ).astype(jnp.bfloat16)
                for t in (tokens, cotangent)
            ]
        )

    if cap < width:
        got_rows = lax.cond(crowded, all_rows, lambda got: got, got_rows)
    rows_low = got_rows[None, :CAP]
    incoming_rows = rows_low.astype(jnp.float32)
    row_gradient = got_rows[None, CAP:].astype(jnp.float32)
    small = blocks[4][:, :3, :part].transpose(1, 0, 2).reshape(3, D)
    gathered = tuple(b.reshape(-1, b.shape[2]) for b in blocks[:4]) + (small[0], small[1], small[2])
    router_val = jnp.einsum("scd,d->sc", rows_low, gathered[4], preferred_element_type=jnp.float32)
    normed_attn, inverse_attn = normalize(incoming_rows, gathered[5].astype(jnp.float32))
    normed_low = normed_attn.astype(jnp.bfloat16)
    packed = jnp.einsum(
        "scd,de->sce", normed_low, gathered[0], preferred_element_type=jnp.float32
    ).astype(jnp.bfloat16)
    queries = split_heads(packed, 0)
    keys_heads = split_heads(packed, D)
    values_heads = split_heads(packed, 2 * D)
    scores = (
        jnp.einsum("sqhe,skhe->shqk", queries, keys_heads, preferred_element_type=jnp.float32)
        * factor
    )
    allowed = (slot_ids[None, :] <= slot_ids[:, None])[None, None] & valid_slot[:, None, None, :]
    scores = jnp.where(allowed, scores, -1e30)
    probs = jax.nn.softmax(scores, axis=-1)
    probs_low = probs.astype(jnp.bfloat16)
    attended = jnp.einsum(
        "shqk,skhe->sqhe", probs_low, values_heads, preferred_element_type=jnp.float32
    ).astype(jnp.bfloat16)
    attended = attended.reshape(incoming_rows.shape)
    branch_attn = jnp.einsum(
        "sce,ed->scd", attended, gathered[1], preferred_element_type=jnp.float32
    )
    middle = incoming_rows + branch_attn
    normed_mid, inverse_mid = normalize(middle, gathered[6].astype(jnp.float32))
    normed_mid_low = normed_mid.astype(jnp.bfloat16)
    upward = jnp.einsum(
        "scd,df->scf", normed_mid_low, gathered[2], preferred_element_type=jnp.float32
    )
    activated = jax.nn.gelu(upward).astype(jnp.bfloat16)
    branch_mlp = jnp.einsum(
        "scf,fd->scd", activated, gathered[3], preferred_element_type=jnp.float32
    )
    combined = branch_attn + branch_mlp
    refreshed_rows = (incoming_rows + router_val[..., None] * combined).astype(jnp.bfloat16)
    back_weights = gathered
    grad_comb = router_val[..., None] * row_gradient
    grad_router_val = jnp.sum(row_gradient * combined, axis=-1)
    total_gradient = row_gradient + grad_router_val[..., None] * back_weights[4].astype(jnp.float32)
    grad_mlp_low = grad_comb.astype(jnp.bfloat16)
    grad_act = jnp.einsum(
        "scd,fd->scf", grad_mlp_low, back_weights[3], preferred_element_type=jnp.float32
    )
    grad_downw = jnp.einsum(
        "scf,scd->fd", activated, grad_mlp_low, preferred_element_type=jnp.float32
    )
    unused, gelu_pull = jax.vjp(jax.nn.gelu, upward)
    grad_up_low = gelu_pull(grad_act)[0].astype(jnp.bfloat16)
    grad_normed_mid = jnp.einsum(
        "scf,df->scd", grad_up_low, back_weights[2], preferred_element_type=jnp.float32
    )
    grad_upw = jnp.einsum(
        "scd,scf->df", normed_mid_low, grad_up_low, preferred_element_type=jnp.float32
    )
    grad_middle, grad_gain_second = rms_back(
        middle, inverse_mid, back_weights[6].astype(jnp.float32), grad_normed_mid
    )
    grad_attn_low = (grad_comb + grad_middle).astype(jnp.bfloat16)
    total_gradient = total_gradient + grad_middle
    grad_attended = jnp.einsum(
        "scd,ed->sce", grad_attn_low, back_weights[1], preferred_element_type=jnp.float32
    ).astype(jnp.bfloat16)
    grad_outw = jnp.einsum(
        "sce,scd->ed", attended, grad_attn_low, preferred_element_type=jnp.float32
    )
    grad_att_heads = grad_attended.reshape(queries.shape)
    grad_probs = jnp.einsum(
        "sqhe,skhe->shqk", grad_att_heads, values_heads, preferred_element_type=jnp.float32
    )
    grad_values = jnp.einsum(
        "shqk,sqhe->skhe", probs_low, grad_att_heads, preferred_element_type=jnp.float32
    )
    grad_scores = probs * (grad_probs - jnp.sum(probs * grad_probs, axis=-1, keepdims=True))
    grad_scores_low = grad_scores.astype(jnp.bfloat16)
    grad_queries = (
        jnp.einsum(
            "shqk,skhe->sqhe", grad_scores_low, keys_heads, preferred_element_type=jnp.float32
        )
        * factor
    )
    grad_keys = (
        jnp.einsum("shqk,sqhe->skhe", grad_scores_low, queries, preferred_element_type=jnp.float32)
        * factor
    )
    flat_shape = incoming_rows.shape
    grad_packed = jnp.concatenate(
        [
            grad_queries.reshape(flat_shape),
            grad_keys.reshape(flat_shape),
            grad_values.reshape(flat_shape),
        ],
        axis=-1,
    ).astype(jnp.bfloat16)
    grad_qkvw = jnp.einsum(
        "scd,sce->de", normed_low, grad_packed, preferred_element_type=jnp.float32
    )
    grad_normed_attn = jnp.einsum(
        "sce,de->scd", grad_packed, back_weights[0], preferred_element_type=jnp.float32
    )
    grad_first_rows, grad_gain_first = rms_back(
        incoming_rows, inverse_attn, back_weights[5].astype(jnp.float32), grad_normed_attn
    )
    total_gradient = total_gradient + grad_first_rows
    grad_routerw = jnp.einsum(
        "scd,sc->d", incoming_rows, grad_router_val, precision=EXACT_PRECISION
    )
    new_rows = jnp.concatenate([refreshed_rows[0], total_gradient[0].astype(jnp.bfloat16)])
    sent_rows = (
        jnp.einsum("cs,cd->sd", pick, new_rows, preferred_element_type=jnp.float32)
        .astype(jnp.bfloat16)
        .reshape(shards, 2 * cap, D)
    )
    small_grads = jnp.stack([grad_routerw, grad_gain_first, grad_gain_second])
    small_grads = small_grads.reshape(3, shards, part).transpose(1, 0, 2)
    small_grads = jnp.pad(small_grads, ((0, 0), (0, 5), (0, 128 - part)))
    partial = [
        g.astype(jnp.bfloat16).reshape(shards, -1, g.shape[1])
        for g in (grad_qkvw, grad_outw, grad_upw, grad_downw)
    ]
    shares = scatter_all(axes, shards, partial + [small_grads], sent_rows, 1)
    totals = tuple(t.astype(jnp.float32) for t in shares[:4]) + tuple(shares[4][j, :part] for j in range(3))
    def place_rows(rows, held):
        spread = jnp.einsum("jip,jid->jpd", select, rows, preferred_element_type=jnp.float32).astype(jnp.bfloat16)
        kept = jnp.where(touched[..., None], spread, held[0])
        return jnp.where(living[..., None], kept, jnp.zeros_like(kept))[None]

    def compact(landed, rows):
        return place_rows(landed[:, :cap], tokens), place_rows(landed[:, cap:], cotangent)

    def entire(landed, rows):
        positions = jnp.arange(SEQ_MAX, dtype=jnp.int32)
        onehot = (routes[:, None] == positions[None, :]).astype(jnp.bfloat16)
        placed = []
        for r, held in ((rows[:CAP], tokens), (rows[CAP:], cotangent)):
            spread = jnp.einsum("cp,cd->pd", onehot, r, preferred_element_type=jnp.float32)
            spread = lax.all_to_all(
                spread.astype(jnp.bfloat16)[None, None], "fsdp", split_axis=2, concat_axis=1, tiled=True
            )
            kept = jnp.where(touched[..., None], spread[0], held[0])
            placed.append(jnp.where(living[..., None], kept, jnp.zeros_like(kept))[None])
        return tuple(placed)

    if cap < width:
        back_out, back_grad = lax.cond(crowded, entire, compact, shares[5], new_rows)
    else:
        back_out, back_grad = compact(shares[5], new_rows)
    return (
        back_out,
        back_grad,
        totals[0],
        totals[1],
        totals[2],
        totals[3],
        totals[4],
        totals[5],
        totals[6],
    )


def wide_body(
    axes,
    tokens,
    cotangent,
    w_qkv,
    w_out,
    w_up,
    w_down,
    w_router,
    gain_attn,
    gain_mlp,
    lengths,
    routed,
    dealing,
):
    factor = 1.0 / math.sqrt(HEAD_DIM)
    shards, place = lax.axis_size("fsdp"), lax.axis_index("fsdp")
    group_seqs, width = tokens.shape[1], tokens.shape[2]
    cap = min(24, width)
    slot_ids = jnp.arange(CAP, dtype=jnp.int32)
    picker = dealing[0][:, None] == jnp.arange(group_seqs, dtype=jnp.int32)[None, :]
    row_lengths = jnp.sum(jnp.where(picker, lengths[0][None, :], 0), axis=1)
    row_routes = jnp.sum(jnp.where(picker[:, :, None], routed[0][None, :, :], 0), axis=1)
    row_routes = jnp.where(slot_ids[None, :] < (row_lengths // 8)[:, None], row_routes, PAST)
    here = place * width + jnp.arange(width, dtype=jnp.int32)
    below = jnp.sum((row_routes[:, :, None] < here[None, None, :]).astype(jnp.int32), axis=1)
    upto = jnp.sum((row_routes[:, :, None] <= here[None, None, :]).astype(jnp.int32), axis=1)
    touched = upto > below
    living = here[None, :] < row_lengths[:, None]
    rank = jnp.where(touched, below - below[:, :1], -1)
    select = (rank[:, None, :] == jnp.arange(cap, dtype=jnp.int32)[None, :, None]).astype(jnp.bfloat16)
    shard_of = row_routes // width
    crowd = jnp.sum(
        (shard_of[:, :, None] == jnp.arange(shards, dtype=jnp.int32)[None, None, :]).astype(jnp.int32), axis=1
    )
    flag = jnp.broadcast_to((jnp.max(crowd) > cap).astype(jnp.float32), (8, 128))
    packed_rows = jnp.concatenate(
        [
            jnp.einsum("jip,jpd->jid", select, t[0], preferred_element_type=jnp.float32).astype(jnp.bfloat16)
            for t in (tokens, cotangent)
        ],
        axis=1,
    )
    seq_lengths = lax.dynamic_slice_in_dim(row_lengths, place, 1)
    routes = lax.dynamic_slice_in_dim(row_routes, place, 1)[0]
    valid_slot = slot_ids[None, :] < (seq_lengths // 8)[:, None]
    seq_shard = routes // width
    seq_rank = slot_ids - jnp.sum((routes[None, :] < (seq_shard * width)[:, None]).astype(jnp.int32), axis=1)
    fits = valid_slot[0] & (seq_rank < cap)
    landing = jnp.where(fits, seq_shard * (2 * cap) + seq_rank, -1)
    cells = jnp.arange(shards * 2 * cap, dtype=jnp.int32)
    pick = jnp.concatenate([landing[:, None] == cells[None, :], (landing[:, None] == (cells - cap)[None, :]) & fits[:, None]])
    pick = pick.astype(jnp.bfloat16)
    part = w_router.shape[0]
    mine = jnp.max(flag)
    other = lax.ppermute(flag, "rep", [(0, 1), (1, 0)])
    crowded = jnp.maximum(mine, jnp.max(other)) > 0
    ring = [(i, (i + 1) % shards) for i in range(shards)]

    def chosen(j):
        return (lax.dynamic_index_in_dim(row_routes, j, 0, keepdims=False)[:, None] == here[None, :]).astype(jnp.bfloat16)

    def all_rows():
        def go(i, rows):
            j = (place - 1 - i) % shards
            mine = [
                jnp.dot(chosen(j), lax.dynamic_index_in_dim(t[0], j, 0, keepdims=False), preferred_element_type=jnp.float32)
                for t in (tokens, cotangent)
            ]
            return lax.ppermute(rows, "fsdp", ring) + jnp.concatenate(mine).astype(jnp.bfloat16)

        return lax.fori_loop(0, shards, go, jnp.zeros((2 * CAP, D), jnp.bfloat16))

    extra = jnp.zeros((2 * CAP, D), jnp.bfloat16)
    if cap < width:
        extra = lax.cond(crowded, all_rows, lambda: jnp.zeros((2 * CAP, D), jnp.bfloat16))
        pick = jnp.where(crowded, jnp.zeros_like(pick), pick)
    weights = [w_qkv, w_out, w_up, w_down]
    lanes = (place * part) % 128
    vectors = jnp.pad(jnp.stack([w_router, gain_attn, gain_mlp]), ((0, 13), (0, 0)))
    vectors = lax.dynamic_update_slice(jnp.zeros((16, 128), jnp.bfloat16), vectors, (0, lanes))
    notes = jnp.broadcast_to(valid_slot.astype(jnp.float32), (8, CAP))
    gq, go, gu, gd, gs, landed, new_rows = whole_block(
        axes, shards, cap, weights, vectors, packed_rows, pick, extra, notes
    )
    small = lax.dynamic_slice(gs, (0, lanes), (8, part))
    gq, go, gu, gd = (g.astype(jnp.float32) for g in (gq, go, gu, gd))
    totals = (gq, go, gu, gd, small[0], small[1], small[2])

    def place_rows(rows, held):
        spread = jnp.einsum("jip,jid->jpd", select, rows, preferred_element_type=jnp.float32).astype(jnp.bfloat16)
        kept = jnp.where(touched[..., None], spread, held[0])
        return jnp.where(living[..., None], kept, jnp.zeros_like(kept))[None]

    def compact(landed, rows):
        return place_rows(landed[:, :cap], tokens), place_rows(landed[:, cap:], cotangent)

    def entire(landed, rows):
        def go(i, held):
            rows, placed = held
            j = (place - i) % shards
            done = []
            for k, (t, whole) in enumerate(zip((tokens, cotangent), placed)):
                spread = jnp.einsum(
                    "cp,cd->pd", chosen(j), rows[k * CAP : k * CAP + CAP], preferred_element_type=jnp.float32
                ).astype(jnp.bfloat16)
                kept = jnp.where(lax.dynamic_index_in_dim(touched, j, 0, keepdims=False)[:, None], spread, t[0, j])
                kept = jnp.where(lax.dynamic_index_in_dim(living, j, 0, keepdims=False)[:, None], kept, jnp.zeros_like(kept))
                done.append(lax.dynamic_update_slice(whole, kept[None, None], (0, j, 0, 0)))
            return lax.ppermute(rows, "fsdp", ring), tuple(done)

        return lax.fori_loop(0, shards, go, (rows, (jnp.zeros_like(tokens), jnp.zeros_like(cotangent))))[1]

    if cap < width:
        back_out, back_grad = lax.cond(crowded, entire, compact, landed, new_rows)
    else:
        back_out, back_grad = compact(landed, new_rows)
    return (
        back_out,
        back_grad,
        totals[0],
        totals[1],
        totals[2],
        totals[3],
        totals[4],
        totals[5],
        totals[6],
    )


def body(axes, *arrays):
    run = wide_body if arrays[2].shape[0] % 16 == 0 else narrow_body
    return run(axes, *arrays)


def solution(mesh):
    placed = (
        P("rep", None, "fsdp", None),
        P("rep", None, "fsdp", None),
        P("fsdp", None),
        P("fsdp", None),
        P("fsdp", None),
        P("fsdp", None),
        P("fsdp"),
        P("fsdp"),
        P("fsdp"),
        P("rep", None),
        P("rep", None, None),
        P("rep", None),
    )
    return jax.shard_map(
        functools.partial(body, grid_axes(mesh)),
        mesh=mesh,
        in_specs=placed,
        out_specs=(
            P("rep", None, "fsdp", None),
            P("rep", None, "fsdp", None),
            P("fsdp", None),
            P("fsdp", None),
            P("fsdp", None),
            P("fsdp", None),
            P("fsdp"),
            P("fsdp"),
            P("fsdp"),
        ),
        check_vma=False,
    )
```

```python
import math
import functools

import jax
import jax.numpy as jnp
from jax import lax
from jax.experimental import pallas as pl
from jax.experimental.pallas import tpu as pltpu
from jax.sharding import PartitionSpec as P

D = 1024
HEADS = 16
HEAD_DIM = 64
SEQ_MAX = 1024
CAP = 128
PAST = 1 << 24


EPSILON = 1e-06
EXACT_PRECISION = lax.Precision.HIGHEST

MESH = pl.DeviceIdType.MESH
ANY = pl.ANY


def grid_axes(mesh):
    devices = mesh.devices[:, 0]
    count = len(devices)
    axes = []
    spots = [getattr(d, "coords", None) for d in devices]
    if all(s is not None for s in spots) and len(set(map(tuple, spots))) == count:
        low = [min(s[k] for s in spots) for k in range(3)]
        at = {tuple(s[k] - low[k] for k in range(3)): f for f, s in enumerate(spots)}
        for k in range(3):
            size = max(s[k] for s in spots) - low[k] + 1
            one = tuple(int(j == k) for j in range(3))
            axes.append((at[one] if size > 1 else 1, size, k))
        ok = all(
            f == sum(stride * spot[k] for stride, _, k in axes) for spot, f in at.items()
        )
        axes = [a[:2] for a in axes] if ok else []
    if not axes:
        axes, left = [], count
        for size in (2, 2):
            size = size if left % size == 0 and left > 1 else 1
            axes.append((count // left, size))
            left //= size
        axes.append((count // left, left))
    return sorted(axes, key=lambda a: -a[1])


def xor(a, b, size):
    out, bit = 0, 1
    while bit < size:
        out = out + ((a // bit + b // bit) % 2) * bit
        bit *= 2
    return out


class Piece:
    def __init__(self, array, half, offset, width):
        self.array, self.half, self.offset, self.width = array, half, offset, width

    def cols(self, core):
        start = self.offset
        if self.half:
            start = core * self.half + start
            start = pl.multiple_of(start, 128)
        return pl.ds(start, self.width)


def colours(axes, widths):
    qkv, out, up, down = (w // 2 for w in widths[:4])
    a, b, c = axes
    third = qkv // 3
    return [
        ((b, c, a), [Piece(1, out, 0, out), Piece(4, 0, 0, widths[4])]),
        ((c, b, a), [Piece(0, qkv, 0, third)]),
        ((a, b, c), [Piece(2, up, 0, up), Piece(0, qkv, third, third)]),
        ((a, c, b), [Piece(3, down, 0, down), Piece(0, qkv, 2 * third, third)]),
    ]


def enter(n, me, core):
    barrier = pltpu.get_barrier_semaphore()

    def hello(i, _):
        pl.semaphore_signal(barrier, inc=1, device_id=((me + i) % n, core), device_id_type=MESH)
        return 0

    lax.fori_loop(1, n, hello, 0)
    pl.semaphore_signal(barrier, inc=1, device_id=(me, 1 - core), device_id_type=MESH)
    pl.semaphore_wait(barrier, n)


def rows_out(n, me, core, rows, landing, send_sem, recv_sem, own_sem):
    own = pltpu.make_async_copy(rows.at[me], landing.at[me], own_sem)
    own.start()

    def go(i, _):
        to = (me + i) % n
        pltpu.make_async_remote_copy(
            src_ref=rows.at[to], dst_ref=landing.at[me], send_sem=send_sem, recv_sem=recv_sem,
            device_id=(to, core), device_id_type=MESH,
        ).start()
        return 0

    lax.fori_loop(1, n, go, 0)
    return own


def rows_each(n, me, core, rows, landing, send_sem, recv_sem, own_sem):
    own = pltpu.make_async_copy(rows.at[me], landing.at[me], own_sem)
    own.start()

    def go(i):
        to = (me + i) % n
        pltpu.make_async_remote_copy(
            src_ref=rows.at[to], dst_ref=landing.at[me], send_sem=send_sem, recv_sem=recv_sem,
            device_id=(to, core), device_id_type=MESH,
        ).start()

    return own, [functools.partial(go, i) for i in (ORDER or range(1, n))]


def rows_wait(n, me, core, rows, landing, send_sem, recv_sem, own):
    own.wait()
    for which in range(2):
        copy = pltpu.make_async_remote_copy(
            src_ref=rows.at[pl.ds(0, n - 1)], dst_ref=landing.at[pl.ds(0, n - 1)],
            send_sem=send_sem, recv_sem=recv_sem, device_id=(me, 1 - core), device_id_type=MESH,
        )
        copy.wait_recv() if which else copy.wait_send()


def gather_kernel(axes, plan, n, *refs):
    k = 5
    ins, rows, flag = refs[:k], refs[k], refs[k + 1]
    outs, landing, other = refs[k + 2 : 2 * k + 2], refs[2 * k + 2], refs[2 * k + 3]
    stages = refs[2 * k + 4 : 3 * k + 4]
    send_sem, recv_sem, pair_send, pair_recv, local_sem, row_sems = refs[3 * k + 4 :]
    me, core = lax.axis_index("fsdp"), lax.axis_index("rep")
    enter(n, me, core)
    told = pltpu.make_async_remote_copy(
        src_ref=flag, dst_ref=other, send_sem=row_sems.at[3], recv_sem=row_sems.at[4],
        device_id=(me, 1 - core), device_id_type=MESH,
    )
    told.start()
    numbered, number = [], 0
    for order, pieces in plan:
        numbered.append((order, [(number + i, p) for i, p in enumerate(pieces)]))
        number += len(pieces)

    def spot(axis):
        return (me // axis[0]) % axis[1]

    def dst(piece, block):
        return outs[piece.array].at[block, :, piece.cols(core)]

    def put(pieces, block, own, phase, way, device, pair=False):
        for i, piece in pieces:
            if pair and not piece.half:
                continue
            src = ins[piece.array].at[:, piece.cols(core)] if own else dst(piece, block)
            pltpu.make_async_remote_copy(
                src_ref=src,
                dst_ref=dst(piece, block),
                send_sem=pair_send.at[i] if pair else send_sem.at[i, phase, way],
                recv_sem=pair_recv.at[i] if pair else recv_sem.at[i, block],
                device_id=device,
                device_id_type=MESH,
            ).start()

    def along(pieces, order, block, own, phase, ways):
        stride, size = order[phase]
        at = spot(order[phase])
        if size == 1:
            return
        if size == 2:
            put(pieces, block, own, phase, 0, (me + (1 - 2 * at) * stride, core))
            return
        for way in ways:
            step = 1 - 2 * way
            pl.when(at < size - 1 if way == 0 else at > 0)(
                functools.partial(put, pieces, block, own, phase, way, (me + step * stride, core))
            )

    def arrived(pieces, order, block, phase, way):
        for i, piece in pieces:
            pltpu.make_async_remote_copy(
                src_ref=dst(piece, block),
                dst_ref=dst(piece, block),
                send_sem=send_sem.at[i, phase, way],
                recv_sem=recv_sem.at[i, block],
                device_id=(me, 1 - core),
                device_id_type=MESH,
            ).wait_recv()
        if order[phase][1] > 2:
            along(pieces, order, block, False, phase, (way,))
        for later in range(phase + 1, 3):
            along(pieces, order, block, False, later, (0, 1))
        put(pieces, block, False, 0, 0, (me, 1 - core), pair=True)

    for order, pieces in numbered:
        for phase in range(3):
            along(pieces, order, me, True, phase, (0, 1))
    own = rows_out(n, me, core, rows, landing, row_sems.at[0], row_sems.at[1], row_sems.at[2])
    local = []
    for j in range(k):
        local.append(pltpu.make_async_copy(ins[j], stages[j], local_sem.at[j]))
        local[-1].start()
    events = []
    for number, (order, pieces) in enumerate(numbered):
        heavy = number >= 2
        sizes = [a[1] for a in order]
        for phase in range(3):
            size = sizes[phase]
            rest = 1
            for s in sizes[:phase]:
                rest *= s
            for t in range(1, size):
                ways = (0,) if size == 2 else (0, 1)
                for way in ways:
                    for j in range(rest):
                        if heavy:
                            key = 20 * t if phase == 0 else 20 * phase + 20 * (j + (t - 1) * rest + 1)
                        else:
                            key = 5 if phase == 0 else 10 + 5 * j if phase == 1 else 15 + 40 * t + 5 * j
                        events.append((key, len(events), order, pieces, phase, t, way, j))
    events.sort(key=lambda e: e[:2])

    def run(order, pieces, phase, t, way, j):
        stride, size = order[phase]
        at = spot(order[phase])
        origin = 1 - at if size == 2 else at - (1 - 2 * way) * t
        block = me + (origin - at) * stride
        for s, z in order[:phase]:
            here = (me // s) % z
            block = block + (xor(here, j % z, z) - here) * s
            j = j // z
        if size == 2:
            arrived(pieces, order, block, phase, 0)
        else:
            pl.when((origin >= 0) & (origin < size))(
                functools.partial(arrived, pieces, order, block, phase, way)
            )

    def settle():
        for j in range(k):
            local[j].wait()
            local[j] = pltpu.make_async_copy(stages[j], outs[j].at[me], local_sem.at[j])
            local[j].start()

    for number, (_, _, order, pieces, phase, t, way, j) in enumerate(events):
        run(order, pieces, phase, t, way, j)
        if number == 3:
            settle()
    for copy in local:
        copy.wait()
    told.wait()
    rows_wait(n, me, core, rows, landing, row_sems.at[0], row_sems.at[1], own)

    def drain(i, piece, count, send, recv, which):
        many = outs[piece.array].at[pl.ds(0, count), :, piece.cols(core)]
        copy = pltpu.make_async_remote_copy(
            src_ref=many, dst_ref=many, send_sem=send, recv_sem=recv,
            device_id=(me, 1 - core), device_id_type=MESH,
        )
        if which == "send":
            copy.wait_send()
        else:
            copy.wait_recv()

    for order, pieces in numbered:
        rest = 1
        for phase in range(3):
            stride, size = order[phase]
            at = spot(order[phase])
            for i, piece in pieces:
                if size == 2:
                    drain(i, piece, rest, send_sem.at[i, phase, 0], recv_sem.at[i, 0], "send")
                elif size > 2:
                    for here in range(size):
                        def both(here=here, i=i, piece=piece, phase=phase, rest=rest, size=size):
                            if here < size - 1:
                                drain(i, piece, (here + 1) * rest, send_sem.at[i, phase, 0], recv_sem.at[i, 0], "send")
                            if here > 0:
                                drain(i, piece, (size - here) * rest, send_sem.at[i, phase, 1], recv_sem.at[i, 0], "send")
                        pl.when(at == here)(both)
            rest *= size
        for i, piece in pieces:
            if piece.half:
                drain(i, piece, n - 1, pair_send.at[i], pair_recv.at[i], "send")
                drain(i, piece, n - 1, pair_send.at[i], pair_recv.at[i], "recv")


def gather_all(axes, n, arrays, rows, flag, collective_id):
    plan = colours(axes, [a.shape[1] for a in arrays])
    pieces = sum(len(p) for _, p in plan)
    vmem = pl.BlockSpec(memory_space=pltpu.VMEM)
    anywhere = pl.BlockSpec(memory_space=ANY)
    dma = pltpu.SemaphoreType.DMA
    return pl.pallas_call(
        functools.partial(gather_kernel, axes, plan, n),
        out_shape=[jax.ShapeDtypeStruct((n,) + a.shape, a.dtype) for a in arrays]
        + [jax.ShapeDtypeStruct(a.shape, a.dtype) for a in (rows, flag)],
        in_specs=[anywhere] * len(arrays) + [vmem, vmem],
        out_specs=[anywhere] * (len(arrays) + 1) + [vmem],
        scratch_shapes=[pltpu.VMEM(a.shape, a.dtype) for a in arrays]
        + [dma((pieces, 3, 2)), dma((pieces, n)), dma((pieces,)), dma((pieces,)), dma((len(arrays),)), dma((5,))],
        compiler_params=pltpu.CompilerParams(collective_id=collective_id, has_side_effects=True),
        name="gather_all",
    )(*arrays, rows, flag)
def add_into(acc, a, got, g, rows):
    step = min(rows, 16)

    def go(i, _):
        at = pl.ds(pl.multiple_of(i * step, step), step)
        acc[a, at, :] = (acc[a, at, :].astype(jnp.float32) + got[g, at, :].astype(jnp.float32)).astype(acc.dtype)
        return 0

    lax.fori_loop(0, rows // step, go, 0)


def turn(at, t, size):
    if size == 2:
        return at + (1 - 2 * at) * (1 - t)
    up = size - 1 - at
    first_up = jnp.where(t < up, size - 1 - t, t - up)
    first_down = jnp.where(t < at, t, size - 1 - (t - at))
    return jnp.where(t == size - 1, at, jnp.where(2 * at < size, first_up, first_down))


def slots(size):
    return 1 if size <= 2 else size + 1


def scatter_kernel(axes, plan, n, *refs):
    k = 5
    ins, rows, outs, landing = refs[:k], refs[k], refs[k + 1 : 2 * k + 1], refs[2 * k + 1]
    total = sum(len(p) for _, p in plan)
    buffers = refs[2 * k + 2 : 2 * k + 2 + 5 * total]
    own_sem, pair_send, pair_recv, send_sem = refs[-10:-6]
    recv_sems, last_send, last_recv, row_sems = refs[-6:-3], refs[-3], refs[-2], refs[-1]
    me, core = lax.axis_index("fsdp"), lax.axis_index("rep")
    enter(n, me, core)
    numbered, number = [], 0
    for order, pieces in plan:
        numbered.append((order, [(number + i, p) for i, p in enumerate(pieces)]))
        number += len(pieces)
    acc = [buffers[5 * i] for i in range(total)]
    pair = [buffers[5 * i + 1] for i in range(total)]
    got = [buffers[5 * i + 2 : 5 * i + 5] for i in range(total)]

    def spot(axis):
        return (me // axis[0]) % axis[1]

    def pair_copy(i, piece, block):
        return pltpu.make_async_remote_copy(
            src_ref=ins[piece.array].at[block, :, piece.cols(1 - core)],
            dst_ref=pair[i].at[block],
            send_sem=pair_send.at[i],
            recv_sem=pair_recv.at[i, block],
            device_id=(me, 1 - core),
            device_id_type=MESH,
        )

    def own_copy(i, piece, block):
        return pltpu.make_async_copy(
            ins[piece.array].at[block, :, piece.cols(core)], acc[i].at[block], own_sem.at[i, block]
        )

    def block_at(order, phase, origin, turns):
        block = me + (origin - spot(order[phase])) * order[phase][0]
        for axis, t in zip(order[:phase], turns):
            block = block + (turn(spot(axis), t, axis[1]) - spot(axis)) * axis[0]
        return block

    def ready(pieces, block):
        for i, piece in pieces:
            own_copy(i, piece, block).wait()
            pair_copy(i, piece, block).wait_recv()
            add_into(acc[i], block, pair[i], block, acc[i].shape[1])

    def hop(i, phase, block, rest, slot, send, device):
        return pltpu.make_async_remote_copy(
            src_ref=acc[i].at[block],
            dst_ref=got[i][phase].at[rest, slot],
            send_sem=send,
            recv_sem=recv_sems[phase].at[i, rest * got[i][phase].shape[1] + slot],
            device_id=device,
            device_id_type=MESH,
        )

    def take(pieces, phase, block, rest, slot):
        for i, piece in pieces:
            hop(i, phase, block, rest, slot, send_sem.at[i, phase], (me, 1 - core)).wait_recv()
            add_into(acc[i], block, got[i][phase].at[rest], slot, acc[i].shape[1])

    def give(pieces, phase, block, rest, slot, device):
        for i, piece in pieces:
            hop(i, phase, block, rest, slot, send_sem.at[i, phase], device).start()

    def event(order, pieces, phase, t, turns, first):
        stride, size = order[phase]
        at = spot(order[phase])
        origin = turn(at, t, size)
        mine = t == size - 1
        block = block_at(order, phase, origin, turns)
        rest = 0
        for axis, away in zip(order[:phase], turns):
            rest = rest * axis[1] + away
        if first:
            ready(pieces, block)
        if size == 1:
            return
        if size == 2:
            pl.when(jnp.logical_not(mine))(
                lambda: give(pieces, phase, block, rest, 0, (me + (1 - 2 * at) * stride, core))
            )
            pl.when(mine)(lambda: take(pieces, phase, block, rest, 0))
            return

        @pl.when(jnp.logical_not(mine))
        def _():
            up = (origin > at).astype(jnp.int32)
            behind = jnp.where(up == 1, at > 0, at < size - 1)
            pl.when(behind)(lambda: take(pieces, phase, block, rest, origin))
            step = 2 * up - 1
            landing = jnp.where((up == 0) & (origin == at - 1), size, origin)
            give(pieces, phase, block, rest, landing, (me + step * stride, core))

        @pl.when(mine)
        def _():
            pl.when(at > 0)(lambda: take(pieces, phase, block, rest, at))
            pl.when(at < size - 1)(lambda: take(pieces, phase, block, rest, size))

    def each(count, fn):
        lax.fori_loop(0, count, lambda e, _: (fn(e), 0)[1], 0)

    def begin(order, pieces, s):
        _, (_, nq), (_, nr) = order

        def go(e):
            block = block_at(order, 2, turn(spot(order[2]), e // nq, nr), (s, e % nq))
            for i, piece in pieces:
                pair_copy(i, piece, block).start()
                own_copy(i, piece, block).start()

        each(nr * nq, go)

    def lead(order, pieces, s):
        _, (_, nq), (_, nr) = order
        each((nr - 1) * nq, lambda e: event(order, pieces, 2, e // nq, (s, e % nq), True))

    def later(order, pieces, s, low, high):
        def go(e):
            event(order, pieces, 2, order[2][1] - 1, (s, low + e), True)
            event(order, pieces, 1, low + e, (s,), False)

        each(high - low, go)

    def finish(order, pieces, s):
        event(order, pieces, 0, s, (), False)

    light, heavy = numbered[:2], numbered[2:]
    steps, few = heavy[0][0][0][1], max(c[0][0][1] for c in light)

    def begin_all(s):
        for colour in heavy:
            pl.when(s < steps)(lambda colour=colour: begin(*colour, s))
        for colour in light:
            pl.when(s < colour[0][0][1])(lambda colour=colour: begin(*colour, s))

    each(max(steps, few), begin_all)
    own = rows_out(n, me, core, rows, landing, row_sems.at[0], row_sems.at[1], row_sems.at[2])
    for colour in heavy + light:
        lead(*colour, 0)

    def step(s):
        for colour in heavy:
            pl.when(s < steps)(lambda colour=colour: later(*colour, s, 0, 1))
        for colour in heavy:
            pl.when(s + 1 < steps)(lambda colour=colour: lead(*colour, s + 1))
        for colour in heavy:
            pl.when((s >= 1) & (s < steps))(lambda colour=colour: finish(*colour, s - 1))
        for colour in light:
            size = colour[0][0][1]
            pl.when(s + 1 < size)(lambda colour=colour: lead(*colour, s + 1))
        for colour in heavy:
            pl.when(s < steps)(lambda colour=colour: later(*colour, s, 1, colour[0][1][1]))
        for colour in light:
            size = colour[0][0][1]

            @pl.when((s >= 1) & (s <= size))
            def _(colour=colour):
                later(*colour, s - 1, 0, colour[0][1][1])
                finish(*colour, s - 1)
        for colour in heavy:
            pl.when(s == steps - 1)(lambda colour=colour: finish(*colour, s))

    each(max(steps, few + 1), step)

    final = []
    for order, pieces in numbered:
        for i, piece in pieces:
            outs[piece.array][:, piece.cols(core)] = acc[i][me]
            if piece.half:
                final.append(
                    pltpu.make_async_remote_copy(
                        src_ref=acc[i].at[me],
                        dst_ref=outs[piece.array].at[:, piece.cols(core)],
                        send_sem=last_send.at[i],
                        recv_sem=last_recv.at[i],
                        device_id=(me, 1 - core),
                        device_id_type=MESH,
                    )
                )
                final[-1].start()
    for copy in final:
        copy.wait()
    rows_wait(n, me, core, rows, landing, row_sems.at[0], row_sems.at[1], own)

    def drain(i, phase, count):
        many = acc[i].at[pl.ds(0, count)]
        pltpu.make_async_remote_copy(
            src_ref=many, dst_ref=many, send_sem=send_sem.at[i, phase], recv_sem=last_recv.at[i],
            device_id=(me, 1 - core), device_id_type=MESH,
        ).wait_send()

    for order, pieces in numbered:
        for i, piece in pieces:
            for phase in range(3):
                if order[phase][1] > 1:
                    count = order[phase][1] - 1
                    for axis in order[:phase]:
                        count *= axis[1]
                    drain(i, phase, count)
            many = acc[i].at[pl.ds(0, n)]
            pltpu.make_async_remote_copy(
                src_ref=many, dst_ref=many, send_sem=pair_send.at[i], recv_sem=last_recv.at[i],
                device_id=(me, 1 - core), device_id_type=MESH,
            ).wait_send()


def scatter_all(axes, n, arrays, rows, collective_id):
    plan = colours(axes, [a.shape[2] for a in arrays])
    pieces = [(order, p) for order, ps in plan for p in ps]
    scratch = []
    for order, p in pieces:
        deep, dtype = arrays[p.array].shape[1], arrays[p.array].dtype
        scratch += [pltpu.VMEM((n, deep, p.width), dtype)] * 2
        count = 1
        for phase in range(3):
            size = order[phase][1]
            scratch.append(pltpu.VMEM((count, slots(size), deep, p.width), dtype))
            count *= size
    total = len(pieces)
    shapes = []
    for phase in range(3):
        most = 1
        for order, _ in plan:
            count = slots(order[phase][1])
            for a in order[:phase]:
                count *= a[1]
            most = max(most, count)
        shapes.append((total, most))
    dma = pltpu.SemaphoreType.DMA
    return pl.pallas_call(
        functools.partial(scatter_kernel, axes, plan, n),
        out_shape=[jax.ShapeDtypeStruct(a.shape[1:], a.dtype) for a in arrays]
        + [jax.ShapeDtypeStruct(rows.shape, rows.dtype)],
        in_specs=[pl.BlockSpec(memory_space=ANY)] * len(arrays) + [pl.BlockSpec(memory_space=pltpu.VMEM)],
        out_specs=[pl.BlockSpec(memory_space=pltpu.VMEM)] * len(arrays) + [pl.BlockSpec(memory_space=ANY)],
        scratch_shapes=scratch
        + [dma((total, n)), dma((total,)), dma((total, n)), dma((total, 3))]
        + [dma(s) for s in shapes]
        + [dma((total,)), dma((total,)), dma((3,))],
        compiler_params=pltpu.CompilerParams(
            collective_id=collective_id, has_side_effects=True, vmem_limit_bytes=60 * 1024 * 1024
        ),
        name="scatter_all",
    )(*arrays, rows)


SQRT_2_PI = math.sqrt(2.0 / math.pi)
NN = (((1,), (0,)), ((), ()))
NT = (((1,), (1,)), ((), ()))
TN = (((0,), (0,)), ((), ()))


def mm(a, b, dims=NN):
    return lax.dot_general(a, b, dims, preferred_element_type=jnp.float32)


def each(count, fn):
    lax.fori_loop(0, count, lambda e, _: (fn(e), 0)[1], 0)


class Part:
    def __init__(self, array, offset, width):
        self.array, self.offset, self.width = array, offset, width

    def of(self, ref, block):
        return ref.at[block, :, pl.ds(self.offset, self.width)]


EARLY, AT0, AT1, CUT, SPLIT = 30, 4, 85, 50, False
AHEAD = 1
ROWS_IN, ROWS_OUT, ORDER = (0, 100), 5, ()


def first_shares(axes, vectors):
    a, b, c = axes
    half = D // 2
    return [
        ((b, c, a), [Part(1, 0, D // 4), Part(4, 0, vectors)]),
        ((c, b, a), [Part(0, 0, D // 4)]),
        ((a, b, c), [Part(0, D // 4, half + D // 4)]),
        ((a, c, b), [Part(0, D, half), Part(1, D // 4, D // 4)]),
    ]


def second_shares(axes):
    a, b, c = axes
    return [
        ((b, c, a), [Part(2, 0, 3 * D // 8)]),
        ((c, b, a), [Part(3, 0, D // 4)]),
        ((a, b, c), [Part(2, 3 * D // 8, 13 * D // 8)]),
        ((a, c, b), [Part(3, D // 4, 3 * D // 4)]),
    ]


def number_parts(plan):
    numbered, number = [], 0
    for order, parts in plan:
        numbered.append((order, [(number + i, p) for i, p in enumerate(parts)]))
        number += len(parts)
    return numbered


def send(src, dst, send_sem, recv_sem, device):
    return pltpu.make_async_remote_copy(
        src_ref=src, dst_ref=dst, send_sem=send_sem, recv_sem=recv_sem, device_id=device, device_id_type=MESH
    )


class Gather:
    def __init__(self, n, me, core, numbered, whole, sems):
        self.n, self.me, self.core, self.numbered, self.whole = n, me, core, numbered, whole
        self.send_sem, self.recv_sem = sems

    def spot(self, axis):
        return (self.me // axis[0]) % axis[1]

    def put(self, parts, block, phase, way, step):
        for i, part in parts:
            dst = part.of(self.whole[part.array], block)
            send(
                dst, dst, self.send_sem.at[i, phase, way], self.recv_sem.at[i, block], (self.me + step, self.core)
            ).start()

    def along(self, parts, order, block, phase, ways):
        stride, size = order[phase]
        at = self.spot(order[phase])
        if size == 2:
            self.put(parts, block, phase, 0, (1 - 2 * at) * stride)
        elif size > 2:
            for way in ways:
                step = (1 - 2 * way) * stride
                pl.when(at < size - 1 if way == 0 else at > 0)(
                    functools.partial(self.put, parts, block, phase, way, step)
                )

    def arrived(self, parts, order, block, phase, way):
        for i, part in parts:
            dst = part.of(self.whole[part.array], block)
            send(
                dst, dst, self.send_sem.at[i, phase, way], self.recv_sem.at[i, block], (self.me, 1 - self.core)
            ).wait_recv()
        if order[phase][1] > 2:
            self.along(parts, order, block, phase, (way,))
        for later in range(phase + 1, 3):
            self.along(parts, order, block, later, (0, 1))

    def start(self):
        for order, parts in self.numbered:
            for phase in range(3):
                self.along(parts, order, self.me, phase, (0, 1))

    def events(self):
        found = []
        for number, (order, parts) in enumerate(self.numbered):
            heavy = number >= 2
            sizes = [a[1] for a in order]
            for phase in range(3):
                size, rest = sizes[phase], math.prod(sizes[:phase])
                for t in range(1, size):
                    for way in (0,) if size == 2 else (0, 1):
                        for j in range(rest):
                            if heavy:
                                key = 20 * t if phase == 0 else 20 * phase + 20 * (j + (t - 1) * rest + 1)
                            else:
                                key = 5 if phase == 0 else 10 + 5 * j if phase == 1 else 15 + 40 * t + 5 * j
                            found.append((key, len(found), order, parts, phase, t, way, j))
        found.sort(key=lambda e: e[:2])
        return [functools.partial(self.run, *e[2:]) for e in found]

    def run(self, order, parts, phase, t, way, j):
        stride, size = order[phase]
        at = self.spot(order[phase])
        origin = 1 - at if size == 2 else at - (1 - 2 * way) * t
        block = self.me + (origin - at) * stride
        for s, z in order[:phase]:
            here = (self.me // s) % z
            block = block + (xor(here, j % z, z) - here) * s
            j = j // z
        if size == 2:
            self.arrived(parts, order, block, phase, 0)
        else:
            pl.when((origin >= 0) & (origin < size))(
                functools.partial(self.arrived, parts, order, block, phase, way)
            )

    def drain(self):
        for order, parts in self.numbered:
            rest = 1
            for phase in range(3):
                size = order[phase][1]
                at = self.spot(order[phase])
                for i, part in parts:
                    def gone(count, way, i=i, part=part, phase=phase):
                        many = part.of(self.whole[part.array], pl.ds(0, count))
                        send(
                            many, many, self.send_sem.at[i, phase, way], self.recv_sem.at[i, 0], (self.me, 1 - self.core)
                        ).wait_send()

                    if size == 2:
                        gone(rest, 0)
                    elif size > 2:
                        for here in range(size):
                            def both(here=here, gone=gone, rest=rest, size=size):
                                if here < size - 1:
                                    gone((here + 1) * rest, 0)
                                if here > 0:
                                    gone((size - here) * rest, 1)
                            pl.when(at == here)(both)
                rest *= size


class Scatter:
    def __init__(self, me, core, numbered, acc, got, sems):
        self.me, self.core, self.numbered, self.acc, self.got = me, core, numbered, acc, got
        self.send_sem, self.recv_sems, self.drain_sem = sems

    def spot(self, axis):
        return (self.me // axis[0]) % axis[1]

    def block_at(self, order, phase, origin, turns):
        block = self.me + (origin - self.spot(order[phase])) * order[phase][0]
        for axis, t in zip(order[:phase], turns):
            block = block + (turn(self.spot(axis), t, axis[1]) - self.spot(axis)) * axis[0]
        return block

    def hop(self, i, part, phase, block, rest, slot, device):
        return send(
            part.of(self.acc[part.array], block),
            self.got[i][phase].at[rest, slot],
            self.send_sem.at[i, phase],
            self.recv_sems[phase].at[i, rest * self.got[i][phase].shape[1] + slot],
            device,
        )

    def take(self, parts, phase, block, rest, slot):
        for i, part in parts:
            self.hop(i, part, phase, block, rest, slot, (self.me, 1 - self.core)).wait_recv()
            acc, got = self.acc[part.array], self.got[i][phase]
            rows = acc.shape[1]
            step = min(rows, 16)
            cols = pl.ds(part.offset, part.width)

            def go(e, acc=acc, got=got, step=step, cols=cols):
                at = pl.ds(pl.multiple_of(e * step, step), step)
                acc[block, at, cols] = acc[block, at, cols] + got[rest, slot, at, :]

            each(rows // step, go)

    def give(self, parts, phase, block, rest, slot, step):
        for i, part in parts:
            self.hop(i, part, phase, block, rest, slot, (self.me + step, self.core)).start()

    def event(self, order, parts, phase, t, turns):
        stride, size = order[phase]
        at = self.spot(order[phase])
        origin = turn(at, t, size)
        mine = t == size - 1
        block = self.block_at(order, phase, origin, turns)
        rest = 0
        for axis, away in zip(order[:phase], turns):
            rest = rest * axis[1] + away
        if size == 1:
            return
        if size == 2:
            pl.when(jnp.logical_not(mine))(
                lambda: self.give(parts, phase, block, rest, 0, (1 - 2 * at) * stride)
            )
            pl.when(mine)(lambda: self.take(parts, phase, block, rest, 0))
            return

        @pl.when(jnp.logical_not(mine))
        def _():
            up = (origin > at).astype(jnp.int32)
            behind = jnp.where(up == 1, at > 0, at < size - 1)
            pl.when(behind)(lambda: self.take(parts, phase, block, rest, origin))
            landing = jnp.where((up == 0) & (origin == at - 1), size, origin)
            self.give(parts, phase, block, rest, landing, (2 * up - 1) * stride)

        @pl.when(mine)
        def _():
            pl.when(at > 0)(lambda: self.take(parts, phase, block, rest, at))
            pl.when(at < size - 1)(lambda: self.take(parts, phase, block, rest, size))

    def lead(self, order, parts, s):
        _, (_, nq), (_, nr) = order
        each((nr - 1) * nq, lambda e: self.event(order, parts, 2, e // nq, (s, e % nq)))

    def later(self, order, parts, s, low, high):
        def go(e):
            self.event(order, parts, 2, order[2][1] - 1, (s, low + e))
            self.event(order, parts, 1, low + e, (s,))

        each(high - low, go)

    def finish(self, order, parts, s):
        self.event(order, parts, 0, s, ())

    def stages(self):
        light, heavy = self.numbered[:2], self.numbered[2:]
        steps, few = heavy[0][0][0][1], max(c[0][0][1] for c in light)
        found = [functools.partial(self.lead, *c, s) for c in heavy[::-1] for s in range(min(AHEAD, steps))]
        found += [functools.partial(self.lead, *colour, 0) for colour in light]
        for s in range(max(steps, few + 1)):
            if s < steps:
                found += [functools.partial(self.later, *colour, s, 0, 1) for colour in heavy]
            if s + AHEAD < steps:
                found += [functools.partial(self.lead, *colour, s + AHEAD) for colour in heavy]
            if 1 <= s < steps:
                found += [functools.partial(self.finish, *colour, s - 1) for colour in heavy]
            found += [functools.partial(self.lead, *c, s + 1) for c in light if s + 1 < c[0][0][1]]
            if s < steps:
                found += [functools.partial(self.later, *c, s, 1, c[0][1][1]) for c in heavy]
            for c in light:
                if 1 <= s <= c[0][0][1]:
                    found += [
                        functools.partial(self.later, *c, s - 1, e, e + 1) for e in range(c[0][1][1])
                    ]
                    found.append(functools.partial(self.finish, *c, s - 1))
            if s == steps - 1:
                found += [functools.partial(self.finish, *colour, s) for colour in heavy]
        return found

    def drain(self):
        for order, parts in self.numbered:
            for i, part in parts:
                for phase in range(3):
                    if order[phase][1] > 1:
                        count = (order[phase][1] - 1) * math.prod([a[1] for a in order[:phase]])
                        many = part.of(self.acc[part.array], pl.ds(0, count))
                        send(
                            many, many, self.send_sem.at[i, phase], self.drain_sem, (self.me, 1 - self.core)
                        ).wait_send()


class Refs:
    pass


def block_kernel(axes, n, cap, *refs):
    names = (
        "wq", "wo", "wu", "wd", "vec", "rows_in", "pick", "extra", "notes", "gq", "go", "gu", "gd", "gs",
        "landed", "new", "Wq", "Wo", "Wu", "Wd", "V", "Wo2", "Aq", "Ao", "Au", "Ad", "As", "As2", "land",
        "rows_out", "X", "DY", "N1", "QKV", "PROBS", "ATT", "PART", "SENT", "GOT1", "GOT2", "GOT3", "GOT4",
        "BA", "N2", "ACT", "GM", "GU", "M1", "GA", "GATT", "GQKV", "GR", "NOTE", "FQ", "FO", "FU", "FD",
    )
    r = Refs()
    for name, ref in zip(names, refs):
        setattr(r, name, ref)
    got_refs, sems = refs[len(names) : -8], refs[-8:]
    g_send, g_recv, g_local, s_send, s_recv0, s_recv1, s_recv2, misc = sems
    R = D // n
    me, core = lax.axis_index("fsdp"), lax.axis_index("rep")
    half = D // 2
    pair = (me, 1 - core)
    units = r.wd.shape[0] // 2
    blocks = [r.Wq, r.Wo, r.Wu, r.Wd, r.V]

    def stage(src, dst, k):
        pltpu.make_async_copy(src, dst, g_local.at[k]).start()

    def column(f, size, start):
        return pl.ds(pl.multiple_of(f * size + start, 128), size)

    for k in range(3):
        stage(r.wq.at[:, pl.ds(pl.multiple_of(k * D + core * half, 128), half)], r.Wq.at[me, :, pl.ds(k * half, half)], 0)
    stage(r.wo.at[:, column(core, half, 0)], r.Wo.at[me], 1)
    each(
        n, lambda f: stage(r.wu.at[:, column(2 * f + core, units, 0)], r.Wu.at[me, :, column(f, units, 0)], 2)
    )
    stage(r.wd.at[pl.ds(pl.multiple_of(core * units, 16), units)], r.Wd.at[me], 3)
    stage(r.vec, r.V.at[me], 4)
    enter(n, me, core)
    for k, whole in enumerate(blocks):
        pltpu.make_async_copy(whole.at[me], whole.at[me], g_local.at[k]).wait()
    counter = [0]

    def to_pair(src, dst):
        k = counter[0]
        counter[0] += 2
        copy = send(src, dst, misc.at[k], misc.at[k + 1], pair)
        copy.start()
        return copy

    numbered = number_parts(first_shares(axes, 128) + second_shares(axes))
    g_sems = (g_send, g_recv)
    gathers = [Gather(n, me, core, part, blocks, g_sems) for part in (numbered[:4], numbered[4:])]
    gathers[0].start()
    row_sems = [misc.at[40 + k] for k in range(6)]
    def spread(items, chunks, low, high):
        done = 0
        for number, item in enumerate(items):
            item()
            want = len(chunks) * (number + 1 - low) // max(high - low, 1) if number + 1 >= low else 0
            while done < min(max(want, 0), len(chunks)):
                chunks[done]()
                done += 1
        for chunk in chunks[done:]:
            chunk()

    own_rows, row_sends = rows_each(n, me, core, r.rows_in, r.land, *row_sems[:3])
    note = to_pair(r.notes, r.NOTE)
    events = gathers[0].events()
    events.insert(len(events) * EARLY // 100, gathers[1].start)
    behind = gathers[1].events()
    late_sends = []
    if ROWS_IN[1] > 100:
        late_sends = row_sends[(n - 1) * 100 // ROWS_IN[1]:]
        row_sends = row_sends[: (n - 1) * 100 // ROWS_IN[1]]
    spread(events, row_sends, len(events) * ROWS_IN[0] // 100, len(events) * min(ROWS_IN[1], 100) // 100)
    for number, chunk in enumerate(late_sends):
        behind.insert(2 * number, chunk)
    mine, theirs = pl.ds(0, CAP), pl.ds(CAP, CAP)
    STEP = 64
    TILE = 256
    flying = Refs()

    def cols(e, size=TILE):
        return pl.ds(pl.multiple_of(e * size, size), size)

    def flat(ref, at):
        return ref[:, :, at].reshape(-1, at.size)

    def vector(v):
        per = 128 // R
        tiles = []
        for t in range(D // 128):
            total = r.V[t * per].astype(jnp.float32)[v : v + 1, :]
            for j in range(1, per):
                total = total + r.V[t * per + j].astype(jnp.float32)[v : v + 1, :]
            tiles.append(total)
        return jnp.concatenate(tiles, axis=1)

    w_router, gain1, gain2 = vector(0), vector(1), vector(2)

    def inverse(v):
        return lax.rsqrt(jnp.mean(v * v, axis=1, keepdims=True) + EPSILON)

    def rows_here():
        rows_wait(n, me, core, r.rows_in, r.land, row_sems[0], row_sems[1], own_rows)
        flying.out_half = to_pair(r.Wo.at[pl.ds((1 - core) * (n // 2), n // 2)], r.Wo2)

    def extract(k, ref):
        def go(e):
            at = pl.ds(k * CAP, CAP)
            ref[:CAP, cols(e)] = (
                mm(r.pick[at, :], r.land[:, :, cols(e)].reshape(-1, TILE)) + r.extra[at, cols(e)].astype(jnp.float32)
            ).astype(jnp.bfloat16)

        each(D // TILE, go)

    def swap_rows():
        flying.both = [to_pair(ref.at[mine], ref.at[theirs]) for ref in (r.X, r.DY)] + [note]

    def first(e):
        at = pl.ds(pl.multiple_of(e * STEP, STEP), STEP)
        x = r.X[at, :].astype(jnp.float32)
        r.N1[at, :] = (x * inverse(x) * gain1).astype(jnp.bfloat16)
        router = jnp.sum(x * w_router, axis=1, keepdims=True)
        r.GM[at, :] = (router * r.DY[at, :].astype(jnp.float32)).astype(jnp.bfloat16)

    def first_rows():
        for copy in flying.both:
            copy.wait()
        each(2 * CAP // STEP, first)

    def project(e):
        r.QKV[:, cols(e)] = mm(r.N1[...], flat(r.Wq, cols(e))).astype(jnp.bfloat16)

    factor = 1.0 / math.sqrt(HEAD_DIM)
    pairs = half // 128
    lane = lax.broadcasted_iota(jnp.int32, (CAP, 128), 1) // HEAD_DIM
    zero = jnp.zeros((CAP, 128), jnp.bfloat16)
    causal = lax.broadcasted_iota(jnp.int32, (CAP, CAP), 1) <= lax.broadcasted_iota(jnp.int32, (CAP, CAP), 0)

    def heads(e):
        s, p = e // pairs, e % pairs
        rows = pl.ds(pl.multiple_of(s * CAP, CAP), CAP)
        q, k, v = (r.QKV[rows, cols(p + j * pairs, 128)] for j in range(3))
        return s, p, rows, q, k, v

    def attend(e):
        s, p, rows, q, k, v = heads(e)
        valid = jnp.where(s == 0, r.notes[0:1, :], r.NOTE[0:1, :]) > 0
        parts = []
        for h in range(2):
            score = mm(jnp.where(lane == h, q, zero), k, NT) * factor
            score = jnp.where(causal & valid, score, -1e30)
            top = jnp.exp(score - jnp.max(score, axis=1, keepdims=True))
            probs = top / jnp.sum(top, axis=1, keepdims=True)
            r.PROBS[2 * e + h] = probs
            parts.append(mm(probs.astype(jnp.bfloat16), v))
        r.ATT[rows, cols(p, 128)] = jnp.where(lane == 0, parts[0], parts[1]).astype(jnp.bfloat16)

    near = pl.ds(pl.multiple_of(core * half, half), half)
    away = pl.ds(pl.multiple_of((1 - core) * half, half), half)
    own_heads = pl.ds(core * (n // 2), n // 2)

    def wo_near():
        return r.Wo[own_heads].reshape(half, half)

    def wo_away():
        return r.Wo2[...].reshape(half, half)

    def project_out(where):
        if where == 0:
            r.BA[:, near] = mm(r.ATT[...], wo_near())
        else:
            flying.out_half.wait()
            r.BA[:, away] = mm(r.ATT[...], wo_away())

    def pass_on(part, got):
        for a, b in ((mine, theirs), (theirs, mine)):
            r.SENT[a, :] = part[b, :].astype(jnp.bfloat16)
        flying.gone = to_pair(r.SENT, got)

    def second(e):
        at = pl.ds(pl.multiple_of(e * STEP, STEP), STEP)
        branch = r.BA[at, :] + r.GOT1[at, :].astype(jnp.float32)
        r.BA[at, :] = branch
        middle = r.X[at, :].astype(jnp.float32) + branch
        r.N2[at, :] = (middle * inverse(middle) * gain2).astype(jnp.bfloat16)

    def second_rows():
        flying.gone.wait()
        each(2 * CAP // STEP, second)

    def some(fn, low, high):
        return lambda: lax.fori_loop(low, high, lambda e, _: (fn(e), 0)[1], 0)

    forward = [rows_here, functools.partial(extract, 0, r.X), functools.partial(extract, 1, r.DY), swap_rows, first_rows]
    forward += [some(project, e, e + 1) for e in range(3 * half // TILE)]
    forward += [some(attend, e, e + 2) for e in range(0, 2 * pairs, 2)]
    forward += [
        functools.partial(project_out, 0), functools.partial(project_out, 1),
        lambda: pass_on(r.BA, r.GOT1), second_rows,
    ]
    spread(behind, forward, len(behind) * AT0 // 100, len(behind) * AT1 // 100)
    hidden = r.Wd.shape[1]
    per = TILE // hidden if hidden < TILE else 1

    def down_rows(e):
        return pl.ds(e * per, per)

    def hidden_units(e):
        up = mm(r.N2[...], flat(r.Wu, cols(e)))
        inner = jnp.tanh(SQRT_2_PI * (up + 0.044715 * up * up * up))
        act = (0.5 * up * (1.0 + inner)).astype(jnp.bfloat16)
        slope = 0.5 * (1.0 + inner) + 0.5 * up * (1.0 - inner * inner) * (
            SQRT_2_PI * (1.0 + 3 * 0.044715 * up * up)
        )
        r.ACT[:, cols(e)] = act
        down = r.Wd[down_rows(e)].reshape(TILE, D)
        grad_act = mm(r.GM[...], down, NT)
        r.GU[:, cols(e)] = (slope * grad_act).astype(jnp.bfloat16)
        r.Ad[down_rows(e)] = mm(act, r.GM[...], TN).astype(jnp.bfloat16).reshape(per, hidden, D)

    tiles = 2 * D // TILE
    each(tiles, hidden_units)

    def up_grads(e):
        r.Au[:, :, cols(e)] = mm(r.N2[...], r.GU[:, cols(e)], TN).astype(jnp.bfloat16).reshape(n, R, TILE)

    total = sum(len(p) for _, p in numbered)
    got = [got_refs[3 * i : 3 * i + 3] for i in range(total)]
    s_sems = (s_send, (s_recv0, s_recv1, s_recv2), misc.at[46])
    acc = [r.Aq, r.Ao, r.Au, r.Ad, r.As]
    late, soon = (Scatter(me, core, part, acc, got, s_sems) for part in (numbered[:4], numbered[4:]))
    many = TILE // R

    def back_up(e):
        block = r.Wu[pl.ds(e * many, many)].reshape(TILE, 2 * D)
        r.PART[:, cols(e)] = mm(r.GU[...], block, NT)

    def mlp(e):
        r.M1[:, cols(e)] = mm(r.ACT[...], r.Wd[:, :, cols(e)].reshape(2 * D, TILE))

    def mlp_out():
        flying.gone.wait()
        r.SENT[mine, :] = r.M1[theirs, :].astype(jnp.bfloat16)
        flying.gone = to_pair(r.SENT.at[mine], r.GOT3)

    zeros = jnp.zeros((1, D), jnp.float32)

    def third(e, total):
        at = pl.ds(pl.multiple_of(e * STEP, STEP), STEP)
        x = r.X[at, :].astype(jnp.float32)
        dy = r.DY[at, :].astype(jnp.float32)
        middle = x + r.BA[at, :]
        inv = inverse(middle)
        grad = r.PART[at, :] + r.GOT2[at, :].astype(jnp.float32)
        scaled = gain2 * grad
        grad_middle = inv * scaled - middle * inv**3 * jnp.mean(scaled * middle, axis=1, keepdims=True)
        router = jnp.sum(x * w_router, axis=1, keepdims=True)
        r.GA[at, :] = (router * dy + grad_middle).astype(jnp.bfloat16)
        r.PART[at, :] = grad_middle
        counted = jnp.where(e < CAP // STEP, 1.0, 0.0)
        return total + counted * jnp.sum(grad * middle * inv, axis=0, keepdims=True)

    def third_rows():
        flying.gain2 = lax.fori_loop(0, 2 * CAP // STEP, third, zeros)

    def out_grads():
        r.Ao[own_heads] = mm(r.ATT[...], r.GA[:, near], TN).astype(jnp.bfloat16).reshape(n // 2, R, half)

    def attended_grads():
        r.GATT[...] = (mm(r.GA[:, near], wo_near(), NT) + mm(r.GA[:, away], wo_away(), NT)).astype(jnp.bfloat16)

    def other_out_grads():
        flying.gone.wait()
        r.Wo2[...] = mm(r.ATT[...], r.GA[:, away], TN).astype(jnp.bfloat16).reshape(n // 2, R, half)
        flying.out = to_pair(r.Wo2, r.Ao.at[own_heads])

    def attend_back(e):
        s, p, rows, q, k, v = heads(e)
        grad = r.GATT[rows, cols(p, 128)]
        gq, gk, gv = [], [], []
        for h in range(2):
            grad_h, q_h = jnp.where(lane == h, grad, zero), jnp.where(lane == h, q, zero)
            probs = r.PROBS[2 * e + h]
            grad_probs = mm(grad_h, v, NT)
            gv.append(mm(probs.astype(jnp.bfloat16), grad_h, TN))
            grad_scores = probs * (grad_probs - jnp.sum(probs * grad_probs, axis=1, keepdims=True))
            grad_scores = grad_scores.astype(jnp.bfloat16)
            gq.append(mm(grad_scores, k))
            gk.append(mm(grad_scores, q_h, TN))
        r.GQKV[rows, cols(p, 128)] = (jnp.where(lane == 0, gq[0], gq[1]) * factor).astype(jnp.bfloat16)
        r.GQKV[rows, cols(p + pairs, 128)] = ((gk[0] + gk[1]) * factor).astype(jnp.bfloat16)
        r.GQKV[rows, cols(p + 2 * pairs, 128)] = (gv[0] + gv[1]).astype(jnp.bfloat16)

    def qkv_grads(e):
        r.Aq[:, :, cols(e)] = mm(r.N1[...], r.GQKV[:, cols(e)], TN).astype(jnp.bfloat16).reshape(n, R, TILE)

    def back_qkv(e):
        block = r.Wq[pl.ds(e * many, many)].reshape(TILE, 3 * half)
        r.M1[:, cols(e)] = mm(r.GQKV[...], block, NT)

    def fourth(e, total):
        at = pl.ds(pl.multiple_of(e * STEP, STEP), STEP)
        x = r.X[at, :].astype(jnp.float32)
        dy = r.DY[at, :].astype(jnp.float32)
        combined = r.BA[at, :] + r.M1[at, :] + r.GOT3[at, :].astype(jnp.float32)
        router = jnp.sum(x * w_router, axis=1, keepdims=True)
        r.new[at, :] = (x + router * combined).astype(jnp.bfloat16)
        grad_router = jnp.sum(dy * combined, axis=1, keepdims=True)
        r.GR[at, :] = dy + grad_router * w_router + r.PART[at, :]
        return total + jnp.sum(grad_router * x, axis=0, keepdims=True)

    def fourth_rows():
        flying.router = lax.fori_loop(0, CAP // STEP, fourth, zeros)

    def last_out():
        r.SENT[theirs, :] = r.M1[theirs, :].astype(jnp.bfloat16)
        flying.gone = to_pair(r.SENT.at[theirs], r.GOT4)

    def fifth(e, total):
        at = pl.ds(pl.multiple_of(e * STEP, STEP), STEP)
        x = r.X[at, :].astype(jnp.float32)
        grad = r.M1[at, :] + r.GOT4[at, :].astype(jnp.float32)
        inv = inverse(x)
        scaled = gain1 * grad
        grad_x = inv * scaled - x * inv**3 * jnp.mean(scaled * x, axis=1, keepdims=True)
        below = pl.ds(pl.multiple_of(CAP + e * STEP, STEP), STEP)
        r.new[below, :] = (r.GR[at, :] + grad_x).astype(jnp.bfloat16)
        return total + jnp.sum(grad * x * inv, axis=0, keepdims=True)

    def fifth_rows():
        flying.gone.wait()
        gain1_grad = lax.fori_loop(0, CAP // STEP, fifth, zeros)
        small = jnp.concatenate([flying.router, gain1_grad, flying.gain2, jnp.zeros((5, D), jnp.float32)], axis=0)
        for block in range(n):
            tile = block * R // 128
            r.As[block] = small[:, tile * 128 : tile * 128 + 128]
        flying.small = to_pair(r.As, r.As2)

    def place(e):
        sent = mm(r.pick[...], r.new[:, cols(e)], TN).astype(jnp.bfloat16)
        r.rows_out[:, :, cols(e)] = sent.reshape(n, -1, TILE)

    def send_late():
        flying.rows, flying.sends = rows_each(n, me, core, r.rows_out, r.landed, *row_sems[3:])
        flying.small.wait()
        flying.out.wait()
        r.As[...] = r.As[...] + r.As2[...]

    backward = [some(up_grads, e, e + 2) for e in range(0, tiles, 2)] if SPLIT else []
    backward += [some(back_up, e, e + 1) for e in range(D // TILE)]
    backward += [lambda: pass_on(r.PART, r.GOT2)]
    backward += [some(mlp, e, e + 1) for e in range(D // TILE)]
    backward += [mlp_out, third_rows, out_grads, attended_grads, other_out_grads]
    backward += [some(attend_back, e, e + 1) for e in range(2 * pairs)]
    backward += [fourth_rows]
    backward += [some(back_qkv, e, e + 1) for e in range(D // TILE)]
    backward += [last_out]
    backward += [some(qkv_grads, e, e + 1) for e in range(3 * half // TILE)]
    backward += [fifth_rows, some(place, 0, D // TILE), send_late]
    stages = soon.stages()
    for stage in stages[:AHEAD]:
        stage()
    each(tiles, up_grads)
    stages = stages[AHEAD:]
    cut = len(stages) * CUT // 100
    spread(stages[:cut], backward, 1, cut)
    rest, more = stages[cut:], late.stages()
    for number, chunk in enumerate(flying.sends):
        more.insert((number + 1) * ROWS_OUT - 1 if ROWS_OUT else 0, chunk)
    while rest or more:
        if more:
            more.pop(0)()
        if rest:
            rest.pop(0)()
    for gather in gathers:
        gather.drain()
    final = [to_pair(acc[k].at[me], ref) for k, ref in enumerate((r.FQ, r.FO, r.FU, r.FD))]

    def give(k, side, ref):
        value = ref[...].astype(jnp.float32)
        if k == 0:
            for j in range(3):
                r.gq[:, pl.ds(pl.multiple_of(j * D + side * half, 128), half)] = value[:, j * half : (j + 1) * half]
        elif k == 1:
            r.go[:, column(side, half, 0)] = value
        elif k == 2:
            for f in range(n):
                r.gu[:, column(2 * f + side, units, 0)] = value[:, f * units : (f + 1) * units]
        else:
            r.gd[pl.ds(pl.multiple_of(side * units, 16), units), :] = value

    for k in range(4):
        give(k, core, acc[k].at[me])
    r.gs[...] = r.As[me]
    for k, ref in enumerate((r.FQ, r.FO, r.FU, r.FD)):
        final[k].wait()
        give(k, 1 - core, ref)
    rows_wait(n, me, core, r.rows_out, r.landed, row_sems[3], row_sems[4], flying.rows)
    late.drain()
    soon.drain()


def whole_block(axes, n, cap, weights, vec, rows_in, pick, extra, notes):
    plan = first_shares(axes, 128) + second_shares(axes)
    bf, f32 = jnp.bfloat16, jnp.float32
    shards = weights
    weights = [
        jax.ShapeDtypeStruct((w.shape[0] // (2 if k == 3 else 1), w.shape[1] // (1 if k == 3 else 2)), bf)
        for k, w in enumerate(shards)
    ]
    R, F = weights[0].shape[0], weights[3].shape[0]
    vmem = pl.BlockSpec(memory_space=pltpu.VMEM)
    anywhere = pl.BlockSpec(memory_space=ANY)
    out = [jax.ShapeDtypeStruct(w.shape, f32) for w in shards]
    out += [
        jax.ShapeDtypeStruct((8, 128), f32),
        jax.ShapeDtypeStruct(rows_in.shape, bf),
        jax.ShapeDtypeStruct((2 * CAP, D), bf),
    ]
    rows = 2 * CAP
    half = D // 2
    V = pltpu.VMEM
    scratch = [V((n,) + w.shape, bf) for w in weights]
    scratch += [V((n,) + vec.shape, bf), V((n // 2, R, half), bf)]
    scratch += [V((n,) + w.shape, bf) for w in weights]
    scratch += [V((n, 8, 128), f32)] * 2
    scratch += [V((n, 2 * cap, D), bf), V((n, 2 * cap, D), bf)]
    scratch += [V((rows, D), bf)] * 3
    scratch += [V((rows, 3 * half), bf), V((HEADS, CAP, CAP), f32), V((rows, half), bf)]
    scratch += [V((rows, D), f32), V((rows, D), bf), V((rows, D), bf), V((rows, D), bf), V((CAP, D), bf), V((CAP, D), bf)]
    scratch += [V((rows, D), f32), V((rows, D), bf)]
    scratch += [V((rows, 2 * D), bf), V((rows, D), bf), V((rows, 2 * D), bf)]
    scratch += [V((rows, D), f32), V((rows, D), bf), V((rows, half), bf), V((rows, 3 * half), bf)]
    scratch += [V((CAP, D), f32), V((8, 128), f32)]
    scratch += [V(w.shape, bf) for w in weights]
    most = [1, 1, 1]
    total = 0
    deep = [R, R, R, F, 8]
    for order, parts in plan:
        total += len(parts)
        for p in parts:
            count = 1
            for phase in range(3):
                size = order[phase][1]
                kind = f32 if p.array == 4 else bf
                scratch.append(V((count, slots(size), deep[p.array], p.width), kind))
                most[phase] = max(most[phase], count * slots(size))
                count *= size
    dma = pltpu.SemaphoreType.DMA
    scratch += [dma((total, 3, 2)), dma((total, n)), dma((5,)), dma((total, 3))]
    scratch += [dma((total, m)) for m in most]
    scratch += [dma((48,))]
    return pl.pallas_call(
        functools.partial(block_kernel, axes, n, cap),
        out_shape=out,
        in_specs=[anywhere] * 6 + [vmem] * 3,
        out_specs=[vmem] * 5 + [anywhere, vmem],
        scratch_shapes=scratch,
        compiler_params=pltpu.CompilerParams(
            collective_id=2, has_side_effects=True, vmem_limit_bytes=67043328
        ),
        name="whole_block",
    )(*shards, vec, rows_in, pick, extra, notes)


def normalize(values, gain):
    inverse = lax.rsqrt(jnp.mean(values * values, axis=-1, keepdims=True) + EPSILON)
    return (values * inverse * gain, inverse)


def rms_back(values, inverse, gain, grad_normed):
    scaled = gain * grad_normed
    grad_values = inverse * scaled - values * inverse**3 * jnp.mean(
        scaled * values, axis=-1, keepdims=True
    )
    grad_gain = jnp.sum(grad_normed * values * inverse, axis=(0, 1))
    return (grad_values, grad_gain)


def split_heads(packed, offset):
    return packed[..., offset : offset + D].reshape(packed.shape[:2] + (HEADS, HEAD_DIM))


def narrow_body(
    axes,
    tokens,
    cotangent,
    w_qkv,
    w_out,
    w_up,
    w_down,
    w_router,
    gain_attn,
    gain_mlp,
    lengths,
    routed,
    dealing,
):
    factor = 1.0 / math.sqrt(HEAD_DIM)
    shards, place = lax.axis_size("fsdp"), lax.axis_index("fsdp")
    group_seqs, width = tokens.shape[1], tokens.shape[2]
    cap = min(24, width)
    slot_ids = jnp.arange(CAP, dtype=jnp.int32)
    picker = dealing[0][:, None] == jnp.arange(group_seqs, dtype=jnp.int32)[None, :]
    row_lengths = jnp.sum(jnp.where(picker, lengths[0][None, :], 0), axis=1)
    row_routes = jnp.sum(jnp.where(picker[:, :, None], routed[0][None, :, :], 0), axis=1)
    row_routes = jnp.where(slot_ids[None, :] < (row_lengths // 8)[:, None], row_routes, PAST)
    here = place * width + jnp.arange(width, dtype=jnp.int32)
    below = jnp.sum((row_routes[:, :, None] < here[None, None, :]).astype(jnp.int32), axis=1)
    upto = jnp.sum((row_routes[:, :, None] <= here[None, None, :]).astype(jnp.int32), axis=1)
    touched = upto > below
    living = here[None, :] < row_lengths[:, None]
    rank = jnp.where(touched, below - below[:, :1], -1)
    select = (rank[:, None, :] == jnp.arange(cap, dtype=jnp.int32)[None, :, None]).astype(jnp.bfloat16)
    shard_of = row_routes // width
    crowd = jnp.sum(
        (shard_of[:, :, None] == jnp.arange(shards, dtype=jnp.int32)[None, None, :]).astype(jnp.int32), axis=1
    )
    flag = jnp.broadcast_to((jnp.max(crowd) > cap).astype(jnp.float32), (8, 128))
    packed_rows = jnp.concatenate(
        [
            jnp.einsum("jip,jpd->jid", select, t[0], preferred_element_type=jnp.float32).astype(jnp.bfloat16)
            for t in (tokens, cotangent)
        ],
        axis=1,
    )
    seq_lengths = lax.dynamic_slice_in_dim(row_lengths, place, 1)
    routes = lax.dynamic_slice_in_dim(row_routes, place, 1)[0]
    valid_slot = slot_ids[None, :] < (seq_lengths // 8)[:, None]
    seq_shard = routes // width
    seq_rank = slot_ids - jnp.sum((routes[None, :] < (seq_shard * width)[:, None]).astype(jnp.int32), axis=1)
    fits = valid_slot[0] & (seq_rank < cap)
    landing = jnp.where(fits, seq_shard * (2 * cap) + seq_rank, -1)
    cells = jnp.arange(shards * 2 * cap, dtype=jnp.int32)
    pick = jnp.concatenate([landing[:, None] == cells[None, :], (landing[:, None] == (cells - cap)[None, :]) & fits[:, None]])
    pick = pick.astype(jnp.bfloat16)
    part = w_router.shape[0]
    vectors = jnp.pad(jnp.stack([w_router, gain_attn, gain_mlp]), ((0, 13), (0, 128 - part)))
    blocks = gather_all(axes, shards, [w_qkv, w_out, w_up, w_down, vectors], packed_rows, flag, 0)
    crowded = jnp.maximum(flag, blocks[6])[0, 0] > 0
    got_rows = jnp.einsum(
        "cs,sd->cd", pick, blocks[5].reshape(-1, D), preferred_element_type=jnp.float32
    ).astype(jnp.bfloat16)

    def all_rows(got):
        positions = jnp.arange(SEQ_MAX, dtype=jnp.int32)
        onehot = (routes[:, None] == positions[None, :]).astype(jnp.bfloat16)
        return jnp.concatenate(
            [
                jnp.dot(
                    onehot,
                    lax.all_to_all(t, "fsdp", split_axis=1, concat_axis=2, tiled=True)[0, 0],
                    preferred_element_type=jnp.float32,
                ).astype(jnp.bfloat16)
                for t in (tokens, cotangent)
            ]
        )

    if cap < width:
        got_rows = lax.cond(crowded, all_rows, lambda got: got, got_rows)
    rows_low = got_rows[None, :CAP]
    incoming_rows = rows_low.astype(jnp.float32)
    row_gradient = got_rows[None, CAP:].astype(jnp.float32)
    small = blocks[4][:, :3, :part].transpose(1, 0, 2).reshape(3, D)
    gathered = tuple(b.reshape(-1, b.shape[2]) for b in blocks[:4]) + (small[0], small[1], small[2])
    router_val = jnp.einsum("scd,d->sc", rows_low, gathered[4], preferred_element_type=jnp.float32)
    normed_attn, inverse_attn = normalize(incoming_rows, gathered[5].astype(jnp.float32))
    normed_low = normed_attn.astype(jnp.bfloat16)
    packed = jnp.einsum(
        "scd,de->sce", normed_low, gathered[0], preferred_element_type=jnp.float32
    ).astype(jnp.bfloat16)
    queries = split_heads(packed, 0)
    keys_heads = split_heads(packed, D)
    values_heads = split_heads(packed, 2 * D)
    scores = (
        jnp.einsum("sqhe,skhe->shqk", queries, keys_heads, preferred_element_type=jnp.float32)
        * factor
    )
    allowed = (slot_ids[None, :] <= slot_ids[:, None])[None, None] & valid_slot[:, None, None, :]
    scores = jnp.where(allowed, scores, -1e30)
    probs = jax.nn.softmax(scores, axis=-1)
    probs_low = probs.astype(jnp.bfloat16)
    attended = jnp.einsum(
        "shqk,skhe->sqhe", probs_low, values_heads, preferred_element_type=jnp.float32
    ).astype(jnp.bfloat16)
    attended = attended.reshape(incoming_rows.shape)
    branch_attn = jnp.einsum(
        "sce,ed->scd", attended, gathered[1], preferred_element_type=jnp.float32
    )
    middle = incoming_rows + branch_attn
    normed_mid, inverse_mid = normalize(middle, gathered[6].astype(jnp.float32))
    normed_mid_low = normed_mid.astype(jnp.bfloat16)
    upward = jnp.einsum(
        "scd,df->scf", normed_mid_low, gathered[2], preferred_element_type=jnp.float32
    )
    activated = jax.nn.gelu(upward).astype(jnp.bfloat16)
    branch_mlp = jnp.einsum(
        "scf,fd->scd", activated, gathered[3], preferred_element_type=jnp.float32
    )
    combined = branch_attn + branch_mlp
    refreshed_rows = (incoming_rows + router_val[..., None] * combined).astype(jnp.bfloat16)
    back_weights = gathered
    grad_comb = router_val[..., None] * row_gradient
    grad_router_val = jnp.sum(row_gradient * combined, axis=-1)
    total_gradient = row_gradient + grad_router_val[..., None] * back_weights[4].astype(jnp.float32)
    grad_mlp_low = grad_comb.astype(jnp.bfloat16)
    grad_act = jnp.einsum(
        "scd,fd->scf", grad_mlp_low, back_weights[3], preferred_element_type=jnp.float32
    )
    grad_downw = jnp.einsum(
        "scf,scd->fd", activated, grad_mlp_low, preferred_element_type=jnp.float32
    )
    unused, gelu_pull = jax.vjp(jax.nn.gelu, upward)
    grad_up_low = gelu_pull(grad_act)[0].astype(jnp.bfloat16)
    grad_normed_mid = jnp.einsum(
        "scf,df->scd", grad_up_low, back_weights[2], preferred_element_type=jnp.float32
    )
    grad_upw = jnp.einsum(
        "scd,scf->df", normed_mid_low, grad_up_low, preferred_element_type=jnp.float32
    )
    grad_middle, grad_gain_second = rms_back(
        middle, inverse_mid, back_weights[6].astype(jnp.float32), grad_normed_mid
    )
    grad_attn_low = (grad_comb + grad_middle).astype(jnp.bfloat16)
    total_gradient = total_gradient + grad_middle
    grad_attended = jnp.einsum(
        "scd,ed->sce", grad_attn_low, back_weights[1], preferred_element_type=jnp.float32
    ).astype(jnp.bfloat16)
    grad_outw = jnp.einsum(
        "sce,scd->ed", attended, grad_attn_low, preferred_element_type=jnp.float32
    )
    grad_att_heads = grad_attended.reshape(queries.shape)
    grad_probs = jnp.einsum(
        "sqhe,skhe->shqk", grad_att_heads, values_heads, preferred_element_type=jnp.float32
    )
    grad_values = jnp.einsum(
        "shqk,sqhe->skhe", probs_low, grad_att_heads, preferred_element_type=jnp.float32
    )
    grad_scores = probs * (grad_probs - jnp.sum(probs * grad_probs, axis=-1, keepdims=True))
    grad_scores_low = grad_scores.astype(jnp.bfloat16)
    grad_queries = (
        jnp.einsum(
            "shqk,skhe->sqhe", grad_scores_low, keys_heads, preferred_element_type=jnp.float32
        )
        * factor
    )
    grad_keys = (
        jnp.einsum("shqk,sqhe->skhe", grad_scores_low, queries, preferred_element_type=jnp.float32)
        * factor
    )
    flat_shape = incoming_rows.shape
    grad_packed = jnp.concatenate(
        [
            grad_queries.reshape(flat_shape),
            grad_keys.reshape(flat_shape),
            grad_values.reshape(flat_shape),
        ],
        axis=-1,
    ).astype(jnp.bfloat16)
    grad_qkvw = jnp.einsum(
        "scd,sce->de", normed_low, grad_packed, preferred_element_type=jnp.float32
    )
    grad_normed_attn = jnp.einsum(
        "sce,de->scd", grad_packed, back_weights[0], preferred_element_type=jnp.float32
    )
    grad_first_rows, grad_gain_first = rms_back(
        incoming_rows, inverse_attn, back_weights[5].astype(jnp.float32), grad_normed_attn
    )
    total_gradient = total_gradient + grad_first_rows
    grad_routerw = jnp.einsum(
        "scd,sc->d", incoming_rows, grad_router_val, precision=EXACT_PRECISION
    )
    new_rows = jnp.concatenate([refreshed_rows[0], total_gradient[0].astype(jnp.bfloat16)])
    sent_rows = (
        jnp.einsum("cs,cd->sd", pick, new_rows, preferred_element_type=jnp.float32)
        .astype(jnp.bfloat16)
        .reshape(shards, 2 * cap, D)
    )
    small_grads = jnp.stack([grad_routerw, grad_gain_first, grad_gain_second])
    small_grads = small_grads.reshape(3, shards, part).transpose(1, 0, 2)
    small_grads = jnp.pad(small_grads, ((0, 0), (0, 5), (0, 128 - part)))
    partial = [
        g.astype(jnp.bfloat16).reshape(shards, -1, g.shape[1])
        for g in (grad_qkvw, grad_outw, grad_upw, grad_downw)
    ]
    shares = scatter_all(axes, shards, partial + [small_grads], sent_rows, 1)
    totals = tuple(t.astype(jnp.float32) for t in shares[:4]) + tuple(shares[4][j, :part] for j in range(3))
    def place_rows(rows, held):
        spread = jnp.einsum("jip,jid->jpd", select, rows, preferred_element_type=jnp.float32).astype(jnp.bfloat16)
        kept = jnp.where(touched[..., None], spread, held[0])
        return jnp.where(living[..., None], kept, jnp.zeros_like(kept))[None]

    def compact(landed, rows):
        return place_rows(landed[:, :cap], tokens), place_rows(landed[:, cap:], cotangent)

    def entire(landed, rows):
        positions = jnp.arange(SEQ_MAX, dtype=jnp.int32)
        onehot = (routes[:, None] == positions[None, :]).astype(jnp.bfloat16)
        placed = []
        for r, held in ((rows[:CAP], tokens), (rows[CAP:], cotangent)):
            spread = jnp.einsum("cp,cd->pd", onehot, r, preferred_element_type=jnp.float32)
            spread = lax.all_to_all(
                spread.astype(jnp.bfloat16)[None, None], "fsdp", split_axis=2, concat_axis=1, tiled=True
            )
            kept = jnp.where(touched[..., None], spread[0], held[0])
            placed.append(jnp.where(living[..., None], kept, jnp.zeros_like(kept))[None])
        return tuple(placed)

    if cap < width:
        back_out, back_grad = lax.cond(crowded, entire, compact, shares[5], new_rows)
    else:
        back_out, back_grad = compact(shares[5], new_rows)
    return (
        back_out,
        back_grad,
        totals[0],
        totals[1],
        totals[2],
        totals[3],
        totals[4],
        totals[5],
        totals[6],
    )


def wide_body(
    axes,
    tokens,
    cotangent,
    w_qkv,
    w_out,
    w_up,
    w_down,
    w_router,
    gain_attn,
    gain_mlp,
    lengths,
    routed,
    dealing,
):
    factor = 1.0 / math.sqrt(HEAD_DIM)
    shards, place = lax.axis_size("fsdp"), lax.axis_index("fsdp")
    group_seqs, width = tokens.shape[1], tokens.shape[2]
    cap = min(24, width)
    slot_ids = jnp.arange(CAP, dtype=jnp.int32)
    picker = dealing[0][:, None] == jnp.arange(group_seqs, dtype=jnp.int32)[None, :]
    row_lengths = jnp.sum(jnp.where(picker, lengths[0][None, :], 0), axis=1)
    row_routes = jnp.sum(jnp.where(picker[:, :, None], routed[0][None, :, :], 0), axis=1)
    row_routes = jnp.where(slot_ids[None, :] < (row_lengths // 8)[:, None], row_routes, PAST)
    here = place * width + jnp.arange(width, dtype=jnp.int32)
    below = jnp.sum((row_routes[:, :, None] < here[None, None, :]).astype(jnp.int32), axis=1)
    upto = jnp.sum((row_routes[:, :, None] <= here[None, None, :]).astype(jnp.int32), axis=1)
    touched = upto > below
    living = here[None, :] < row_lengths[:, None]
    rank = jnp.where(touched, below - below[:, :1], -1)
    select = (rank[:, None, :] == jnp.arange(cap, dtype=jnp.int32)[None, :, None]).astype(jnp.bfloat16)
    shard_of = row_routes // width
    crowd = jnp.sum(
        (shard_of[:, :, None] == jnp.arange(shards, dtype=jnp.int32)[None, None, :]).astype(jnp.int32), axis=1
    )
    flag = jnp.broadcast_to((jnp.max(crowd) > cap).astype(jnp.float32), (8, 128))
    packed_rows = jnp.concatenate(
        [
            jnp.einsum("jip,jpd->jid", select, t[0], preferred_element_type=jnp.float32).astype(jnp.bfloat16)
            for t in (tokens, cotangent)
        ],
        axis=1,
    )
    seq_lengths = lax.dynamic_slice_in_dim(row_lengths, place, 1)
    routes = lax.dynamic_slice_in_dim(row_routes, place, 1)[0]
    valid_slot = slot_ids[None, :] < (seq_lengths // 8)[:, None]
    seq_shard = routes // width
    seq_rank = slot_ids - jnp.sum((routes[None, :] < (seq_shard * width)[:, None]).astype(jnp.int32), axis=1)
    fits = valid_slot[0] & (seq_rank < cap)
    landing = jnp.where(fits, seq_shard * (2 * cap) + seq_rank, -1)
    cells = jnp.arange(shards * 2 * cap, dtype=jnp.int32)
    pick = jnp.concatenate([landing[:, None] == cells[None, :], (landing[:, None] == (cells - cap)[None, :]) & fits[:, None]])
    pick = pick.astype(jnp.bfloat16)
    part = w_router.shape[0]
    mine = jnp.max(flag)
    other = lax.ppermute(flag, "rep", [(0, 1), (1, 0)])
    crowded = jnp.maximum(mine, jnp.max(other)) > 0
    ring = [(i, (i + 1) % shards) for i in range(shards)]

    def chosen(j):
        return (lax.dynamic_index_in_dim(row_routes, j, 0, keepdims=False)[:, None] == here[None, :]).astype(jnp.bfloat16)

    def all_rows():
        def go(i, rows):
            j = (place - 1 - i) % shards
            mine = [
                jnp.dot(chosen(j), lax.dynamic_index_in_dim(t[0], j, 0, keepdims=False), preferred_element_type=jnp.float32)
                for t in (tokens, cotangent)
            ]
            return lax.ppermute(rows, "fsdp", ring) + jnp.concatenate(mine).astype(jnp.bfloat16)

        return lax.fori_loop(0, shards, go, jnp.zeros((2 * CAP, D), jnp.bfloat16))

    extra = jnp.zeros((2 * CAP, D), jnp.bfloat16)
    if cap < width:
        extra = lax.cond(crowded, all_rows, lambda: jnp.zeros((2 * CAP, D), jnp.bfloat16))
        pick = jnp.where(crowded, jnp.zeros_like(pick), pick)
    weights = [w_qkv, w_out, w_up, w_down]
    lanes = (place * part) % 128
    vectors = jnp.pad(jnp.stack([w_router, gain_attn, gain_mlp]), ((0, 13), (0, 0)))
    vectors = lax.dynamic_update_slice(jnp.zeros((16, 128), jnp.bfloat16), vectors, (0, lanes))
    notes = jnp.broadcast_to(valid_slot.astype(jnp.float32), (8, CAP))
    gq, go, gu, gd, gs, landed, new_rows = whole_block(
        axes, shards, cap, weights, vectors, packed_rows, pick, extra, notes
    )
    small = lax.dynamic_slice(gs, (0, lanes), (8, part))
    totals = (gq, go, gu, gd, small[0], small[1], small[2])

    def place_rows(rows, held):
        spread = jnp.einsum("jip,jid->jpd", select, rows, preferred_element_type=jnp.float32).astype(jnp.bfloat16)
        kept = jnp.where(touched[..., None], spread, held[0])
        return jnp.where(living[..., None], kept, jnp.zeros_like(kept))[None]

    def compact(landed, rows):
        return place_rows(landed[:, :cap], tokens), place_rows(landed[:, cap:], cotangent)

    def entire(landed, rows):
        def go(i, held):
            rows, placed = held
            j = (place - i) % shards
            done = []
            for k, (t, whole) in enumerate(zip((tokens, cotangent), placed)):
                spread = jnp.einsum(
                    "cp,cd->pd", chosen(j), rows[k * CAP : k * CAP + CAP], preferred_element_type=jnp.float32
                ).astype(jnp.bfloat16)
                kept = jnp.where(lax.dynamic_index_in_dim(touched, j, 0, keepdims=False)[:, None], spread, t[0, j])
                kept = jnp.where(lax.dynamic_index_in_dim(living, j, 0, keepdims=False)[:, None], kept, jnp.zeros_like(kept))
                done.append(lax.dynamic_update_slice(whole, kept[None, None], (0, j, 0, 0)))
            return lax.ppermute(rows, "fsdp", ring), tuple(done)

        return lax.fori_loop(0, shards, go, (rows, (jnp.zeros_like(tokens), jnp.zeros_like(cotangent))))[1]

    if cap < width:
        back_out, back_grad = lax.cond(crowded, entire, compact, landed, new_rows)
    else:
        back_out, back_grad = compact(landed, new_rows)
    return (
        back_out,
        back_grad,
        totals[0],
        totals[1],
        totals[2],
        totals[3],
        totals[4],
        totals[5],
        totals[6],
    )


def body(axes, *arrays):
    run = wide_body if arrays[2].shape[0] % 16 == 0 else narrow_body
    return run(axes, *arrays)


def solution(mesh):
    placed = (
        P("rep", None, "fsdp", None),
        P("rep", None, "fsdp", None),
        P("fsdp", None),
        P("fsdp", None),
        P("fsdp", None),
        P("fsdp", None),
        P("fsdp"),
        P("fsdp"),
        P("fsdp"),
        P("rep", None),
        P("rep", None, None),
        P("rep", None),
    )
    return jax.shard_map(
        functools.partial(body, grid_axes(mesh)),
        mesh=mesh,
        in_specs=placed,
        out_specs=(
            P("rep", None, "fsdp", None),
            P("rep", None, "fsdp", None),
            P("fsdp", None),
            P("fsdp", None),
            P("fsdp", None),
            P("fsdp", None),
            P("fsdp"),
            P("fsdp"),
            P("fsdp"),
        ),
        check_vma=False,
    )
```

```python
import math
import functools

import jax
import jax.numpy as jnp
from jax import lax
from jax.experimental import pallas as pl
from jax.experimental.pallas import tpu as pltpu
from jax.sharding import PartitionSpec as P

D = 1024
HEADS = 16
HEAD_DIM = 64
SEQ_MAX = 1024
CAP = 128
PAST = 1 << 24


EPSILON = 1e-06
EXACT_PRECISION = lax.Precision.HIGHEST

MESH = pl.DeviceIdType.MESH
ANY = pl.ANY


def grid_axes(mesh):
    devices = mesh.devices[:, 0]
    count = len(devices)
    axes = []
    spots = [getattr(d, "coords", None) for d in devices]
    if all(s is not None for s in spots) and len(set(map(tuple, spots))) == count:
        low = [min(s[k] for s in spots) for k in range(3)]
        at = {tuple(s[k] - low[k] for k in range(3)): f for f, s in enumerate(spots)}
        for k in range(3):
            size = max(s[k] for s in spots) - low[k] + 1
            one = tuple(int(j == k) for j in range(3))
            axes.append((at[one] if size > 1 else 1, size, k))
        ok = all(
            f == sum(stride * spot[k] for stride, _, k in axes) for spot, f in at.items()
        )
        axes = [a[:2] for a in axes] if ok else []
    if not axes:
        axes, left = [], count
        for size in (2, 2):
            size = size if left % size == 0 and left > 1 else 1
            axes.append((count // left, size))
            left //= size
        axes.append((count // left, left))
    return sorted(axes, key=lambda a: -a[1])


def xor(a, b, size):
    out, bit = 0, 1
    while bit < size:
        out = out + ((a // bit + b // bit) % 2) * bit
        bit *= 2
    return out


class Piece:
    def __init__(self, array, half, offset, width):
        self.array, self.half, self.offset, self.width = array, half, offset, width

    def cols(self, core):
        start = self.offset
        if self.half:
            start = core * self.half + start
            start = pl.multiple_of(start, 128)
        return pl.ds(start, self.width)


def colours(axes, widths):
    qkv, out, up, down = (w // 2 for w in widths[:4])
    a, b, c = axes
    third = qkv // 3
    return [
        ((b, c, a), [Piece(1, out, 0, out), Piece(4, 0, 0, widths[4])]),
        ((c, b, a), [Piece(0, qkv, 0, third)]),
        ((a, b, c), [Piece(2, up, 0, up), Piece(0, qkv, third, third)]),
        ((a, c, b), [Piece(3, down, 0, down), Piece(0, qkv, 2 * third, third)]),
    ]


def enter(n, me, core):
    barrier = pltpu.get_barrier_semaphore()

    def hello(i, _):
        pl.semaphore_signal(barrier, inc=1, device_id=((me + i) % n, core), device_id_type=MESH)
        return 0

    lax.fori_loop(1, n, hello, 0)
    pl.semaphore_signal(barrier, inc=1, device_id=(me, 1 - core), device_id_type=MESH)
    pl.semaphore_wait(barrier, n)


def rows_out(n, me, core, rows, landing, send_sem, recv_sem, own_sem):
    own = pltpu.make_async_copy(rows.at[me], landing.at[me], own_sem)
    own.start()

    def go(i, _):
        to = (me + i) % n
        pltpu.make_async_remote_copy(
            src_ref=rows.at[to], dst_ref=landing.at[me], send_sem=send_sem, recv_sem=recv_sem,
            device_id=(to, core), device_id_type=MESH,
        ).start()
        return 0

    lax.fori_loop(1, n, go, 0)
    return own


def rows_each(n, me, core, rows, landing, send_sem, recv_sem, own_sem):
    own = pltpu.make_async_copy(rows.at[me], landing.at[me], own_sem)
    own.start()

    def go(i):
        to = (me + i) % n
        pltpu.make_async_remote_copy(
            src_ref=rows.at[to], dst_ref=landing.at[me], send_sem=send_sem, recv_sem=recv_sem,
            device_id=(to, core), device_id_type=MESH,
        ).start()

    return own, [functools.partial(go, i) for i in (ORDER or range(1, n))]


def rows_wait(n, me, core, rows, landing, send_sem, recv_sem, own):
    own.wait()
    for which in range(2):
        copy = pltpu.make_async_remote_copy(
            src_ref=rows.at[pl.ds(0, n - 1)], dst_ref=landing.at[pl.ds(0, n - 1)],
            send_sem=send_sem, recv_sem=recv_sem, device_id=(me, 1 - core), device_id_type=MESH,
        )
        copy.wait_recv() if which else copy.wait_send()


def gather_kernel(axes, plan, n, *refs):
    k = 5
    ins, rows, flag = refs[:k], refs[k], refs[k + 1]
    outs, landing, other = refs[k + 2 : 2 * k + 2], refs[2 * k + 2], refs[2 * k + 3]
    stages = refs[2 * k + 4 : 3 * k + 4]
    send_sem, recv_sem, pair_send, pair_recv, local_sem, row_sems = refs[3 * k + 4 :]
    me, core = lax.axis_index("fsdp"), lax.axis_index("rep")
    enter(n, me, core)
    told = pltpu.make_async_remote_copy(
        src_ref=flag, dst_ref=other, send_sem=row_sems.at[3], recv_sem=row_sems.at[4],
        device_id=(me, 1 - core), device_id_type=MESH,
    )
    told.start()
    numbered, number = [], 0
    for order, pieces in plan:
        numbered.append((order, [(number + i, p) for i, p in enumerate(pieces)]))
        number += len(pieces)

    def spot(axis):
        return (me // axis[0]) % axis[1]

    def dst(piece, block):
        return outs[piece.array].at[block, :, piece.cols(core)]

    def put(pieces, block, own, phase, way, device, pair=False):
        for i, piece in pieces:
            if pair and not piece.half:
                continue
            src = ins[piece.array].at[:, piece.cols(core)] if own else dst(piece, block)
            pltpu.make_async_remote_copy(
                src_ref=src,
                dst_ref=dst(piece, block),
                send_sem=pair_send.at[i] if pair else send_sem.at[i, phase, way],
                recv_sem=pair_recv.at[i] if pair else recv_sem.at[i, block],
                device_id=device,
                device_id_type=MESH,
            ).start()

    def along(pieces, order, block, own, phase, ways):
        stride, size = order[phase]
        at = spot(order[phase])
        if size == 1:
            return
        if size == 2:
            put(pieces, block, own, phase, 0, (me + (1 - 2 * at) * stride, core))
            return
        for way in ways:
            step = 1 - 2 * way
            pl.when(at < size - 1 if way == 0 else at > 0)(
                functools.partial(put, pieces, block, own, phase, way, (me + step * stride, core))
            )

    def arrived(pieces, order, block, phase, way):
        for i, piece in pieces:
            pltpu.make_async_remote_copy(
                src_ref=dst(piece, block),
                dst_ref=dst(piece, block),
                send_sem=send_sem.at[i, phase, way],
                recv_sem=recv_sem.at[i, block],
                device_id=(me, 1 - core),
                device_id_type=MESH,
            ).wait_recv()
        if order[phase][1] > 2:
            along(pieces, order, block, False, phase, (way,))
        for later in range(phase + 1, 3):
            along(pieces, order, block, False, later, (0, 1))
        put(pieces, block, False, 0, 0, (me, 1 - core), pair=True)

    for order, pieces in numbered:
        for phase in range(3):
            along(pieces, order, me, True, phase, (0, 1))
    own = rows_out(n, me, core, rows, landing, row_sems.at[0], row_sems.at[1], row_sems.at[2])
    local = []
    for j in range(k):
        local.append(pltpu.make_async_copy(ins[j], stages[j], local_sem.at[j]))
        local[-1].start()
    events = []
    for number, (order, pieces) in enumerate(numbered):
        heavy = number >= 2
        sizes = [a[1] for a in order]
        for phase in range(3):
            size = sizes[phase]
            rest = 1
            for s in sizes[:phase]:
                rest *= s
            for t in range(1, size):
                ways = (0,) if size == 2 else (0, 1)
                for way in ways:
                    for j in range(rest):
                        if heavy:
                            key = 20 * t if phase == 0 else 20 * phase + 20 * (j + (t - 1) * rest + 1)
                        else:
                            key = 5 if phase == 0 else 10 + 5 * j if phase == 1 else 15 + 40 * t + 5 * j
                        events.append((key, len(events), order, pieces, phase, t, way, j))
    events.sort(key=lambda e: e[:2])

    def run(order, pieces, phase, t, way, j):
        stride, size = order[phase]
        at = spot(order[phase])
        origin = 1 - at if size == 2 else at - (1 - 2 * way) * t
        block = me + (origin - at) * stride
        for s, z in order[:phase]:
            here = (me // s) % z
            block = block + (xor(here, j % z, z) - here) * s
            j = j // z
        if size == 2:
            arrived(pieces, order, block, phase, 0)
        else:
            pl.when((origin >= 0) & (origin < size))(
                functools.partial(arrived, pieces, order, block, phase, way)
            )

    def settle():
        for j in range(k):
            local[j].wait()
            local[j] = pltpu.make_async_copy(stages[j], outs[j].at[me], local_sem.at[j])
            local[j].start()

    for number, (_, _, order, pieces, phase, t, way, j) in enumerate(events):
        run(order, pieces, phase, t, way, j)
        if number == 3:
            settle()
    for copy in local:
        copy.wait()
    told.wait()
    rows_wait(n, me, core, rows, landing, row_sems.at[0], row_sems.at[1], own)

    def drain(i, piece, count, send, recv, which):
        many = outs[piece.array].at[pl.ds(0, count), :, piece.cols(core)]
        copy = pltpu.make_async_remote_copy(
            src_ref=many, dst_ref=many, send_sem=send, recv_sem=recv,
            device_id=(me, 1 - core), device_id_type=MESH,
        )
        if which == "send":
            copy.wait_send()
        else:
            copy.wait_recv()

    for order, pieces in numbered:
        rest = 1
        for phase in range(3):
            stride, size = order[phase]
            at = spot(order[phase])
            for i, piece in pieces:
                if size == 2:
                    drain(i, piece, rest, send_sem.at[i, phase, 0], recv_sem.at[i, 0], "send")
                elif size > 2:
                    for here in range(size):
                        def both(here=here, i=i, piece=piece, phase=phase, rest=rest, size=size):
                            if here < size - 1:
                                drain(i, piece, (here + 1) * rest, send_sem.at[i, phase, 0], recv_sem.at[i, 0], "send")
                            if here > 0:
                                drain(i, piece, (size - here) * rest, send_sem.at[i, phase, 1], recv_sem.at[i, 0], "send")
                        pl.when(at == here)(both)
            rest *= size
        for i, piece in pieces:
            if piece.half:
                drain(i, piece, n - 1, pair_send.at[i], pair_recv.at[i], "send")
                drain(i, piece, n - 1, pair_send.at[i], pair_recv.at[i], "recv")


def gather_all(axes, n, arrays, rows, flag, collective_id):
    plan = colours(axes, [a.shape[1] for a in arrays])
    pieces = sum(len(p) for _, p in plan)
    vmem = pl.BlockSpec(memory_space=pltpu.VMEM)
    anywhere = pl.BlockSpec(memory_space=ANY)
    dma = pltpu.SemaphoreType.DMA
    return pl.pallas_call(
        functools.partial(gather_kernel, axes, plan, n),
        out_shape=[jax.ShapeDtypeStruct((n,) + a.shape, a.dtype) for a in arrays]
        + [jax.ShapeDtypeStruct(a.shape, a.dtype) for a in (rows, flag)],
        in_specs=[anywhere] * len(arrays) + [vmem, vmem],
        out_specs=[anywhere] * (len(arrays) + 1) + [vmem],
        scratch_shapes=[pltpu.VMEM(a.shape, a.dtype) for a in arrays]
        + [dma((pieces, 3, 2)), dma((pieces, n)), dma((pieces,)), dma((pieces,)), dma((len(arrays),)), dma((5,))],
        compiler_params=pltpu.CompilerParams(collective_id=collective_id, has_side_effects=True),
        name="gather_all",
    )(*arrays, rows, flag)
def add_into(acc, a, got, g, rows):
    step = min(rows, 16)

    def go(i, _):
        at = pl.ds(pl.multiple_of(i * step, step), step)
        acc[a, at, :] = (acc[a, at, :].astype(jnp.float32) + got[g, at, :].astype(jnp.float32)).astype(acc.dtype)
        return 0

    lax.fori_loop(0, rows // step, go, 0)


def turn(at, t, size):
    if size == 2:
        return at + (1 - 2 * at) * (1 - t)
    up = size - 1 - at
    first_up = jnp.where(t < up, size - 1 - t, t - up)
    first_down = jnp.where(t < at, t, size - 1 - (t - at))
    return jnp.where(t == size - 1, at, jnp.where(2 * at < size, first_up, first_down))


def slots(size):
    return 1 if size <= 2 else size + 1


def scatter_kernel(axes, plan, n, *refs):
    k = 5
    ins, rows, outs, landing = refs[:k], refs[k], refs[k + 1 : 2 * k + 1], refs[2 * k + 1]
    total = sum(len(p) for _, p in plan)
    buffers = refs[2 * k + 2 : 2 * k + 2 + 5 * total]
    own_sem, pair_send, pair_recv, send_sem = refs[-10:-6]
    recv_sems, last_send, last_recv, row_sems = refs[-6:-3], refs[-3], refs[-2], refs[-1]
    me, core = lax.axis_index("fsdp"), lax.axis_index("rep")
    enter(n, me, core)
    numbered, number = [], 0
    for order, pieces in plan:
        numbered.append((order, [(number + i, p) for i, p in enumerate(pieces)]))
        number += len(pieces)
    acc = [buffers[5 * i] for i in range(total)]
    pair = [buffers[5 * i + 1] for i in range(total)]
    got = [buffers[5 * i + 2 : 5 * i + 5] for i in range(total)]

    def spot(axis):
        return (me // axis[0]) % axis[1]

    def pair_copy(i, piece, block):
        return pltpu.make_async_remote_copy(
            src_ref=ins[piece.array].at[block, :, piece.cols(1 - core)],
            dst_ref=pair[i].at[block],
            send_sem=pair_send.at[i],
            recv_sem=pair_recv.at[i, block],
            device_id=(me, 1 - core),
            device_id_type=MESH,
        )

    def own_copy(i, piece, block):
        return pltpu.make_async_copy(
            ins[piece.array].at[block, :, piece.cols(core)], acc[i].at[block], own_sem.at[i, block]
        )

    def block_at(order, phase, origin, turns):
        block = me + (origin - spot(order[phase])) * order[phase][0]
        for axis, t in zip(order[:phase], turns):
            block = block + (turn(spot(axis), t, axis[1]) - spot(axis)) * axis[0]
        return block

    def ready(pieces, block):
        for i, piece in pieces:
            own_copy(i, piece, block).wait()
            pair_copy(i, piece, block).wait_recv()
            add_into(acc[i], block, pair[i], block, acc[i].shape[1])

    def hop(i, phase, block, rest, slot, send, device):
        return pltpu.make_async_remote_copy(
            src_ref=acc[i].at[block],
            dst_ref=got[i][phase].at[rest, slot],
            send_sem=send,
            recv_sem=recv_sems[phase].at[i, rest * got[i][phase].shape[1] + slot],
            device_id=device,
            device_id_type=MESH,
        )

    def take(pieces, phase, block, rest, slot):
        for i, piece in pieces:
            hop(i, phase, block, rest, slot, send_sem.at[i, phase], (me, 1 - core)).wait_recv()
            add_into(acc[i], block, got[i][phase].at[rest], slot, acc[i].shape[1])

    def give(pieces, phase, block, rest, slot, device):
        for i, piece in pieces:
            hop(i, phase, block, rest, slot, send_sem.at[i, phase], device).start()

    def event(order, pieces, phase, t, turns, first):
        stride, size = order[phase]
        at = spot(order[phase])
        origin = turn(at, t, size)
        mine = t == size - 1
        block = block_at(order, phase, origin, turns)
        rest = 0
        for axis, away in zip(order[:phase], turns):
            rest = rest * axis[1] + away
        if first:
            ready(pieces, block)
        if size == 1:
            return
        if size == 2:
            pl.when(jnp.logical_not(mine))(
                lambda: give(pieces, phase, block, rest, 0, (me + (1 - 2 * at) * stride, core))
            )
            pl.when(mine)(lambda: take(pieces, phase, block, rest, 0))
            return

        @pl.when(jnp.logical_not(mine))
        def _():
            up = (origin > at).astype(jnp.int32)
            behind = jnp.where(up == 1, at > 0, at < size - 1)
            pl.when(behind)(lambda: take(pieces, phase, block, rest, origin))
            step = 2 * up - 1
            landing = jnp.where((up == 0) & (origin == at - 1), size, origin)
            give(pieces, phase, block, rest, landing, (me + step * stride, core))

        @pl.when(mine)
        def _():
            pl.when(at > 0)(lambda: take(pieces, phase, block, rest, at))
            pl.when(at < size - 1)(lambda: take(pieces, phase, block, rest, size))

    def each(count, fn):
        lax.fori_loop(0, count, lambda e, _: (fn(e), 0)[1], 0)

    def begin(order, pieces, s):
        _, (_, nq), (_, nr) = order

        def go(e):
            block = block_at(order, 2, turn(spot(order[2]), e // nq, nr), (s, e % nq))
            for i, piece in pieces:
                pair_copy(i, piece, block).start()
                own_copy(i, piece, block).start()

        each(nr * nq, go)

    def lead(order, pieces, s):
        _, (_, nq), (_, nr) = order
        each((nr - 1) * nq, lambda e: event(order, pieces, 2, e // nq, (s, e % nq), True))

    def later(order, pieces, s, low, high):
        def go(e):
            event(order, pieces, 2, order[2][1] - 1, (s, low + e), True)
            event(order, pieces, 1, low + e, (s,), False)

        each(high - low, go)

    def finish(order, pieces, s):
        event(order, pieces, 0, s, (), False)

    light, heavy = numbered[:2], numbered[2:]
    steps, few = heavy[0][0][0][1], max(c[0][0][1] for c in light)

    def begin_all(s):
        for colour in heavy:
            pl.when(s < steps)(lambda colour=colour: begin(*colour, s))
        for colour in light:
            pl.when(s < colour[0][0][1])(lambda colour=colour: begin(*colour, s))

    each(max(steps, few), begin_all)
    own = rows_out(n, me, core, rows, landing, row_sems.at[0], row_sems.at[1], row_sems.at[2])
    for colour in heavy + light:
        lead(*colour, 0)

    def step(s):
        for colour in heavy:
            pl.when(s < steps)(lambda colour=colour: later(*colour, s, 0, 1))
        for colour in heavy:
            pl.when(s + 1 < steps)(lambda colour=colour: lead(*colour, s + 1))
        for colour in heavy:
            pl.when((s >= 1) & (s < steps))(lambda colour=colour: finish(*colour, s - 1))
        for colour in light:
            size = colour[0][0][1]
            pl.when(s + 1 < size)(lambda colour=colour: lead(*colour, s + 1))
        for colour in heavy:
            pl.when(s < steps)(lambda colour=colour: later(*colour, s, 1, colour[0][1][1]))
        for colour in light:
            size = colour[0][0][1]

            @pl.when((s >= 1) & (s <= size))
            def _(colour=colour):
                later(*colour, s - 1, 0, colour[0][1][1])
                finish(*colour, s - 1)
        for colour in heavy:
            pl.when(s == steps - 1)(lambda colour=colour: finish(*colour, s))

    each(max(steps, few + 1), step)

    final = []
    for order, pieces in numbered:
        for i, piece in pieces:
            outs[piece.array][:, piece.cols(core)] = acc[i][me]
            if piece.half:
                final.append(
                    pltpu.make_async_remote_copy(
                        src_ref=acc[i].at[me],
                        dst_ref=outs[piece.array].at[:, piece.cols(core)],
                        send_sem=last_send.at[i],
                        recv_sem=last_recv.at[i],
                        device_id=(me, 1 - core),
                        device_id_type=MESH,
                    )
                )
                final[-1].start()
    for copy in final:
        copy.wait()
    rows_wait(n, me, core, rows, landing, row_sems.at[0], row_sems.at[1], own)

    def drain(i, phase, count):
        many = acc[i].at[pl.ds(0, count)]
        pltpu.make_async_remote_copy(
            src_ref=many, dst_ref=many, send_sem=send_sem.at[i, phase], recv_sem=last_recv.at[i],
            device_id=(me, 1 - core), device_id_type=MESH,
        ).wait_send()

    for order, pieces in numbered:
        for i, piece in pieces:
            for phase in range(3):
                if order[phase][1] > 1:
                    count = order[phase][1] - 1
                    for axis in order[:phase]:
                        count *= axis[1]
                    drain(i, phase, count)
            many = acc[i].at[pl.ds(0, n)]
            pltpu.make_async_remote_copy(
                src_ref=many, dst_ref=many, send_sem=pair_send.at[i], recv_sem=last_recv.at[i],
                device_id=(me, 1 - core), device_id_type=MESH,
            ).wait_send()


def scatter_all(axes, n, arrays, rows, collective_id):
    plan = colours(axes, [a.shape[2] for a in arrays])
    pieces = [(order, p) for order, ps in plan for p in ps]
    scratch = []
    for order, p in pieces:
        deep, dtype = arrays[p.array].shape[1], arrays[p.array].dtype
        scratch += [pltpu.VMEM((n, deep, p.width), dtype)] * 2
        count = 1
        for phase in range(3):
            size = order[phase][1]
            scratch.append(pltpu.VMEM((count, slots(size), deep, p.width), dtype))
            count *= size
    total = len(pieces)
    shapes = []
    for phase in range(3):
        most = 1
        for order, _ in plan:
            count = slots(order[phase][1])
            for a in order[:phase]:
                count *= a[1]
            most = max(most, count)
        shapes.append((total, most))
    dma = pltpu.SemaphoreType.DMA
    return pl.pallas_call(
        functools.partial(scatter_kernel, axes, plan, n),
        out_shape=[jax.ShapeDtypeStruct(a.shape[1:], a.dtype) for a in arrays]
        + [jax.ShapeDtypeStruct(rows.shape, rows.dtype)],
        in_specs=[pl.BlockSpec(memory_space=ANY)] * len(arrays) + [pl.BlockSpec(memory_space=pltpu.VMEM)],
        out_specs=[pl.BlockSpec(memory_space=pltpu.VMEM)] * len(arrays) + [pl.BlockSpec(memory_space=ANY)],
        scratch_shapes=scratch
        + [dma((total, n)), dma((total,)), dma((total, n)), dma((total, 3))]
        + [dma(s) for s in shapes]
        + [dma((total,)), dma((total,)), dma((3,))],
        compiler_params=pltpu.CompilerParams(
            collective_id=collective_id, has_side_effects=True, vmem_limit_bytes=60 * 1024 * 1024
        ),
        name="scatter_all",
    )(*arrays, rows)


SQRT_2_PI = math.sqrt(2.0 / math.pi)
NN = (((1,), (0,)), ((), ()))
NT = (((1,), (1,)), ((), ()))
TN = (((0,), (0,)), ((), ()))


def mm(a, b, dims=NN):
    return lax.dot_general(a, b, dims, preferred_element_type=jnp.float32)


def each(count, fn):
    lax.fori_loop(0, count, lambda e, _: (fn(e), 0)[1], 0)


class Part:
    def __init__(self, array, offset, width):
        self.array, self.offset, self.width = array, offset, width

    def of(self, ref, block):
        return ref.at[block, :, pl.ds(self.offset, self.width)]


EARLY, AT0, AT1, CUT, SPLIT = 30, 4, 85, 45, False
AHEAD = 1
ROWS_IN, ROWS_OUT, ORDER = (0, 100), 5, ()


def first_shares(axes, vectors):
    a, b, c = axes
    half = D // 2
    return [
        ((b, c, a), [Part(1, 0, D // 4), Part(4, 0, vectors)]),
        ((c, b, a), [Part(0, 0, D // 4)]),
        ((a, b, c), [Part(0, D // 4, half + D // 4)]),
        ((a, c, b), [Part(0, D, half), Part(1, D // 4, D // 4)]),
    ]


def second_shares(axes):
    a, b, c = axes
    return [
        ((b, c, a), [Part(2, 0, 3 * D // 8)]),
        ((c, b, a), [Part(3, 0, D // 4)]),
        ((a, b, c), [Part(2, 3 * D // 8, 13 * D // 8)]),
        ((a, c, b), [Part(3, D // 4, 3 * D // 4)]),
    ]


def number_parts(plan):
    numbered, number = [], 0
    for order, parts in plan:
        numbered.append((order, [(number + i, p) for i, p in enumerate(parts)]))
        number += len(parts)
    return numbered


def send(src, dst, send_sem, recv_sem, device):
    return pltpu.make_async_remote_copy(
        src_ref=src, dst_ref=dst, send_sem=send_sem, recv_sem=recv_sem, device_id=device, device_id_type=MESH
    )


class Gather:
    def __init__(self, n, me, core, numbered, whole, sems):
        self.n, self.me, self.core, self.numbered, self.whole = n, me, core, numbered, whole
        self.send_sem, self.recv_sem = sems

    def spot(self, axis):
        return (self.me // axis[0]) % axis[1]

    def put(self, parts, block, phase, way, step):
        for i, part in parts:
            dst = part.of(self.whole[part.array], block)
            send(
                dst, dst, self.send_sem.at[i, phase, way], self.recv_sem.at[i, block], (self.me + step, self.core)
            ).start()

    def along(self, parts, order, block, phase, ways):
        stride, size = order[phase]
        at = self.spot(order[phase])
        if size == 2:
            self.put(parts, block, phase, 0, (1 - 2 * at) * stride)
        elif size > 2:
            for way in ways:
                step = (1 - 2 * way) * stride
                pl.when(at < size - 1 if way == 0 else at > 0)(
                    functools.partial(self.put, parts, block, phase, way, step)
                )

    def arrived(self, parts, order, block, phase, way):
        for i, part in parts:
            dst = part.of(self.whole[part.array], block)
            send(
                dst, dst, self.send_sem.at[i, phase, way], self.recv_sem.at[i, block], (self.me, 1 - self.core)
            ).wait_recv()
        if order[phase][1] > 2:
            self.along(parts, order, block, phase, (way,))
        for later in range(phase + 1, 3):
            self.along(parts, order, block, later, (0, 1))

    def start(self):
        for order, parts in self.numbered:
            for phase in range(3):
                self.along(parts, order, self.me, phase, (0, 1))

    def events(self):
        found = []
        for number, (order, parts) in enumerate(self.numbered):
            heavy = number >= 2
            sizes = [a[1] for a in order]
            for phase in range(3):
                size, rest = sizes[phase], math.prod(sizes[:phase])
                for t in range(1, size):
                    for way in (0,) if size == 2 else (0, 1):
                        for j in range(rest):
                            if heavy:
                                key = 20 * t if phase == 0 else 20 * phase + 20 * (j + (t - 1) * rest + 1)
                            else:
                                key = 5 if phase == 0 else 10 + 5 * j if phase == 1 else 15 + 40 * t + 5 * j
                            found.append((key, len(found), order, parts, phase, t, way, j))
        found.sort(key=lambda e: e[:2])
        return [functools.partial(self.run, *e[2:]) for e in found]

    def run(self, order, parts, phase, t, way, j):
        stride, size = order[phase]
        at = self.spot(order[phase])
        origin = 1 - at if size == 2 else at - (1 - 2 * way) * t
        block = self.me + (origin - at) * stride
        for s, z in order[:phase]:
            here = (self.me // s) % z
            block = block + (xor(here, j % z, z) - here) * s
            j = j // z
        if size == 2:
            self.arrived(parts, order, block, phase, 0)
        else:
            pl.when((origin >= 0) & (origin < size))(
                functools.partial(self.arrived, parts, order, block, phase, way)
            )

    def drain(self):
        for order, parts in self.numbered:
            rest = 1
            for phase in range(3):
                size = order[phase][1]
                at = self.spot(order[phase])
                for i, part in parts:
                    def gone(count, way, i=i, part=part, phase=phase):
                        many = part.of(self.whole[part.array], pl.ds(0, count))
                        send(
                            many, many, self.send_sem.at[i, phase, way], self.recv_sem.at[i, 0], (self.me, 1 - self.core)
                        ).wait_send()

                    if size == 2:
                        gone(rest, 0)
                    elif size > 2:
                        for here in range(size):
                            def both(here=here, gone=gone, rest=rest, size=size):
                                if here < size - 1:
                                    gone((here + 1) * rest, 0)
                                if here > 0:
                                    gone((size - here) * rest, 1)
                            pl.when(at == here)(both)
                rest *= size


class Scatter:
    def __init__(self, me, core, numbered, acc, got, sems):
        self.me, self.core, self.numbered, self.acc, self.got = me, core, numbered, acc, got
        self.send_sem, self.recv_sems, self.drain_sem = sems

    def spot(self, axis):
        return (self.me // axis[0]) % axis[1]

    def block_at(self, order, phase, origin, turns):
        block = self.me + (origin - self.spot(order[phase])) * order[phase][0]
        for axis, t in zip(order[:phase], turns):
            block = block + (turn(self.spot(axis), t, axis[1]) - self.spot(axis)) * axis[0]
        return block

    def hop(self, i, part, phase, block, rest, slot, device):
        return send(
            part.of(self.acc[part.array], block),
            self.got[i][phase].at[rest, slot],
            self.send_sem.at[i, phase],
            self.recv_sems[phase].at[i, rest * self.got[i][phase].shape[1] + slot],
            device,
        )

    def take(self, parts, phase, block, rest, slot):
        for i, part in parts:
            self.hop(i, part, phase, block, rest, slot, (self.me, 1 - self.core)).wait_recv()
            acc, got = self.acc[part.array], self.got[i][phase]
            rows = acc.shape[1]
            step = min(rows, 16)
            cols = pl.ds(part.offset, part.width)

            def go(e, acc=acc, got=got, step=step, cols=cols):
                at = pl.ds(pl.multiple_of(e * step, step), step)
                acc[block, at, cols] = acc[block, at, cols] + got[rest, slot, at, :]

            each(rows // step, go)

    def give(self, parts, phase, block, rest, slot, step):
        for i, part in parts:
            self.hop(i, part, phase, block, rest, slot, (self.me + step, self.core)).start()

    def event(self, order, parts, phase, t, turns):
        stride, size = order[phase]
        at = self.spot(order[phase])
        origin = turn(at, t, size)
        mine = t == size - 1
        block = self.block_at(order, phase, origin, turns)
        rest = 0
        for axis, away in zip(order[:phase], turns):
            rest = rest * axis[1] + away
        if size == 1:
            return
        if size == 2:
            pl.when(jnp.logical_not(mine))(
                lambda: self.give(parts, phase, block, rest, 0, (1 - 2 * at) * stride)
            )
            pl.when(mine)(lambda: self.take(parts, phase, block, rest, 0))
            return

        @pl.when(jnp.logical_not(mine))
        def _():
            up = (origin > at).astype(jnp.int32)
            behind = jnp.where(up == 1, at > 0, at < size - 1)
            pl.when(behind)(lambda: self.take(parts, phase, block, rest, origin))
            landing = jnp.where((up == 0) & (origin == at - 1), size, origin)
            self.give(parts, phase, block, rest, landing, (2 * up - 1) * stride)

        @pl.when(mine)
        def _():
            pl.when(at > 0)(lambda: self.take(parts, phase, block, rest, at))
            pl.when(at < size - 1)(lambda: self.take(parts, phase, block, rest, size))

    def lead(self, order, parts, s):
        _, (_, nq), (_, nr) = order
        each((nr - 1) * nq, lambda e: self.event(order, parts, 2, e // nq, (s, e % nq)))

    def later(self, order, parts, s, low, high):
        def go(e):
            self.event(order, parts, 2, order[2][1] - 1, (s, low + e))
            self.event(order, parts, 1, low + e, (s,))

        each(high - low, go)

    def finish(self, order, parts, s):
        self.event(order, parts, 0, s, ())

    def stages(self):
        light, heavy = self.numbered[:2], self.numbered[2:]
        steps, few = heavy[0][0][0][1], max(c[0][0][1] for c in light)
        found = [functools.partial(self.lead, *c, s) for c in heavy[::-1] for s in range(min(AHEAD, steps))]
        found += [functools.partial(self.lead, *colour, 0) for colour in light]
        for s in range(max(steps, few + 1)):
            if s < steps:
                found += [functools.partial(self.later, *colour, s, 0, 1) for colour in heavy]
            if s + AHEAD < steps:
                found += [functools.partial(self.lead, *colour, s + AHEAD) for colour in heavy]
            if 1 <= s < steps:
                found += [functools.partial(self.finish, *colour, s - 1) for colour in heavy]
            found += [functools.partial(self.lead, *c, s + 1) for c in light if s + 1 < c[0][0][1]]
            if s < steps:
                found += [functools.partial(self.later, *c, s, 1, c[0][1][1]) for c in heavy]
            for c in light:
                if 1 <= s <= c[0][0][1]:
                    found += [
                        functools.partial(self.later, *c, s - 1, e, e + 1) for e in range(c[0][1][1])
                    ]
                    found.append(functools.partial(self.finish, *c, s - 1))
            if s == steps - 1:
                found += [functools.partial(self.finish, *colour, s) for colour in heavy]
        return found

    def drain(self):
        for order, parts in self.numbered:
            for i, part in parts:
                for phase in range(3):
                    if order[phase][1] > 1:
                        count = (order[phase][1] - 1) * math.prod([a[1] for a in order[:phase]])
                        many = part.of(self.acc[part.array], pl.ds(0, count))
                        send(
                            many, many, self.send_sem.at[i, phase], self.drain_sem, (self.me, 1 - self.core)
                        ).wait_send()


class Refs:
    pass


def block_kernel(axes, n, cap, *refs):
    names = (
        "wq", "wo", "wu", "wd", "vec", "rows_in", "pick", "extra", "notes", "gq", "go", "gu", "gd", "gs",
        "landed", "new", "Wq", "Wo", "Wu", "Wd", "V", "Wo2", "Aq", "Ao", "Au", "Ad", "As", "As2", "land",
        "rows_out", "X", "DY", "N1", "QKV", "PROBS", "ATT", "PART", "SENT", "GOT1", "GOT2", "GOT3", "GOT4",
        "BA", "N2", "ACT", "GM", "GU", "M1", "GA", "GATT", "GQKV", "GR", "NOTE", "FQ", "FO", "FU", "FD",
    )
    r = Refs()
    for name, ref in zip(names, refs):
        setattr(r, name, ref)
    got_refs, sems = refs[len(names) : -8], refs[-8:]
    g_send, g_recv, g_local, s_send, s_recv0, s_recv1, s_recv2, misc = sems
    R = D // n
    me, core = lax.axis_index("fsdp"), lax.axis_index("rep")
    half = D // 2
    pair = (me, 1 - core)
    units = r.wd.shape[0] // 2
    blocks = [r.Wq, r.Wo, r.Wu, r.Wd, r.V]

    def stage(src, dst, k):
        pltpu.make_async_copy(src, dst, g_local.at[k]).start()

    def column(f, size, start):
        return pl.ds(pl.multiple_of(f * size + start, 128), size)

    for k in range(3):
        stage(r.wq.at[:, pl.ds(pl.multiple_of(k * D + core * half, 128), half)], r.Wq.at[me, :, pl.ds(k * half, half)], 0)
    stage(r.wo.at[:, column(core, half, 0)], r.Wo.at[me], 1)
    each(
        n, lambda f: stage(r.wu.at[:, column(2 * f + core, units, 0)], r.Wu.at[me, :, column(f, units, 0)], 2)
    )
    stage(r.wd.at[pl.ds(pl.multiple_of(core * units, 16), units)], r.Wd.at[me], 3)
    stage(r.vec, r.V.at[me], 4)
    enter(n, me, core)
    for k, whole in enumerate(blocks):
        pltpu.make_async_copy(whole.at[me], whole.at[me], g_local.at[k]).wait()
    counter = [0]

    def to_pair(src, dst):
        k = counter[0]
        counter[0] += 2
        copy = send(src, dst, misc.at[k], misc.at[k + 1], pair)
        copy.start()
        return copy

    numbered = number_parts(first_shares(axes, 128) + second_shares(axes))
    g_sems = (g_send, g_recv)
    gathers = [Gather(n, me, core, part, blocks, g_sems) for part in (numbered[:4], numbered[4:])]
    gathers[0].start()
    row_sems = [misc.at[40 + k] for k in range(6)]
    def spread(items, chunks, low, high):
        done = 0
        for number, item in enumerate(items):
            item()
            want = len(chunks) * (number + 1 - low) // max(high - low, 1) if number + 1 >= low else 0
            while done < min(max(want, 0), len(chunks)):
                chunks[done]()
                done += 1
        for chunk in chunks[done:]:
            chunk()

    own_rows, row_sends = rows_each(n, me, core, r.rows_in, r.land, *row_sems[:3])
    note = to_pair(r.notes, r.NOTE)
    events = gathers[0].events()
    events.insert(len(events) * EARLY // 100, gathers[1].start)
    behind = gathers[1].events()
    late_sends = []
    if ROWS_IN[1] > 100:
        late_sends = row_sends[(n - 1) * 100 // ROWS_IN[1]:]
        row_sends = row_sends[: (n - 1) * 100 // ROWS_IN[1]]
    spread(events, row_sends, len(events) * ROWS_IN[0] // 100, len(events) * min(ROWS_IN[1], 100) // 100)
    for number, chunk in enumerate(late_sends):
        behind.insert(2 * number, chunk)
    mine, theirs = pl.ds(0, CAP), pl.ds(CAP, CAP)
    STEP = 64
    TILE = 256
    flying = Refs()

    def cols(e, size=TILE):
        return pl.ds(pl.multiple_of(e * size, size), size)

    def flat(ref, at):
        return ref[:, :, at].reshape(-1, at.size)

    def vector(v):
        per = 128 // R
        tiles = []
        for t in range(D // 128):
            total = r.V[t * per].astype(jnp.float32)[v : v + 1, :]
            for j in range(1, per):
                total = total + r.V[t * per + j].astype(jnp.float32)[v : v + 1, :]
            tiles.append(total)
        return jnp.concatenate(tiles, axis=1)

    w_router, gain1, gain2 = vector(0), vector(1), vector(2)

    def inverse(v):
        return lax.rsqrt(jnp.mean(v * v, axis=1, keepdims=True) + EPSILON)

    def rows_here():
        rows_wait(n, me, core, r.rows_in, r.land, row_sems[0], row_sems[1], own_rows)
        flying.out_half = to_pair(r.Wo.at[pl.ds((1 - core) * (n // 2), n // 2)], r.Wo2)

    def extract(k, ref):
        def go(e):
            at = pl.ds(k * CAP, CAP)
            ref[:CAP, cols(e)] = (
                mm(r.pick[at, :], r.land[:, :, cols(e)].reshape(-1, TILE)) + r.extra[at, cols(e)].astype(jnp.float32)
            ).astype(jnp.bfloat16)

        each(D // TILE, go)

    def swap_rows():
        flying.both = [to_pair(ref.at[mine], ref.at[theirs]) for ref in (r.X, r.DY)] + [note]

    def first(e):
        at = pl.ds(pl.multiple_of(e * STEP, STEP), STEP)
        x = r.X[at, :].astype(jnp.float32)
        r.N1[at, :] = (x * inverse(x) * gain1).astype(jnp.bfloat16)
        router = jnp.sum(x * w_router, axis=1, keepdims=True)
        r.GM[at, :] = (router * r.DY[at, :].astype(jnp.float32)).astype(jnp.bfloat16)

    def first_rows():
        for copy in flying.both:
            copy.wait()
        each(2 * CAP // STEP, first)

    def project(e):
        r.QKV[:, cols(e)] = mm(r.N1[...], flat(r.Wq, cols(e))).astype(jnp.bfloat16)

    factor = 1.0 / math.sqrt(HEAD_DIM)
    pairs = half // 128
    lane = lax.broadcasted_iota(jnp.int32, (CAP, 128), 1) // HEAD_DIM
    zero = jnp.zeros((CAP, 128), jnp.bfloat16)
    causal = lax.broadcasted_iota(jnp.int32, (CAP, CAP), 1) <= lax.broadcasted_iota(jnp.int32, (CAP, CAP), 0)

    def heads(e):
        s, p = e // pairs, e % pairs
        rows = pl.ds(pl.multiple_of(s * CAP, CAP), CAP)
        q, k, v = (r.QKV[rows, cols(p + j * pairs, 128)] for j in range(3))
        return s, p, rows, q, k, v

    def attend(e):
        s, p, rows, q, k, v = heads(e)
        valid = jnp.where(s == 0, r.notes[0:1, :], r.NOTE[0:1, :]) > 0
        parts = []
        for h in range(2):
            score = mm(jnp.where(lane == h, q, zero), k, NT) * factor
            score = jnp.where(causal & valid, score, -1e30)
            top = jnp.exp(score - jnp.max(score, axis=1, keepdims=True))
            probs = top / jnp.sum(top, axis=1, keepdims=True)
            r.PROBS[2 * e + h] = probs
            parts.append(mm(probs.astype(jnp.bfloat16), v))
        r.ATT[rows, cols(p, 128)] = jnp.where(lane == 0, parts[0], parts[1]).astype(jnp.bfloat16)

    near = pl.ds(pl.multiple_of(core * half, half), half)
    away = pl.ds(pl.multiple_of((1 - core) * half, half), half)
    own_heads = pl.ds(core * (n // 2), n // 2)

    def wo_near():
        return r.Wo[own_heads].reshape(half, half)

    def wo_away():
        return r.Wo2[...].reshape(half, half)

    def project_out(where):
        if where == 0:
            r.BA[:, near] = mm(r.ATT[...], wo_near())
        else:
            flying.out_half.wait()
            r.BA[:, away] = mm(r.ATT[...], wo_away())

    def pass_on(part, got):
        for a, b in ((mine, theirs), (theirs, mine)):
            r.SENT[a, :] = part[b, :].astype(jnp.bfloat16)
        flying.gone = to_pair(r.SENT, got)

    def second(e):
        at = pl.ds(pl.multiple_of(e * STEP, STEP), STEP)
        branch = r.BA[at, :] + r.GOT1[at, :].astype(jnp.float32)
        r.BA[at, :] = branch
        middle = r.X[at, :].astype(jnp.float32) + branch
        r.N2[at, :] = (middle * inverse(middle) * gain2).astype(jnp.bfloat16)

    def second_rows():
        flying.gone.wait()
        each(2 * CAP // STEP, second)

    def some(fn, low, high):
        return lambda: lax.fori_loop(low, high, lambda e, _: (fn(e), 0)[1], 0)

    forward = [rows_here, functools.partial(extract, 0, r.X), functools.partial(extract, 1, r.DY), swap_rows, first_rows]
    forward += [some(project, e, e + 1) for e in range(3 * half // TILE)]
    forward += [some(attend, e, e + 2) for e in range(0, 2 * pairs, 2)]
    forward += [
        functools.partial(project_out, 0), functools.partial(project_out, 1),
        lambda: pass_on(r.BA, r.GOT1), second_rows,
    ]
    spread(behind, forward, len(behind) * AT0 // 100, len(behind) * AT1 // 100)
    hidden = r.Wd.shape[1]
    per = TILE // hidden if hidden < TILE else 1

    def down_rows(e):
        return pl.ds(e * per, per)

    def hidden_units(e):
        up = mm(r.N2[...], flat(r.Wu, cols(e)))
        inner = jnp.tanh(SQRT_2_PI * (up + 0.044715 * up * up * up))
        act = (0.5 * up * (1.0 + inner)).astype(jnp.bfloat16)
        slope = 0.5 * (1.0 + inner) + 0.5 * up * (1.0 - inner * inner) * (
            SQRT_2_PI * (1.0 + 3 * 0.044715 * up * up)
        )
        r.ACT[:, cols(e)] = act
        down = r.Wd[down_rows(e)].reshape(TILE, D)
        grad_act = mm(r.GM[...], down, NT)
        r.GU[:, cols(e)] = (slope * grad_act).astype(jnp.bfloat16)
        r.Ad[down_rows(e)] = mm(act, r.GM[...], TN).astype(jnp.bfloat16).reshape(per, hidden, D)

    tiles = 2 * D // TILE
    each(tiles, hidden_units)

    def up_grads(e):
        r.Au[:, :, cols(e)] = mm(r.N2[...], r.GU[:, cols(e)], TN).astype(jnp.bfloat16).reshape(n, R, TILE)

    total = sum(len(p) for _, p in numbered)
    got = [got_refs[3 * i : 3 * i + 3] for i in range(total)]
    s_sems = (s_send, (s_recv0, s_recv1, s_recv2), misc.at[46])
    acc = [r.Aq, r.Ao, r.Au, r.Ad, r.As]
    late, soon = (Scatter(me, core, part, acc, got, s_sems) for part in (numbered[:4], numbered[4:]))
    many = TILE // R

    def back_up(e):
        block = r.Wu[pl.ds(e * many, many)].reshape(TILE, 2 * D)
        r.PART[:, cols(e)] = mm(r.GU[...], block, NT)

    def mlp(e):
        r.M1[:, cols(e)] = mm(r.ACT[...], r.Wd[:, :, cols(e)].reshape(2 * D, TILE))

    def mlp_out():
        flying.gone.wait()
        r.SENT[mine, :] = r.M1[theirs, :].astype(jnp.bfloat16)
        flying.gone = to_pair(r.SENT.at[mine], r.GOT3)

    zeros = jnp.zeros((1, D), jnp.float32)

    def third(e, total):
        at = pl.ds(pl.multiple_of(e * STEP, STEP), STEP)
        x = r.X[at, :].astype(jnp.float32)
        dy = r.DY[at, :].astype(jnp.float32)
        middle = x + r.BA[at, :]
        inv = inverse(middle)
        grad = r.PART[at, :] + r.GOT2[at, :].astype(jnp.float32)
        scaled = gain2 * grad
        grad_middle = inv * scaled - middle * inv**3 * jnp.mean(scaled * middle, axis=1, keepdims=True)
        router = jnp.sum(x * w_router, axis=1, keepdims=True)
        r.GA[at, :] = (router * dy + grad_middle).astype(jnp.bfloat16)
        r.PART[at, :] = grad_middle
        counted = jnp.where(e < CAP // STEP, 1.0, 0.0)
        return total + counted * jnp.sum(grad * middle * inv, axis=0, keepdims=True)

    def third_rows():
        flying.gain2 = lax.fori_loop(0, 2 * CAP // STEP, third, zeros)

    def out_grads():
        r.Ao[own_heads] = mm(r.ATT[...], r.GA[:, near], TN).astype(jnp.bfloat16).reshape(n // 2, R, half)

    def attended_grads():
        r.GATT[...] = (mm(r.GA[:, near], wo_near(), NT) + mm(r.GA[:, away], wo_away(), NT)).astype(jnp.bfloat16)

    def other_out_grads():
        flying.gone.wait()
        r.Wo2[...] = mm(r.ATT[...], r.GA[:, away], TN).astype(jnp.bfloat16).reshape(n // 2, R, half)
        flying.out = to_pair(r.Wo2, r.Ao.at[own_heads])

    def attend_back(e):
        s, p, rows, q, k, v = heads(e)
        grad = r.GATT[rows, cols(p, 128)]
        gq, gk, gv = [], [], []
        for h in range(2):
            grad_h, q_h = jnp.where(lane == h, grad, zero), jnp.where(lane == h, q, zero)
            probs = r.PROBS[2 * e + h]
            grad_probs = mm(grad_h, v, NT)
            gv.append(mm(probs.astype(jnp.bfloat16), grad_h, TN))
            grad_scores = probs * (grad_probs - jnp.sum(probs * grad_probs, axis=1, keepdims=True))
            grad_scores = grad_scores.astype(jnp.bfloat16)
            gq.append(mm(grad_scores, k))
            gk.append(mm(grad_scores, q_h, TN))
        r.GQKV[rows, cols(p, 128)] = (jnp.where(lane == 0, gq[0], gq[1]) * factor).astype(jnp.bfloat16)
        r.GQKV[rows, cols(p + pairs, 128)] = ((gk[0] + gk[1]) * factor).astype(jnp.bfloat16)
        r.GQKV[rows, cols(p + 2 * pairs, 128)] = (gv[0] + gv[1]).astype(jnp.bfloat16)

    def qkv_grads(e):
        r.Aq[:, :, cols(e)] = mm(r.N1[...], r.GQKV[:, cols(e)], TN).astype(jnp.bfloat16).reshape(n, R, TILE)

    def back_qkv(e):
        block = r.Wq[pl.ds(e * many, many)].reshape(TILE, 3 * half)
        r.M1[:, cols(e)] = mm(r.GQKV[...], block, NT)

    def fourth(e, total):
        at = pl.ds(pl.multiple_of(e * STEP, STEP), STEP)
        x = r.X[at, :].astype(jnp.float32)
        dy = r.DY[at, :].astype(jnp.float32)
        combined = r.BA[at, :] + r.M1[at, :] + r.GOT3[at, :].astype(jnp.float32)
        router = jnp.sum(x * w_router, axis=1, keepdims=True)
        r.new[at, :] = (x + router * combined).astype(jnp.bfloat16)
        grad_router = jnp.sum(dy * combined, axis=1, keepdims=True)
        r.GR[at, :] = dy + grad_router * w_router + r.PART[at, :]
        return total + jnp.sum(grad_router * x, axis=0, keepdims=True)

    def fourth_rows():
        flying.router = lax.fori_loop(0, CAP // STEP, fourth, zeros)

    def last_out():
        r.SENT[theirs, :] = r.M1[theirs, :].astype(jnp.bfloat16)
        flying.gone = to_pair(r.SENT.at[theirs], r.GOT4)

    def fifth(e, total):
        at = pl.ds(pl.multiple_of(e * STEP, STEP), STEP)
        x = r.X[at, :].astype(jnp.float32)
        grad = r.M1[at, :] + r.GOT4[at, :].astype(jnp.float32)
        inv = inverse(x)
        scaled = gain1 * grad
        grad_x = inv * scaled - x * inv**3 * jnp.mean(scaled * x, axis=1, keepdims=True)
        below = pl.ds(pl.multiple_of(CAP + e * STEP, STEP), STEP)
        r.new[below, :] = (r.GR[at, :] + grad_x).astype(jnp.bfloat16)
        return total + jnp.sum(grad * x * inv, axis=0, keepdims=True)

    def fifth_rows():
        flying.gone.wait()
        gain1_grad = lax.fori_loop(0, CAP // STEP, fifth, zeros)
        small = jnp.concatenate([flying.router, gain1_grad, flying.gain2, jnp.zeros((5, D), jnp.float32)], axis=0)
        for block in range(n):
            tile = block * R // 128
            r.As[block] = small[:, tile * 128 : tile * 128 + 128]
        flying.small = to_pair(r.As, r.As2)

    def place(e):
        sent = mm(r.pick[...], r.new[:, cols(e)], TN).astype(jnp.bfloat16)
        r.rows_out[:, :, cols(e)] = sent.reshape(n, -1, TILE)

    def send_late():
        flying.rows, flying.sends = rows_each(n, me, core, r.rows_out, r.landed, *row_sems[3:])
        flying.small.wait()
        flying.out.wait()
        r.As[...] = r.As[...] + r.As2[...]

    backward = [some(up_grads, e, e + 2) for e in range(0, tiles, 2)] if SPLIT else []
    backward += [some(back_up, e, e + 1) for e in range(D // TILE)]
    backward += [lambda: pass_on(r.PART, r.GOT2)]
    backward += [some(mlp, e, e + 1) for e in range(D // TILE)]
    backward += [mlp_out, third_rows, out_grads, attended_grads, other_out_grads]
    backward += [some(attend_back, e, e + 1) for e in range(2 * pairs)]
    backward += [fourth_rows]
    backward += [some(back_qkv, e, e + 1) for e in range(D // TILE)]
    backward += [last_out]
    backward += [some(qkv_grads, e, e + 1) for e in range(3 * half // TILE)]
    backward += [fifth_rows, some(place, 0, D // TILE), send_late]
    stages = soon.stages()
    for stage in stages[:AHEAD]:
        stage()
    each(tiles, up_grads)
    stages = stages[AHEAD:]
    cut = len(stages) * CUT // 100
    spread(stages[:cut], backward, 1, cut)
    rest, more = stages[cut:], late.stages()
    for number, chunk in enumerate(flying.sends):
        more.insert((number + 1) * ROWS_OUT - 1 if ROWS_OUT else 0, chunk)
    while rest or more:
        if more:
            more.pop(0)()
        if rest:
            rest.pop(0)()
    for gather in gathers:
        gather.drain()
    final = [to_pair(acc[k].at[me], ref) for k, ref in enumerate((r.FQ, r.FO, r.FU, r.FD))]

    def give(k, side, ref):
        value = ref[...].astype(jnp.float32)
        if k == 0:
            for j in range(3):
                r.gq[:, pl.ds(pl.multiple_of(j * D + side * half, 128), half)] = value[:, j * half : (j + 1) * half]
        elif k == 1:
            r.go[:, column(side, half, 0)] = value
        elif k == 2:
            for f in range(n):
                r.gu[:, column(2 * f + side, units, 0)] = value[:, f * units : (f + 1) * units]
        else:
            r.gd[pl.ds(pl.multiple_of(side * units, 16), units), :] = value

    for k in range(4):
        give(k, core, acc[k].at[me])
    r.gs[...] = r.As[me]
    for k, ref in enumerate((r.FQ, r.FO, r.FU, r.FD)):
        final[k].wait()
        give(k, 1 - core, ref)
    rows_wait(n, me, core, r.rows_out, r.landed, row_sems[3], row_sems[4], flying.rows)
    late.drain()
    soon.drain()


def whole_block(axes, n, cap, weights, vec, rows_in, pick, extra, notes):
    plan = first_shares(axes, 128) + second_shares(axes)
    bf, f32 = jnp.bfloat16, jnp.float32
    shards = weights
    weights = [
        jax.ShapeDtypeStruct((w.shape[0] // (2 if k == 3 else 1), w.shape[1] // (1 if k == 3 else 2)), bf)
        for k, w in enumerate(shards)
    ]
    R, F = weights[0].shape[0], weights[3].shape[0]
    vmem = pl.BlockSpec(memory_space=pltpu.VMEM)
    anywhere = pl.BlockSpec(memory_space=ANY)
    out = [jax.ShapeDtypeStruct(w.shape, f32) for w in shards]
    out += [
        jax.ShapeDtypeStruct((8, 128), f32),
        jax.ShapeDtypeStruct(rows_in.shape, bf),
        jax.ShapeDtypeStruct((2 * CAP, D), bf),
    ]
    rows = 2 * CAP
    half = D // 2
    V = pltpu.VMEM
    scratch = [V((n,) + w.shape, bf) for w in weights]
    scratch += [V((n,) + vec.shape, bf), V((n // 2, R, half), bf)]
    scratch += [V((n,) + w.shape, bf) for w in weights]
    scratch += [V((n, 8, 128), f32)] * 2
    scratch += [V((n, 2 * cap, D), bf), V((n, 2 * cap, D), bf)]
    scratch += [V((rows, D), bf)] * 3
    scratch += [V((rows, 3 * half), bf), V((HEADS, CAP, CAP), f32), V((rows, half), bf)]
    scratch += [V((rows, D), f32), V((rows, D), bf), V((rows, D), bf), V((rows, D), bf), V((CAP, D), bf), V((CAP, D), bf)]
    scratch += [V((rows, D), f32), V((rows, D), bf)]
    scratch += [V((rows, 2 * D), bf), V((rows, D), bf), V((rows, 2 * D), bf)]
    scratch += [V((rows, D), f32), V((rows, D), bf), V((rows, half), bf), V((rows, 3 * half), bf)]
    scratch += [V((CAP, D), f32), V((8, 128), f32)]
    scratch += [V(w.shape, bf) for w in weights]
    most = [1, 1, 1]
    total = 0
    deep = [R, R, R, F, 8]
    for order, parts in plan:
        total += len(parts)
        for p in parts:
            count = 1
            for phase in range(3):
                size = order[phase][1]
                kind = f32 if p.array == 4 else bf
                scratch.append(V((count, slots(size), deep[p.array], p.width), kind))
                most[phase] = max(most[phase], count * slots(size))
                count *= size
    dma = pltpu.SemaphoreType.DMA
    scratch += [dma((total, 3, 2)), dma((total, n)), dma((5,)), dma((total, 3))]
    scratch += [dma((total, m)) for m in most]
    scratch += [dma((48,))]
    return pl.pallas_call(
        functools.partial(block_kernel, axes, n, cap),
        out_shape=out,
        in_specs=[anywhere] * 6 + [vmem] * 3,
        out_specs=[vmem] * 5 + [anywhere, vmem],
        scratch_shapes=scratch,
        compiler_params=pltpu.CompilerParams(
            collective_id=2, has_side_effects=True, vmem_limit_bytes=67043328
        ),
        name="whole_block",
    )(*shards, vec, rows_in, pick, extra, notes)


def normalize(values, gain):
    inverse = lax.rsqrt(jnp.mean(values * values, axis=-1, keepdims=True) + EPSILON)
    return (values * inverse * gain, inverse)


def rms_back(values, inverse, gain, grad_normed):
    scaled = gain * grad_normed
    grad_values = inverse * scaled - values * inverse**3 * jnp.mean(
        scaled * values, axis=-1, keepdims=True
    )
    grad_gain = jnp.sum(grad_normed * values * inverse, axis=(0, 1))
    return (grad_values, grad_gain)


def split_heads(packed, offset):
    return packed[..., offset : offset + D].reshape(packed.shape[:2] + (HEADS, HEAD_DIM))


def narrow_body(
    axes,
    tokens,
    cotangent,
    w_qkv,
    w_out,
    w_up,
    w_down,
    w_router,
    gain_attn,
    gain_mlp,
    lengths,
    routed,
    dealing,
):
    factor = 1.0 / math.sqrt(HEAD_DIM)
    shards, place = lax.axis_size("fsdp"), lax.axis_index("fsdp")
    group_seqs, width = tokens.shape[1], tokens.shape[2]
    cap = min(24, width)
    slot_ids = jnp.arange(CAP, dtype=jnp.int32)
    picker = dealing[0][:, None] == jnp.arange(group_seqs, dtype=jnp.int32)[None, :]
    row_lengths = jnp.sum(jnp.where(picker, lengths[0][None, :], 0), axis=1)
    row_routes = jnp.sum(jnp.where(picker[:, :, None], routed[0][None, :, :], 0), axis=1)
    row_routes = jnp.where(slot_ids[None, :] < (row_lengths // 8)[:, None], row_routes, PAST)
    here = place * width + jnp.arange(width, dtype=jnp.int32)
    below = jnp.sum((row_routes[:, :, None] < here[None, None, :]).astype(jnp.int32), axis=1)
    upto = jnp.sum((row_routes[:, :, None] <= here[None, None, :]).astype(jnp.int32), axis=1)
    touched = upto > below
    living = here[None, :] < row_lengths[:, None]
    rank = jnp.where(touched, below - below[:, :1], -1)
    select = (rank[:, None, :] == jnp.arange(cap, dtype=jnp.int32)[None, :, None]).astype(jnp.bfloat16)
    shard_of = row_routes // width
    crowd = jnp.sum(
        (shard_of[:, :, None] == jnp.arange(shards, dtype=jnp.int32)[None, None, :]).astype(jnp.int32), axis=1
    )
    flag = jnp.broadcast_to((jnp.max(crowd) > cap).astype(jnp.float32), (8, 128))
    packed_rows = jnp.concatenate(
        [
            jnp.einsum("jip,jpd->jid", select, t[0], preferred_element_type=jnp.float32).astype(jnp.bfloat16)
            for t in (tokens, cotangent)
        ],
        axis=1,
    )
    seq_lengths = lax.dynamic_slice_in_dim(row_lengths, place, 1)
    routes = lax.dynamic_slice_in_dim(row_routes, place, 1)[0]
    valid_slot = slot_ids[None, :] < (seq_lengths // 8)[:, None]
    seq_shard = routes // width
    seq_rank = slot_ids - jnp.sum((routes[None, :] < (seq_shard * width)[:, None]).astype(jnp.int32), axis=1)
    fits = valid_slot[0] & (seq_rank < cap)
    landing = jnp.where(fits, seq_shard * (2 * cap) + seq_rank, -1)
    cells = jnp.arange(shards * 2 * cap, dtype=jnp.int32)
    pick = jnp.concatenate([landing[:, None] == cells[None, :], (landing[:, None] == (cells - cap)[None, :]) & fits[:, None]])
    pick = pick.astype(jnp.bfloat16)
    part = w_router.shape[0]
    vectors = jnp.pad(jnp.stack([w_router, gain_attn, gain_mlp]), ((0, 13), (0, 128 - part)))
    blocks = gather_all(axes, shards, [w_qkv, w_out, w_up, w_down, vectors], packed_rows, flag, 0)
    crowded = jnp.maximum(flag, blocks[6])[0, 0] > 0
    got_rows = jnp.einsum(
        "cs,sd->cd", pick, blocks[5].reshape(-1, D), preferred_element_type=jnp.float32
    ).astype(jnp.bfloat16)

    def all_rows(got):
        positions = jnp.arange(SEQ_MAX, dtype=jnp.int32)
        onehot = (routes[:, None] == positions[None, :]).astype(jnp.bfloat16)
        return jnp.concatenate(
            [
                jnp.dot(
                    onehot,
                    lax.all_to_all(t, "fsdp", split_axis=1, concat_axis=2, tiled=True)[0, 0],
                    preferred_element_type=jnp.float32,
                ).astype(jnp.bfloat16)
                for t in (tokens, cotangent)
            ]
        )

    if cap < width:
        got_rows = lax.cond(crowded, all_rows, lambda got: got, got_rows)
    rows_low = got_rows[None, :CAP]
    incoming_rows = rows_low.astype(jnp.float32)
    row_gradient = got_rows[None, CAP:].astype(jnp.float32)
    small = blocks[4][:, :3, :part].transpose(1, 0, 2).reshape(3, D)
    gathered = tuple(b.reshape(-1, b.shape[2]) for b in blocks[:4]) + (small[0], small[1], small[2])
    router_val = jnp.einsum("scd,d->sc", rows_low, gathered[4], preferred_element_type=jnp.float32)
    normed_attn, inverse_attn = normalize(incoming_rows, gathered[5].astype(jnp.float32))
    normed_low = normed_attn.astype(jnp.bfloat16)
    packed = jnp.einsum(
        "scd,de->sce", normed_low, gathered[0], preferred_element_type=jnp.float32
    ).astype(jnp.bfloat16)
    queries = split_heads(packed, 0)
    keys_heads = split_heads(packed, D)
    values_heads = split_heads(packed, 2 * D)
    scores = (
        jnp.einsum("sqhe,skhe->shqk", queries, keys_heads, preferred_element_type=jnp.float32)
        * factor
    )
    allowed = (slot_ids[None, :] <= slot_ids[:, None])[None, None] & valid_slot[:, None, None, :]
    scores = jnp.where(allowed, scores, -1e30)
    probs = jax.nn.softmax(scores, axis=-1)
    probs_low = probs.astype(jnp.bfloat16)
    attended = jnp.einsum(
        "shqk,skhe->sqhe", probs_low, values_heads, preferred_element_type=jnp.float32
    ).astype(jnp.bfloat16)
    attended = attended.reshape(incoming_rows.shape)
    branch_attn = jnp.einsum(
        "sce,ed->scd", attended, gathered[1], preferred_element_type=jnp.float32
    )
    middle = incoming_rows + branch_attn
    normed_mid, inverse_mid = normalize(middle, gathered[6].astype(jnp.float32))
    normed_mid_low = normed_mid.astype(jnp.bfloat16)
    upward = jnp.einsum(
        "scd,df->scf", normed_mid_low, gathered[2], preferred_element_type=jnp.float32
    )
    activated = jax.nn.gelu(upward).astype(jnp.bfloat16)
    branch_mlp = jnp.einsum(
        "scf,fd->scd", activated, gathered[3], preferred_element_type=jnp.float32
    )
    combined = branch_attn + branch_mlp
    refreshed_rows = (incoming_rows + router_val[..., None] * combined).astype(jnp.bfloat16)
    back_weights = gathered
    grad_comb = router_val[..., None] * row_gradient
    grad_router_val = jnp.sum(row_gradient * combined, axis=-1)
    total_gradient = row_gradient + grad_router_val[..., None] * back_weights[4].astype(jnp.float32)
    grad_mlp_low = grad_comb.astype(jnp.bfloat16)
    grad_act = jnp.einsum(
        "scd,fd->scf", grad_mlp_low, back_weights[3], preferred_element_type=jnp.float32
    )
    grad_downw = jnp.einsum(
        "scf,scd->fd", activated, grad_mlp_low, preferred_element_type=jnp.float32
    )
    unused, gelu_pull = jax.vjp(jax.nn.gelu, upward)
    grad_up_low = gelu_pull(grad_act)[0].astype(jnp.bfloat16)
    grad_normed_mid = jnp.einsum(
        "scf,df->scd", grad_up_low, back_weights[2], preferred_element_type=jnp.float32
    )
    grad_upw = jnp.einsum(
        "scd,scf->df", normed_mid_low, grad_up_low, preferred_element_type=jnp.float32
    )
    grad_middle, grad_gain_second = rms_back(
        middle, inverse_mid, back_weights[6].astype(jnp.float32), grad_normed_mid
    )
    grad_attn_low = (grad_comb + grad_middle).astype(jnp.bfloat16)
    total_gradient = total_gradient + grad_middle
    grad_attended = jnp.einsum(
        "scd,ed->sce", grad_attn_low, back_weights[1], preferred_element_type=jnp.float32
    ).astype(jnp.bfloat16)
    grad_outw = jnp.einsum(
        "sce,scd->ed", attended, grad_attn_low, preferred_element_type=jnp.float32
    )
    grad_att_heads = grad_attended.reshape(queries.shape)
    grad_probs = jnp.einsum(
        "sqhe,skhe->shqk", grad_att_heads, values_heads, preferred_element_type=jnp.float32
    )
    grad_values = jnp.einsum(
        "shqk,sqhe->skhe", probs_low, grad_att_heads, preferred_element_type=jnp.float32
    )
    grad_scores = probs * (grad_probs - jnp.sum(probs * grad_probs, axis=-1, keepdims=True))
    grad_scores_low = grad_scores.astype(jnp.bfloat16)
    grad_queries = (
        jnp.einsum(
            "shqk,skhe->sqhe", grad_scores_low, keys_heads, preferred_element_type=jnp.float32
        )
        * factor
    )
    grad_keys = (
        jnp.einsum("shqk,sqhe->skhe", grad_scores_low, queries, preferred_element_type=jnp.float32)
        * factor
    )
    flat_shape = incoming_rows.shape
    grad_packed = jnp.concatenate(
        [
            grad_queries.reshape(flat_shape),
            grad_keys.reshape(flat_shape),
            grad_values.reshape(flat_shape),
        ],
        axis=-1,
    ).astype(jnp.bfloat16)
    grad_qkvw = jnp.einsum(
        "scd,sce->de", normed_low, grad_packed, preferred_element_type=jnp.float32
    )
    grad_normed_attn = jnp.einsum(
        "sce,de->scd", grad_packed, back_weights[0], preferred_element_type=jnp.float32
    )
    grad_first_rows, grad_gain_first = rms_back(
        incoming_rows, inverse_attn, back_weights[5].astype(jnp.float32), grad_normed_attn
    )
    total_gradient = total_gradient + grad_first_rows
    grad_routerw = jnp.einsum(
        "scd,sc->d", incoming_rows, grad_router_val, precision=EXACT_PRECISION
    )
    new_rows = jnp.concatenate([refreshed_rows[0], total_gradient[0].astype(jnp.bfloat16)])
    sent_rows = (
        jnp.einsum("cs,cd->sd", pick, new_rows, preferred_element_type=jnp.float32)
        .astype(jnp.bfloat16)
        .reshape(shards, 2 * cap, D)
    )
    small_grads = jnp.stack([grad_routerw, grad_gain_first, grad_gain_second])
    small_grads = small_grads.reshape(3, shards, part).transpose(1, 0, 2)
    small_grads = jnp.pad(small_grads, ((0, 0), (0, 5), (0, 128 - part)))
    partial = [
        g.astype(jnp.bfloat16).reshape(shards, -1, g.shape[1])
        for g in (grad_qkvw, grad_outw, grad_upw, grad_downw)
    ]
    shares = scatter_all(axes, shards, partial + [small_grads], sent_rows, 1)
    totals = tuple(t.astype(jnp.float32) for t in shares[:4]) + tuple(shares[4][j, :part] for j in range(3))
    def place_rows(rows, held):
        spread = jnp.einsum("jip,jid->jpd", select, rows, preferred_element_type=jnp.float32).astype(jnp.bfloat16)
        kept = jnp.where(touched[..., None], spread, held[0])
        return jnp.where(living[..., None], kept, jnp.zeros_like(kept))[None]

    def compact(landed, rows):
        return place_rows(landed[:, :cap], tokens), place_rows(landed[:, cap:], cotangent)

    def entire(landed, rows):
        positions = jnp.arange(SEQ_MAX, dtype=jnp.int32)
        onehot = (routes[:, None] == positions[None, :]).astype(jnp.bfloat16)
        placed = []
        for r, held in ((rows[:CAP], tokens), (rows[CAP:], cotangent)):
            spread = jnp.einsum("cp,cd->pd", onehot, r, preferred_element_type=jnp.float32)
            spread = lax.all_to_all(
                spread.astype(jnp.bfloat16)[None, None], "fsdp", split_axis=2, concat_axis=1, tiled=True
            )
            kept = jnp.where(touched[..., None], spread[0], held[0])
            placed.append(jnp.where(living[..., None], kept, jnp.zeros_like(kept))[None])
        return tuple(placed)

    if cap < width:
        back_out, back_grad = lax.cond(crowded, entire, compact, shares[5], new_rows)
    else:
        back_out, back_grad = compact(shares[5], new_rows)
    return (
        back_out,
        back_grad,
        totals[0],
        totals[1],
        totals[2],
        totals[3],
        totals[4],
        totals[5],
        totals[6],
    )


def wide_body(
    axes,
    tokens,
    cotangent,
    w_qkv,
    w_out,
    w_up,
    w_down,
    w_router,
    gain_attn,
    gain_mlp,
    lengths,
    routed,
    dealing,
):
    factor = 1.0 / math.sqrt(HEAD_DIM)
    shards, place = lax.axis_size("fsdp"), lax.axis_index("fsdp")
    group_seqs, width = tokens.shape[1], tokens.shape[2]
    cap = min(24, width)
    slot_ids = jnp.arange(CAP, dtype=jnp.int32)
    picker = dealing[0][:, None] == jnp.arange(group_seqs, dtype=jnp.int32)[None, :]
    row_lengths = jnp.sum(jnp.where(picker, lengths[0][None, :], 0), axis=1)
    row_routes = jnp.sum(jnp.where(picker[:, :, None], routed[0][None, :, :], 0), axis=1)
    row_routes = jnp.where(slot_ids[None, :] < (row_lengths // 8)[:, None], row_routes, PAST)
    here = place * width + jnp.arange(width, dtype=jnp.int32)
    below = jnp.sum((row_routes[:, :, None] < here[None, None, :]).astype(jnp.int32), axis=1)
    upto = jnp.sum((row_routes[:, :, None] <= here[None, None, :]).astype(jnp.int32), axis=1)
    touched = upto > below
    living = here[None, :] < row_lengths[:, None]
    rank = jnp.where(touched, below - below[:, :1], -1)
    select = (rank[:, None, :] == jnp.arange(cap, dtype=jnp.int32)[None, :, None]).astype(jnp.bfloat16)
    shard_of = row_routes // width
    crowd = jnp.sum(
        (shard_of[:, :, None] == jnp.arange(shards, dtype=jnp.int32)[None, None, :]).astype(jnp.int32), axis=1
    )
    flag = jnp.broadcast_to((jnp.max(crowd) > cap).astype(jnp.float32), (8, 128))
    packed_rows = jnp.concatenate(
        [
            jnp.einsum("jip,jpd->jid", select, t[0], preferred_element_type=jnp.float32).astype(jnp.bfloat16)
            for t in (tokens, cotangent)
        ],
        axis=1,
    )
    seq_lengths = lax.dynamic_slice_in_dim(row_lengths, place, 1)
    routes = lax.dynamic_slice_in_dim(row_routes, place, 1)[0]
    valid_slot = slot_ids[None, :] < (seq_lengths // 8)[:, None]
    seq_shard = routes // width
    seq_rank = slot_ids - jnp.sum((routes[None, :] < (seq_shard * width)[:, None]).astype(jnp.int32), axis=1)
    fits = valid_slot[0] & (seq_rank < cap)
    landing = jnp.where(fits, seq_shard * (2 * cap) + seq_rank, -1)
    cells = jnp.arange(shards * 2 * cap, dtype=jnp.int32)
    pick = jnp.concatenate([landing[:, None] == cells[None, :], (landing[:, None] == (cells - cap)[None, :]) & fits[:, None]])
    pick = pick.astype(jnp.bfloat16)
    part = w_router.shape[0]
    mine = jnp.max(flag)
    other = lax.ppermute(flag, "rep", [(0, 1), (1, 0)])
    crowded = jnp.maximum(mine, jnp.max(other)) > 0
    ring = [(i, (i + 1) % shards) for i in range(shards)]

    def chosen(j):
        return (lax.dynamic_index_in_dim(row_routes, j, 0, keepdims=False)[:, None] == here[None, :]).astype(jnp.bfloat16)

    def all_rows():
        def go(i, rows):
            j = (place - 1 - i) % shards
            mine = [
                jnp.dot(chosen(j), lax.dynamic_index_in_dim(t[0], j, 0, keepdims=False), preferred_element_type=jnp.float32)
                for t in (tokens, cotangent)
            ]
            return lax.ppermute(rows, "fsdp", ring) + jnp.concatenate(mine).astype(jnp.bfloat16)

        return lax.fori_loop(0, shards, go, jnp.zeros((2 * CAP, D), jnp.bfloat16))

    extra = jnp.zeros((2 * CAP, D), jnp.bfloat16)
    if cap < width:
        extra = lax.cond(crowded, all_rows, lambda: jnp.zeros((2 * CAP, D), jnp.bfloat16))
        pick = jnp.where(crowded, jnp.zeros_like(pick), pick)
    weights = [w_qkv, w_out, w_up, w_down]
    lanes = (place * part) % 128
    vectors = jnp.pad(jnp.stack([w_router, gain_attn, gain_mlp]), ((0, 13), (0, 0)))
    vectors = lax.dynamic_update_slice(jnp.zeros((16, 128), jnp.bfloat16), vectors, (0, lanes))
    notes = jnp.broadcast_to(valid_slot.astype(jnp.float32), (8, CAP))
    gq, go, gu, gd, gs, landed, new_rows = whole_block(
        axes, shards, cap, weights, vectors, packed_rows, pick, extra, notes
    )
    small = lax.dynamic_slice(gs, (0, lanes), (8, part))
    totals = (gq, go, gu, gd, small[0], small[1], small[2])

    def place_rows(rows, held):
        spread = jnp.einsum("jip,jid->jpd", select, rows, preferred_element_type=jnp.float32).astype(jnp.bfloat16)
        kept = jnp.where(touched[..., None], spread, held[0])
        return jnp.where(living[..., None], kept, jnp.zeros_like(kept))[None]

    def compact(landed, rows):
        return place_rows(landed[:, :cap], tokens), place_rows(landed[:, cap:], cotangent)

    def entire(landed, rows):
        def go(i, held):
            rows, placed = held
            j = (place - i) % shards
            done = []
            for k, (t, whole) in enumerate(zip((tokens, cotangent), placed)):
                spread = jnp.einsum(
                    "cp,cd->pd", chosen(j), rows[k * CAP : k * CAP + CAP], preferred_element_type=jnp.float32
                ).astype(jnp.bfloat16)
                kept = jnp.where(lax.dynamic_index_in_dim(touched, j, 0, keepdims=False)[:, None], spread, t[0, j])
                kept = jnp.where(lax.dynamic_index_in_dim(living, j, 0, keepdims=False)[:, None], kept, jnp.zeros_like(kept))
                done.append(lax.dynamic_update_slice(whole, kept[None, None], (0, j, 0, 0)))
            return lax.ppermute(rows, "fsdp", ring), tuple(done)

        return lax.fori_loop(0, shards, go, (rows, (jnp.zeros_like(tokens), jnp.zeros_like(cotangent))))[1]

    if cap < width:
        back_out, back_grad = lax.cond(crowded, entire, compact, landed, new_rows)
    else:
        back_out, back_grad = compact(landed, new_rows)
    return (
        back_out,
        back_grad,
        totals[0],
        totals[1],
        totals[2],
        totals[3],
        totals[4],
        totals[5],
        totals[6],
    )


def body(axes, *arrays):
    run = wide_body if arrays[2].shape[0] % 16 == 0 else narrow_body
    return run(axes, *arrays)


def solution(mesh):
    placed = (
        P("rep", None, "fsdp", None),
        P("rep", None, "fsdp", None),
        P("fsdp", None),
        P("fsdp", None),
        P("fsdp", None),
        P("fsdp", None),
        P("fsdp"),
        P("fsdp"),
        P("fsdp"),
        P("rep", None),
        P("rep", None, None),
        P("rep", None),
    )
    return jax.shard_map(
        functools.partial(body, grid_axes(mesh)),
        mesh=mesh,
        in_specs=placed,
        out_specs=(
            P("rep", None, "fsdp", None),
            P("rep", None, "fsdp", None),
            P("fsdp", None),
            P("fsdp", None),
            P("fsdp", None),
            P("fsdp", None),
            P("fsdp"),
            P("fsdp"),
            P("fsdp"),
        ),
        check_vma=False,
    )
```
